128 devices in a mesh: mesh: 16 (over z, x), bg: 8 (over y, core).
Axes of the slice: x: 4, y: 4, z: 4, core: 2. Of those that a mesh axis runs over, the one named last changes fastest.
Arguments:
- displacement: float32 [3, 64, 32, 128], P(None, 'mesh', 'bg'), may hold values from -0.4 to 0.4
- bg_coef: float32 [8, 2097152], P(None, ('mesh', 'bg')), may hold values from -0.3 to 0.3
- query_elem: int32 [128, 128, 136], P(('mesh', 'bg')), may hold values from 0 to 16383
- query_point: int32 [128, 128, 136], P(('mesh', 'bg')), may hold values from 0 to 6912, as said below
- query_coord: float32 [128, 128, 3, 136], P(('mesh', 'bg')), may hold values from 0 to 1
Outputs:
- new_displacement: float32 [3, 64, 32, 128], P(None, 'mesh', 'bg')
- line_coeffs: float32 [2, 5], replicated
The draws below stay inside these ranges and needn't reach their ends.
Inputs may be any that keep to these rules, and one draw needn't show every extreme that they name: `query_point`: in each row every quadrature point 0 to 6911 of the row's device fills exactly one slot; all other slots hold 6912 and are empty. In every draw some owner's bucket is full in every row.
All inputs are finite; a program needn't handle non-finite values.
Results may differ from the reference program's by a relative error of at most 0.0003.
Values sent between devices are 32-bit elements; how exact they have to be, the bound alone decides.
No kernel may reach another device: no remote copies, remote signals or barrier semaphores. Data moves between devices by JAX's collectives and lax.ppermute only.
A program may use at most 64 MiB of HBM per device.

```python
import jax
import jax.numpy as jnp
import numpy as np
from jax import lax

EX = 64
EY = 2
EZ = 2
BGE_DEV = 16384
PASSES = 2
LS_STEPS = 4
QPTS_DEV = 6912
CAP = 136
NXN = 128
NYN = 32
NZN = 64
BGE = 2097152
NELEM = 32768
N_MESH = 16
N_BG = 8
DEVICES = 128


def draw_displacement(key, part):
    shape_full = (3, NZN, NYN, NXN)
    depth = jnp.arange(NZN, dtype=jnp.float32)[None, :, None, None] / NZN
    amplitude = 0.03 * (1.0 + 2.0 * depth)
    noise = jax.random.truncated_normal(key, -4.0, 4.0, shape_full, jnp.float32)
    return noise * amplitude


def draw_query_point(key, part):
    slot_positions = DEVICES * CAP
    heavy = jax.random.randint(jax.random.fold_in(key, 1), (), 0, DEVICES)
    extra_credit = jax.random.randint(jax.random.fold_in(key, 2), (DEVICES,), 0, 4) * 32
    owning_device = jnp.arange(slot_positions, dtype=jnp.int32) // CAP

    def one_row(row_lookup_key):
        quality_level = jax.random.randint(jax.random.fold_in(row_lookup_key, 3), (slot_positions,), 0, 64) + extra_credit[owning_device]
        quality_level = jnp.where(owning_device == heavy, 200, quality_level)
        score = quality_level * slot_positions + jnp.arange(slot_positions, dtype=jnp.int32)
        order = jnp.argsort(-score)
        chosen = order[:QPTS_DEV]
        labels = jax.random.permutation(jax.random.fold_in(row_lookup_key, 4), QPTS_DEV).astype(jnp.int32)
        return jnp.full((slot_positions,), QPTS_DEV, jnp.int32).at[chosen].set(labels)
    rows = jax.vmap(one_row)(jax.random.split(jax.random.fold_in(key, 5), DEVICES))
    return rows.reshape(DEVICES, DEVICES, CAP)


def with_ends(entries, stream_key, least, top_value):
    shape = entries.shape
    index_at = [jax.random.randint(jax.random.fold_in(stream_key, axis), (), 0, shape[axis]) for axis in range(len(shape))]
    entries = entries.at[tuple(index_at)].set(least)
    longest = shape.index(max(shape))
    index_at[longest] = (index_at[longest] + 1) % shape[longest]
    return entries.at[tuple(index_at)].set(top_value)


def block_levels(key, extent, cuts, smallest, high):
    level, own = 1.0, jax.random.fold_in(key, 6)
    for axis_at, blocks in cuts:
        steps = jnp.exp(jax.random.uniform(jax.random.fold_in(own, axis_at), (blocks,), jnp.float32, smallest / len(cuts), high / len(cuts)))
        level = level * jnp.repeat(steps, extent[axis_at] // blocks).reshape([-1 if axis == axis_at else 1 for axis in range(len(extent))])
    return level


def setup_inputs(seed: int = 0) -> dict:
    arg_keys = jax.random.split(jax.random.key(seed), 6)
    return {
        "displacement": draw_displacement(jax.random.fold_in(arg_keys[5], 71), 0),
        "bg_coef": jnp.clip(jax.random.uniform(arg_keys[1], (8, BGE), jnp.float32, -0.3, 0.3) * block_levels(arg_keys[1], (8, BGE), ((1, 128),), -0.4, 0.0), -0.3, 0.3),
        "query_elem": with_ends(jax.random.randint(arg_keys[2], (DEVICES, DEVICES, CAP), 0, BGE_DEV), jax.random.fold_in(arg_keys[2], 1), 0, BGE_DEV - 1).astype(jnp.int32),
        "query_point": draw_query_point(jax.random.fold_in(arg_keys[5], 71), 0),
        "query_coord": jnp.clip(1.0 * jax.random.uniform(arg_keys[4], (DEVICES, DEVICES, 3, CAP), jnp.float32) ** block_levels(arg_keys[4], (DEVICES, DEVICES, 3, CAP), ((0, 128),), -0.2, 0.2), 0.0, 1.0),
    }


GAUSS_POINTS = np.array([0.5 - 0.5 * np.sqrt(0.6), 0.5, 0.5 + 0.5 * np.sqrt(0.6)])
GAUSS_WEIGHTS = np.array([5.0 / 18.0, 8.0 / 18.0, 5.0 / 18.0])

def basis_tables(elements, periodic):
    node_count = 2 * elements if periodic else 2 * elements + 1
    values = np.zeros((node_count, 3 * elements))
    slopes = np.zeros((node_count, 3 * elements))
    points = GAUSS_POINTS
    shape_values = [2.0 * (points - 0.5) * (points - 1.0), -4.0 * points * (points - 1.0), 2.0 * points * (points - 0.5)]
    shape_slopes = [4.0 * points - 3.0, 4.0 - 8.0 * points, 4.0 * points - 1.0]
    for offset in range(3):
        node_rows = (2 * np.arange(elements) + offset) % node_count
        for gauss_index in range(3):
            columns = 3 * np.arange(elements) + gauss_index
            values[node_rows, columns] += shape_values[offset][gauss_index]
            slopes[node_rows, columns] += shape_slopes[offset][gauss_index]
    return (jnp.asarray(values, dtype=jnp.float32), jnp.asarray(slopes, dtype=jnp.float32))

def quad_weights(z_elems, y_elems, x_elems):
    along_z = jnp.asarray(np.tile(GAUSS_WEIGHTS, z_elems), dtype=jnp.float32)
    along_y = jnp.asarray(np.tile(GAUSS_WEIGHTS, y_elems), dtype=jnp.float32)
    along_x = jnp.asarray(np.tile(GAUSS_WEIGHTS, x_elems), dtype=jnp.float32)
    return along_z[:, None, None] * along_y[None, :, None] * along_x[None, None, :]

def gradients(node_field, tables):
    z_value, z_slope, y_value, y_slope, value_along_x, x_slope = tables
    highest = lax.Precision.HIGHEST
    value_z = jnp.einsum('czyx,zk->ckyx', node_field, z_value, precision=highest)
    slope_z = jnp.einsum('czyx,zk->ckyx', node_field, z_slope, precision=highest)
    value_zy = jnp.einsum('ckyx,yl->cklx', value_z, y_value, precision=highest)
    slope_y = jnp.einsum('ckyx,yl->cklx', value_z, y_slope, precision=highest)
    slope_zy = jnp.einsum('ckyx,yl->cklx', slope_z, y_value, precision=highest)
    deriv_x = jnp.einsum('cklx,xm->cklm', value_zy, x_slope, precision=highest)
    deriv_y = jnp.einsum('cklx,xm->cklm', slope_y, value_along_x, precision=highest)
    deriv_z = jnp.einsum('cklx,xm->cklm', slope_zy, value_along_x, precision=highest)
    return jnp.stack([deriv_x, deriv_y, deriv_z], axis=1)

def identity_block():
    return jnp.eye(3, dtype=jnp.float32)[:, :, None, None, None]

def gram(left_part, right_part):
    return lax.optimization_barrier(jnp.sum(left_part[:, :, None] * right_part[:, None, :], axis=0))

def energy(node_field, tables, target_size_scale, weights):
    jacobian = gradients(node_field, tables) + identity_block()
    strain = gram(jacobian, jacobian) * target_size_scale - identity_block()
    return jnp.sum(weights * lax.optimization_barrier(jnp.sum(strain * strain, axis=(0, 1))))

def line_terms(node_field, direction, tables, target_size_scale, weights):
    jacobian = gradients(node_field, tables) + identity_block()
    motion = gradients(direction, tables)
    strain_zero = gram(jacobian, jacobian) * target_size_scale - identity_block()
    mixed = gram(jacobian, motion)
    strain_one = (mixed + jnp.swapaxes(mixed, 0, 1)) * target_size_scale
    strain_two = gram(motion, motion) * target_size_scale

    def weighted(first_part, latter_portion):
        return jnp.sum(weights * lax.optimization_barrier(jnp.sum(first_part * latter_portion, axis=(0, 1))))
    zero_zero = weighted(strain_zero, strain_zero)
    zero_one = weighted(strain_zero, strain_one)
    zero_two = weighted(strain_zero, strain_two)
    one_two = weighted(strain_one, strain_two)
    two_two = weighted(strain_two, strain_two)
    gauss_newton = weighted(strain_one, strain_one)
    return (zero_zero, 2.0 * zero_one, gauss_newton + 2.0 * zero_two, 2.0 * one_two, two_two, gauss_newton)

def line_search(terms):
    const_term, linear, quadratic, cubic_term, quartic, gauss_newton = terms
    step_len = jnp.zeros((), jnp.float32)
    for search_turn in range(LS_STEPS):
        slope = linear + step_len * (2.0 * quadratic + step_len * (3.0 * cubic_term + step_len * 4.0 * quartic))
        curvature = 2.0 * quadratic + step_len * (6.0 * cubic_term + step_len * 12.0 * quartic)
        step_len = step_len - slope / jnp.maximum(curvature, gauss_newton + 1e-06)
    return step_len

def inverse_square(coefs, coords):
    along_x = coords[:, 0]
    along_y = coords[:, 1]
    along_z = coords[:, 2]
    summed = jnp.zeros_like(along_x)
    for corner in range(8):
        weight_x = along_x if corner & 1 else 1.0 - along_x
        weight_y = along_y if corner & 2 else 1.0 - along_y
        weight_z = along_z if corner & 4 else 1.0 - along_z
        summed = summed + weight_x * weight_y * weight_z * coefs[:, corner]
    return jnp.exp(-2.0 * summed)

def reference(displacement, bg_coef, query_elem, query_point, query_coord):
    devices = N_MESH * N_BG
    offsets = (jnp.arange(devices, dtype=jnp.int32) * BGE_DEV)[:, None]

    def per_source(items):
        elem_ids, point_ids, coords = items
        coefs = jnp.stack([jnp.take(bg_coef[corner], elem_ids + offsets) for corner in range(8)], axis=1)
        found_vals = inverse_square(coefs, coords)
        return jnp.zeros((QPTS_DEV,), jnp.float32).at[point_ids.reshape(-1)].set(found_vals.reshape(-1), mode='drop')
    spread = lax.map(per_source, (query_elem, query_point, query_coord))
    spread = spread.reshape(N_MESH, N_BG, 3 * EZ, 3 * EY, 3 * EX).transpose(0, 2, 1, 3, 4)
    target_size_scale = spread.reshape(N_MESH * 3 * EZ, N_BG * 3 * EY, 3 * EX)
    weights = quad_weights(EZ * N_MESH, EY * N_BG, EX)
    tables = basis_tables(EZ * N_MESH, True) + basis_tables(EY * N_BG, True) + basis_tables(EX, True)

    def total_energy(values):
        return energy(values, tables, target_size_scale, weights)
    node_field = displacement
    history = []
    for newton_pass in range(PASSES):
        direction = -jax.grad(total_energy)(node_field)
        line_poly = line_terms(node_field, direction, tables, target_size_scale, weights)
        step_len = line_search(line_poly)
        node_field = node_field + step_len * direction
        history.append(jnp.stack(line_poly[:5]) / NELEM)
    return (node_field, jnp.stack(history))
```

```python
import functools

import jax
import jax.numpy as jnp
import numpy as np
from jax import lax
from jax.experimental import pallas as pl
from jax.experimental.pallas import tpu as pltpu
from jax.sharding import PartitionSpec as P

SRC = 128
SLOTS = 136
TABLE = 16384
COLS = 256


def lookup_kernel(asked_ref, table_ref, found_ref, split_ref, turned_ref, result_ref):
    for block in range(5):
        lanes = slice(block * 128, block * 128 + 128)
        turned_ref[lanes, :] = asked_ref[:, lanes].T
    for pair in range(TABLE // (2 * COLS)):
        start = pair * 2 * COLS
        rows = jnp.concatenate(
            [table_ref[:, start : start + COLS], table_ref[:, start + COLS : start + 2 * COLS]], axis=0
        )
        upper = rows.astype(jnp.bfloat16)
        split_ref[pair * 16 : pair * 16 + 16, :COLS] = upper
        split_ref[pair * 16 : pair * 16 + 16, COLS:] = (rows - upper.astype(jnp.float32)).astype(jnp.bfloat16)

    corner = lax.broadcasted_iota(jnp.int32, (8, 256), 0)
    bit_x = (corner & 1) == 1
    bit_y = (corner & 2) == 2
    bit_z = (corner & 4) == 4
    column_at = lax.broadcasted_iota(jnp.int32, (COLS, 256), 0)

    def group(main, tail, at):
        ids = turned_ref[pl.ds(main[0], 8), :].astype(jnp.int32)
        xs, ys, zs = (turned_ref[pl.ds(main[j], 8), :] for j in (1, 2, 3))
        for pair in range(4):
            def both(values):
                return jnp.concatenate([values[2 * pair : 2 * pair + 1], values[2 * pair + 1 : 2 * pair + 2]], axis=1)
            pair_ids = both(ids)
            column = pair_ids & (COLS - 1)
            row8 = jnp.broadcast_to(pair_ids >> 8, (8, 256))
            chosen = (column_at == column).astype(jnp.float32).astype(jnp.bfloat16)
            picked = jnp.dot(split_ref[:, :COLS], chosen, preferred_element_type=jnp.float32) + jnp.dot(
                split_ref[:, COLS:], chosen, preferred_element_type=jnp.float32
            )
            coefs = [jnp.zeros((8, 256), jnp.float32) for _ in range(4)]
            for row in range(TABLE // COLS):
                coefs[row % 4] = jnp.where(row8 == row, picked[row * 8 : row * 8 + 8], coefs[row % 4])
            coef = (coefs[0] + coefs[1]) + (coefs[2] + coefs[3])
            px, py, pz = both(xs), both(ys), both(zs)
            weight = jnp.where(bit_x, px, 1.0 - px) * jnp.where(bit_y, py, 1.0 - py) * jnp.where(bit_z, pz, 1.0 - pz)
            lsize = jnp.sum(weight * coef, axis=0, keepdims=True)
            value = jnp.exp(-2.0 * lsize)
            result_ref[pl.ds(at + 2 * pair, 1), :] = value[:, :128]
            result_ref[pl.ds(at + 2 * pair + 1, 1), :] = value[:, 128:]

    def step(i, carry):
        base = pl.multiple_of(i * 8, 8)
        group([base, base + 128, base + 256, base + 384], None, base)
        return carry

    lax.fori_loop(0, 16, step, 0)
    group([512, 520, 528, 536], None, 128)
    found_ref[:, :128] = result_ref[:128, :].T
    found_ref[:, 128:] = result_ref[128:, :].T


def lookup(asked, table):
    return pl.pallas_call(
        lookup_kernel,
        out_shape=jax.ShapeDtypeStruct((SRC, SLOTS), jnp.float32),
        scratch_shapes=[
            pltpu.VMEM((8 * TABLE // COLS, 2 * COLS), jnp.bfloat16),
            pltpu.VMEM((640, 128), jnp.float32),
            pltpu.VMEM((SLOTS, 128), jnp.float32),
        ],
        name="lookup",
    )(asked, table)


def place_kernel(found_ref, point_ref, size_ref, value_ref, row_ref, lane_ref):
    value_ref[:128, :] = found_ref[:, :128].T
    value_ref[128:, :] = found_ref[:, 128:].T
    point = jnp.concatenate([point_ref[:, :128].T, point_ref[:, 128:].T], axis=0)
    line = (point * 10923) >> 21
    qx = point - line * 192
    qz = (line * 43) >> 8
    qy = line - qz * 6
    ex = (qx * 171) >> 9
    jx = qx - ex * 3
    ey = (qy * 11) >> 5
    jy = qy - ey * 3
    ez = (qz * 11) >> 5
    jz = qz - ez * 3
    row_ref[...] = ((jz * 3 + jy) * 3 + jx) * 2 + ey
    lane_ref[...] = ez * 64 + ex
    lane_at = lax.broadcasted_iota(jnp.int32, (128, 128), 0)
    row_at = lax.broadcasted_iota(jnp.int32, (56, 128), 0)

    def step(i, total):
        base = pl.multiple_of(i * 8, 8)
        values = value_ref[pl.ds(base, 8), :]
        rows = row_ref[pl.ds(base, 8), :]
        lanes = lane_ref[pl.ds(base, 8), :]
        left, right = [], []
        for r in range(8):
            value = values[r : r + 1]
            placed = jnp.where(row_at == rows[r : r + 1], jnp.broadcast_to(value, (56, 128)), 0.0)
            upper = placed.astype(jnp.bfloat16).astype(jnp.float32)
            left.append(jnp.concatenate([upper, placed - upper], axis=0).astype(jnp.bfloat16))
            right.append((lane_at == lanes[r : r + 1]).astype(jnp.float32).astype(jnp.bfloat16))
        left = jnp.concatenate(left, axis=1)
        right = jnp.concatenate(right, axis=1)
        return total + lax.dot_general(left, right, (((1,), (1,)), ((), ())), preferred_element_type=jnp.float32)

    total = lax.fori_loop(0, SLOTS // 8, step, jnp.zeros((112, 128), jnp.float32))
    size_ref[...] = (total[:56] + total[56:])[:54]


def place(found, point):
    return pl.pallas_call(
        place_kernel,
        out_shape=jax.ShapeDtypeStruct((54, 128), jnp.float32),
        scratch_shapes=[
            pltpu.VMEM((SLOTS, 128), jnp.float32),
            pltpu.VMEM((SLOTS, 128), jnp.int32),
            pltpu.VMEM((SLOTS, 128), jnp.int32),
        ],
        name="place",
    )(found, point)


HALF_GAP = float(np.sqrt(0.15))
OUTER, MIDDLE = 5.0 / 18.0, 8.0 / 18.0
NEIGHBOURS = [(z, y) for z in (-1, 0, 1) for y in (-1, 0, 1)]


def lane_index():
    return lax.broadcasted_iota(jnp.int32, (8, 128), 1)


def x_up(v):
    return jnp.where((lane_index() & 63) == 63, pltpu.roll(v, 63, 1), pltpu.roll(v, 127, 1))


def x_down(v):
    return jnp.where((lane_index() & 63) == 0, pltpu.roll(v, 65, 1), pltpu.roll(v, 1, 1))


def z_up(v):
    turned = pltpu.roll(v, 64, 1)
    return jnp.where(lane_index() < 64, turned, pltpu.roll(turned, 4, 0))


def z_down(v):
    turned = pltpu.roll(v, 64, 1)
    return jnp.where(lane_index() < 64, pltpu.roll(turned, 4, 0), turned)


def y_up(v):
    return pltpu.roll(v, 7, 0)


def y_down(v):
    return pltpu.roll(v, 1, 0)


def spread(low, mid, high, slopes=True, values=True):
    bend = (low + high) - 2.0 * mid
    rise = high - low
    vals = slps = None
    if values:
        centre = mid + (2.0 * HALF_GAP * HALF_GAP) * bend
        lean = HALF_GAP * rise
        vals = (centre - lean, mid, centre + lean)
    if slopes:
        change = (4.0 * HALF_GAP) * bend
        slps = (rise - change, rise, rise + change)
    return vals, slps


def collect(vals, slps):
    bend = rise = mid = None
    if vals is not None:
        outer = vals[0] + vals[2]
        bend = (2.0 * HALF_GAP * HALF_GAP) * outer
        rise = HALF_GAP * (vals[2] - vals[0])
        mid = outer + vals[1]
    if slps is not None:
        slope_bend = (4.0 * HALF_GAP) * (slps[2] - slps[0])
        slope_rise = (slps[0] + slps[2]) + slps[1]
        bend = slope_bend if bend is None else bend + slope_bend
        rise = slope_rise if rise is None else rise + slope_rise
    twice = -2.0 * bend
    return bend - rise, twice if mid is None else mid + twice, bend + rise


def at_point(c, k, jz, jy, jx):
    row = (((jz * 3 + jy) * 3 + jx) * 9 + k) * 8
    return pl.ds(pl.multiple_of(row + c * 24, 8), 8)


def forward(c, local, out_ref):
    along_z = [[spread(local(0, y, x), local(1, y, x), local(2, y, x)) for x in range(3)] for y in range(3)]
    for jz in range(3):
        value = [[along_z[y][x][0][jz] for x in range(3)] for y in range(3)]
        slope = [[along_z[y][x][1][jz] for x in range(3)] for y in range(3)]
        plain = [spread(value[0][x], value[1][x], value[2][x]) for x in range(3)]
        steep = [spread(slope[0][x], slope[1][x], slope[2][x], slopes=False)[0] for x in range(3)]
        for jy in range(3):
            dx = spread(*(plain[x][0][jy] for x in range(3)), values=False)[1]
            dy = spread(*(plain[x][1][jy] for x in range(3)), slopes=False)[0]
            dz = spread(*(steep[x][jy] for x in range(3)), slopes=False)[0]
            for jx in range(3):
                for k, part in enumerate((dx, dy, dz)):
                    out_ref[at_point(c, k, jz, jy, jx), :] = part[jx]


def backward(c, from_ref, out_ref):
    planes = []
    for jz in range(3):
        lines = []
        for jy in range(3):
            dx, dy, dz = (
                tuple(from_ref[at_point(c, k, jz, jy, jx), :] for jx in range(3)) for k in range(3)
            )
            lines.append((collect(None, dx), collect(dy, None), collect(dz, None)))
        value = [
            collect(tuple(lines[jy][0][x] for jy in range(3)), tuple(lines[jy][1][x] for jy in range(3)))
            for x in range(3)
        ]
        slope = [collect(tuple(lines[jy][2][x] for jy in range(3)), None) for x in range(3)]
        planes.append((value, slope))
    whole = [
        [
            collect(
                tuple(planes[jz][0][x][y] for jz in range(3)), tuple(planes[jz][1][x][y] for jz in range(3))
            )
            for x in range(3)
        ]
        for y in range(3)
    ]
    folded_x = [[(whole[y][0][z] + x_down(whole[y][2][z]), whole[y][1][z]) for z in range(3)] for y in range(3)]
    for x in range(2):
        folded = [(folded_x[0][z][x] + y_down(folded_x[2][z][x]), folded_x[1][z][x]) for z in range(3)]
        for y in range(2):
            for z, node in enumerate((folded[0][y] + z_down(folded[2][y]), folded[1][y])):
                row = (z * 4 + y * 2 + x) * 8
                out_ref[pl.ds(pl.multiple_of(row + c * 64, 8), 8), :] = node


def symmetric(build):
    upper = {(k, l): build(k, l) for k in range(3) for l in range(k, 3)}
    return {(k, l): upper[min(k, l), max(k, l)] for k in range(3) for l in range(3)}


def inner(a, b):
    square = (a[0, 0] * b[0, 0] + a[1, 1] * b[1, 1]) + a[2, 2] * b[2, 2]
    cross = (a[0, 1] * b[0, 1] + a[0, 2] * b[0, 2]) + a[1, 2] * b[1, 2]
    return square + 2.0 * cross


def column_dot(a, b, k, l):
    return (a[0][k] * b[0][l] + a[1][k] * b[1][l]) + a[2][k] * b[2][l]


def load_tensor(ref, jz, jy, jx):
    tensor = [[ref[at_point(c, k, jz, jy, jx), :] for k in range(3)] for c in range(3)]
    return tensor


def jacobian_at(ref, jz, jy, jx):
    tensor = load_tensor(ref, jz, jy, jx)
    return [[tensor[c][k] + 1.0 if c == k else tensor[c][k] for k in range(3)] for c in range(3)]


def strain_of(jac, size):
    return symmetric(lambda k, l: column_dot(jac, jac, k, l) * size - (1.0 if k == l else 0.0))


def weight_at(jz, jy, jx):
    along_z = jnp.where(jz == 1, MIDDLE, OUTER).astype(jnp.float32)
    return along_z * ((MIDDLE if jy == 1 else OUTER) * (MIDDLE if jx == 1 else OUTER))


def newton_step(totals):
    _, linear, quadratic, cubic, quartic, floor = (totals[:, i : i + 1] for i in range(6))
    step = jnp.zeros_like(linear)
    for _ in range(4):
        slope = linear + step * (2.0 * quadratic + step * (3.0 * cubic + step * 4.0 * quartic))
        curvature = 2.0 * quadratic + step * (6.0 * cubic + step * 12.0 * quartic)
        step = step - slope / jnp.maximum(curvature, floor + 1e-06)
    return step


def add_up(terms_ref):
    return jnp.sum(terms_ref[...], axis=0, keepdims=True)


def ring(pieces, count, out_ref, out_at, z_shift, y_shift):
    low = lax.broadcasted_iota(jnp.int32, (count, 128), 1) < 64
    places = ((-1, 1), (0, 0), (0, 1), (1, 0)) if not y_shift else ((0, 0), (0, 1), (1, 0), (1, 1))
    for upper in range(2):
        for y, (piece_y, row) in enumerate(places):
            rows = pl.ds(row, count, stride=2)
            here = pieces[0, piece_y]
            above = pieces[1, piece_y]
            if z_shift:
                here = pltpu.roll(here[rows, :], 64, 1)
                above = pltpu.roll(above[rows, :], 64, 1)
                value = jnp.where(low, above, here) if upper else jnp.where(low, here, above)
            elif upper:
                value = jnp.where(low, above[rows, :], pieces[-1, piece_y][rows, :])
            else:
                value = here[rows, :]
            out_ref[pl.ds(out_at + upper * 4 + y, count, stride=8), :] = value


def pass_kernel(first, *refs):
    refs = list(refs)
    field = {at: refs.pop(0) for at in NEIGHBOURS}
    if not first:
        shift = {at: refs.pop(0) for at in NEIGHBOURS}
    sizes = {at: refs.pop(0) for at in NEIGHBOURS}
    if first:
        move_ref, terms_out, nodes_ref, size_ref, jac_ref, part_ref, turn_ref = refs
    else:
        terms_in, move_ref, terms_out, own_ref, nodes_ref, size_ref, jac_ref, part_ref, turn_ref, sum_ref = refs
        step = newton_step(add_up(terms_in))
        for i, at in enumerate(NEIGHBOURS):
            sum_ref[i] = field[at][...] + step * shift[at][...]
        field = {at: sum_ref.at[i] for i, at in enumerate(NEIGHBOURS)}
        own_ref[...] = field[0, 0][...]
    for z_shift in range(2):
        for y_shift in range(2):
            ring(field, 24, nodes_ref, (z_shift * 2 + y_shift) * 192, z_shift, y_shift)
    ring(sizes, 27, size_ref, 0, 0, 0)

    def known(c):
        def local(z, y, x):
            row = ((z == 2) * 2 + (y == 2)) * 192 + ((z % 2) * 4 + (y % 2) * 2 + x % 2) * 8
            value = nodes_ref[pl.ds(pl.multiple_of(row + c * 64, 8), 8), :]
            return x_up(value) if x == 2 else value
        return local

    def sought(c):
        def local(z, y, x):
            row = ((z % 2) * 4 + (y % 2) * 2 + x % 2) * 8
            value = turn_ref[pl.ds(pl.multiple_of(row + c * 64, 8), 8), :]
            if x == 2:
                value = x_up(value)
            if y == 2:
                value = y_up(value)
            return z_up(value) if z == 2 else value
        return local

    def each(body):
        def run(i, carry):
            body(i)
            return carry
        lax.fori_loop(0, 3, run, 0)

    def size_at(jz, jy, jx):
        return size_ref[pl.ds(pl.multiple_of((jz * 9 + jy * 3 + jx) * 8, 8), 8), :]

    each(lambda c: forward(c, known(c), jac_ref))

    def stress(jz):
        for jy in range(3):
            for jx in range(3):
                jac = jacobian_at(jac_ref, jz, jy, jx)
                size = size_at(jz, jy, jx)
                strain = strain_of(jac, size)
                scale = size * (-4.0 * weight_at(jz, jy, jx))
                for c in range(3):
                    for k in range(3):
                        part = (strain[k, 0] * jac[c][0] + strain[k, 1] * jac[c][1]) + strain[k, 2] * jac[c][2]
                        part_ref[at_point(c, k, jz, jy, jx), :] = part * scale

    each(stress)
    each(lambda c: backward(c, part_ref, turn_ref))
    for row in range(2):
        move_ref[pl.ds(row, 24, stride=2), :] = turn_ref[pl.ds(row + 1, 24, stride=8), :]
    each(lambda c: forward(c, sought(c), part_ref))

    def line(jz, sums):
        for jy in range(3):
            for jx in range(3):
                jac = jacobian_at(jac_ref, jz, jy, jx)
                motion = load_tensor(part_ref, jz, jy, jx)
                size = size_at(jz, jy, jx)
                weight = weight_at(jz, jy, jx)
                zero = strain_of(jac, size)
                one = symmetric(lambda k, l: (column_dot(jac, motion, k, l) + column_dot(motion, jac, k, l)) * size)
                two = symmetric(lambda k, l: column_dot(motion, motion, k, l) * size)
                pairs = ((zero, zero), (zero, one), (zero, two), (one, two), (two, two), (one, one))
                sums = tuple(total + weight * inner(*pair) for total, pair in zip(sums, pairs))
        return sums

    sums = lax.fori_loop(0, 3, line, tuple(jnp.zeros((8, 128), jnp.float32) for _ in range(6)))
    sub = lax.broadcasted_iota(jnp.int32, (8, 128), 0)
    own = (sub == 1) | (sub == 2)
    zz, zo, zt, ot, tt, gn = (jnp.sum(jnp.where(own, total, 0.0), keepdims=True) for total in sums)
    lane = lax.broadcasted_iota(jnp.int32, (1, 128), 1)
    terms = jnp.zeros((1, 128), jnp.float32)
    for i, term in enumerate((zz, 2.0 * zo, gn + 2.0 * zt, 2.0 * ot, tt, gn)):
        terms = jnp.where(lane == i, term, terms)
    terms_out[...] = jnp.broadcast_to(terms, (SRC, 128))


def newton_pass(field, shift, sizes, terms):
    first = shift is None
    node = jax.ShapeDtypeStruct((48, 128), jnp.float32)
    outs = [node, jax.ShapeDtypeStruct((SRC, 128), jnp.float32)] + ([] if first else [node])
    scratch = [
        pltpu.VMEM((4 * 192, 128), jnp.float32),
        pltpu.VMEM((27 * 8, 128), jnp.float32),
        pltpu.VMEM((243 * 8, 128), jnp.float32),
        pltpu.VMEM((243 * 8, 128), jnp.float32),
        pltpu.VMEM((24 * 8, 128), jnp.float32),
    ] + ([] if first else [pltpu.VMEM((9, 48, 128), jnp.float32)])
    args = list(field) + ([] if first else list(shift)) + list(sizes) + ([] if first else [terms])
    return pl.pallas_call(
        functools.partial(pass_kernel, first),
        out_shape=outs,
        scratch_shapes=scratch,
        name="pass_one" if first else "pass_two",
    )(*args)


def interleave(back):
    row = lax.broadcasted_iota(jnp.int32, (128, 128), 0)
    col = lax.broadcasted_iota(jnp.int32, (128, 128), 1)
    if back:
        row, col = col, row
    return (col == (row & 1) * 64 + (row >> 1)).astype(jnp.float32)


def split_kernel(nodes_ref, out_ref, rows_ref):
    rows = nodes_ref[...].reshape(48, 128)
    rows_ref[...] = jnp.dot(rows, interleave(False), precision=lax.Precision.HIGHEST, preferred_element_type=jnp.float32)
    low = lax.broadcasted_iota(jnp.int32, (1, 128), 1) < 64
    for c in range(3):
        for az in range(2):
            for ay in range(2):
                for ey in range(2):
                    at = c * 16 + az * 4 + ey * 2 + ay
                    first = rows_ref[at : at + 1, :]
                    second = rows_ref[at + 8 : at + 9, :]
                    to = (c * 8 + az * 4 + ay * 2) * 2 + ey
                    out_ref[to : to + 1, :] = jnp.where(low, first, pltpu.roll(second, 64, 1))
                    out_ref[to + 2 : to + 3, :] = jnp.where(low, pltpu.roll(first, 64, 1), second)


def split_nodes(nodes):
    return pl.pallas_call(
        split_kernel,
        out_shape=jax.ShapeDtypeStruct((48, 128), jnp.float32),
        scratch_shapes=[pltpu.VMEM((48, 128), jnp.float32)],
        name="split_nodes",
    )(nodes)


def finish_kernel(own_ref, move_ref, first_ref, second_ref, out_ref, coeff_ref, rows_ref, new_ref):
    first = add_up(first_ref)
    second = add_up(second_ref)
    new_ref[...] = own_ref[...] + newton_step(second) * move_ref[...]
    low = lax.broadcasted_iota(jnp.int32, (1, 128), 1) < 64
    for c in range(3):
        for az in range(2):
            for ay in range(2):
                for ey in range(2):
                    at = (c * 8 + az * 4 + ay * 2) * 2 + ey
                    even = new_ref[at : at + 1, :]
                    odd = new_ref[at + 2 : at + 3, :]
                    to = c * 16 + az * 4 + ey * 2 + ay
                    rows_ref[to : to + 1, :] = jnp.where(low, even, pltpu.roll(odd, 64, 1))
                    rows_ref[to + 8 : to + 9, :] = jnp.where(low, pltpu.roll(even, 64, 1), odd)
    rows = jnp.dot(rows_ref[...], interleave(True), precision=lax.Precision.HIGHEST, preferred_element_type=jnp.float32)
    out_ref[...] = rows.reshape(3, 4, 4, 128)
    coeff_ref[0:1, :] = first[:, :5] * (1.0 / 32768.0)
    coeff_ref[1:2, :] = second[:, :5] * (1.0 / 32768.0)


def finish(own, move, first, second):
    return pl.pallas_call(
        finish_kernel,
        out_shape=[jax.ShapeDtypeStruct((3, 4, 4, 128), jnp.float32), jax.ShapeDtypeStruct((2, 5), jnp.float32)],
        scratch_shapes=[pltpu.VMEM((48, 128), jnp.float32), pltpu.VMEM((48, 128), jnp.float32)],
        name="finish",
    )(own, move, first, second)


def pack_kernel(elem_ref, coord_ref, out_ref):
    elem = elem_ref[...].astype(jnp.float32)
    out_ref[:, :128] = elem[:, :128]
    tails = [elem[:, 128:]]
    for j in range(3):
        coord = coord_ref[:, j, :]
        out_ref[:, 128 + j * 128 : 256 + j * 128] = coord[:, :128]
        tails.append(coord[:, 128:])
    out_ref[:, 512:] = jnp.concatenate(tails + [jnp.zeros((SRC, 96), jnp.float32)], axis=1)


def pack(elem, coord):
    return pl.pallas_call(
        pack_kernel, out_shape=jax.ShapeDtypeStruct((SRC, 640), jnp.float32), name="pack"
    )(elem, coord)


def exchange(values):
    return lax.all_to_all(values, ("mesh", "bg"), split_axis=0, concat_axis=0, tiled=True)


def around(block):
    def moved(values, axis, by):
        count = lax.axis_size(axis)
        return lax.ppermute(values, axis, [(i, (i - by) % count) for i in range(count)])

    pieces = {(0, 0): block}
    for z in (-1, 1):
        pieces[z, 0] = moved(block, "mesh", z)
    for z in (0, -1, 1):
        for y in (-1, 1):
            pieces[z, y] = moved(pieces[z, 0], "bg", y)
    return [pieces[at] for at in NEIGHBOURS]


def shards(displacement, bg_coef, query_elem, query_point, query_coord):
    own = split_nodes(displacement)
    asked = exchange(pack(query_elem.reshape(SRC, SLOTS), query_coord.reshape(SRC, 3, SLOTS)))
    field = around(own)
    found = exchange(lookup(asked, bg_coef))
    sizes = around(place(found, query_point.reshape(SRC, SLOTS)))
    move, terms = newton_pass(field, None, sizes, None)
    first_terms = exchange(terms)
    last_move, last_terms, last_own = newton_pass(field, around(move), sizes, first_terms)
    return finish(last_own, last_move, first_terms, exchange(last_terms))


def solution(mesh):
    in_specs = (
        P(None, "mesh", "bg", None),
        P(None, ("mesh", "bg")),
        P(("mesh", "bg"), None, None),
        P(("mesh", "bg"), None, None),
        P(("mesh", "bg"), None, None, None),
    )
    out_specs = (P(None, "mesh", "bg", None), P())
    return jax.shard_map(shards, mesh=mesh, in_specs=in_specs, out_specs=out_specs, check_vma=False)
```

```python
import functools

import jax
import jax.numpy as jnp
import numpy as np
from jax import lax
from jax.experimental import pallas as pl
from jax.experimental.pallas import tpu as pltpu
from jax.sharding import PartitionSpec as P

SRC = 128
SLOTS = 136
TABLE = 16384
COLS = 256


def lookup_kernel(asked_ref, table_ref, found_ref, split_ref, turned_ref, result_ref):
    for block in range(5):
        lanes = slice(block * 128, block * 128 + 128)
        turned_ref[lanes, :] = asked_ref[:, 0, lanes].T
    for pair in range(TABLE // (2 * COLS)):
        start = pair * 2 * COLS
        rows = jnp.concatenate(
            [table_ref[:, start : start + COLS], table_ref[:, start + COLS : start + 2 * COLS]], axis=0
        )
        upper = rows.astype(jnp.bfloat16)
        split_ref[pair * 16 : pair * 16 + 16, :COLS] = upper
        split_ref[pair * 16 : pair * 16 + 16, COLS:] = (rows - upper.astype(jnp.float32)).astype(jnp.bfloat16)

    corner = lax.broadcasted_iota(jnp.int32, (8, 256), 0)
    bit_x = (corner & 1) == 1
    bit_y = (corner & 2) == 2
    bit_z = (corner & 4) == 4
    column_at = lax.broadcasted_iota(jnp.int32, (COLS, 256), 0)

    def group(main, tail, at):
        ids = turned_ref[pl.ds(main[0], 8), :].astype(jnp.int32)
        xs, ys, zs = (turned_ref[pl.ds(main[j], 8), :] for j in (1, 2, 3))
        for pair in range(4):
            def both(values):
                return jnp.concatenate([values[2 * pair : 2 * pair + 1], values[2 * pair + 1 : 2 * pair + 2]], axis=1)
            pair_ids = both(ids)
            column = pair_ids & (COLS - 1)
            row8 = jnp.broadcast_to(pair_ids >> 8, (8, 256))
            chosen = (column_at == column).astype(jnp.float32).astype(jnp.bfloat16)
            picked = jnp.dot(split_ref[:, :COLS], chosen, preferred_element_type=jnp.float32) + jnp.dot(
                split_ref[:, COLS:], chosen, preferred_element_type=jnp.float32
            )
            coefs = [jnp.zeros((8, 256), jnp.float32) for _ in range(4)]
            for row in range(TABLE // COLS):
                coefs[row % 4] = jnp.where(row8 == row, picked[row * 8 : row * 8 + 8], coefs[row % 4])
            coef = (coefs[0] + coefs[1]) + (coefs[2] + coefs[3])
            px, py, pz = both(xs), both(ys), both(zs)
            weight = jnp.where(bit_x, px, 1.0 - px) * jnp.where(bit_y, py, 1.0 - py) * jnp.where(bit_z, pz, 1.0 - pz)
            lsize = jnp.sum(weight * coef, axis=0, keepdims=True)
            value = jnp.exp(-2.0 * lsize)
            result_ref[pl.ds(at + 2 * pair, 1), :] = value[:, :128]
            result_ref[pl.ds(at + 2 * pair + 1, 1), :] = value[:, 128:]

    def step(i, carry):
        base = pl.multiple_of(i * 8, 8)
        group([base, base + 128, base + 256, base + 384], None, base)
        return carry

    lax.fori_loop(0, 16, step, 0)
    group([512, 520, 528, 536], None, 128)
    found_ref[:, 0, :128] = result_ref[:128, :].T
    found_ref[:, 0, 128:] = result_ref[128:, :].T


def lookup(asked, table):
    return pl.pallas_call(
        lookup_kernel,
        out_shape=jax.ShapeDtypeStruct((SRC, 1, SLOTS), jnp.float32),
        scratch_shapes=[
            pltpu.VMEM((8 * TABLE // COLS, 2 * COLS), jnp.bfloat16),
            pltpu.VMEM((640, 128), jnp.float32),
            pltpu.VMEM((SLOTS, 128), jnp.float32),
        ],
        name="lookup",
    )(asked, table)


def place_kernel(found_ref, point_ref, size_ref, value_ref, row_ref, lane_ref):
    value_ref[:128, :] = found_ref[:, 0, :128].T
    value_ref[128:, :] = found_ref[:, 0, 128:].T
    point = point_ref[...]
    line = (point * 10923) >> 21
    qx = point - line * 192
    qz = (line * 43) >> 8
    qy = line - qz * 6
    ex = (qx * 171) >> 9
    jx = qx - ex * 3
    ey = (qy * 11) >> 5
    jy = qy - ey * 3
    ez = (qz * 11) >> 5
    jz = qz - ez * 3
    row_ref[...] = ((jz * 3 + jy) * 3 + jx) * 2 + ey
    lane_ref[...] = ez * 64 + ex
    lane_at = lax.broadcasted_iota(jnp.int32, (128, 128), 0)
    row_at = lax.broadcasted_iota(jnp.int32, (56, 128), 0)

    def step(i, total):
        base = pl.multiple_of(i * 8, 8)
        values = value_ref[pl.ds(base, 8), :]
        rows = row_ref[pl.ds(base, 8), :]
        lanes = lane_ref[pl.ds(base, 8), :]
        left, right = [], []
        for r in range(8):
            value = values[r : r + 1]
            placed = jnp.where(row_at == rows[r : r + 1], jnp.broadcast_to(value, (56, 128)), 0.0)
            upper = placed.astype(jnp.bfloat16).astype(jnp.float32)
            left.append(jnp.concatenate([upper, placed - upper], axis=0).astype(jnp.bfloat16))
            right.append((lane_at == lanes[r : r + 1]).astype(jnp.float32).astype(jnp.bfloat16))
        left = jnp.concatenate(left, axis=1)
        right = jnp.concatenate(right, axis=1)
        return total + lax.dot_general(left, right, (((1,), (1,)), ((), ())), preferred_element_type=jnp.float32)

    total = lax.fori_loop(0, SLOTS // 8, step, jnp.zeros((112, 128), jnp.float32))
    size_ref[...] = (total[:56] + total[56:])[:54]


def place(found, point):
    return pl.pallas_call(
        place_kernel,
        out_shape=jax.ShapeDtypeStruct((54, 128), jnp.float32),
        scratch_shapes=[
            pltpu.VMEM((SLOTS, 128), jnp.float32),
            pltpu.VMEM((SLOTS, 128), jnp.int32),
            pltpu.VMEM((SLOTS, 128), jnp.int32),
        ],
        name="place",
    )(found, point)


HALF_GAP = float(np.sqrt(0.15))
OUTER, MIDDLE = 5.0 / 18.0, 8.0 / 18.0


def field_pieces(refs):
    own, y_low, y_high, z_low, z_high, corner_low, corner_high = refs
    return {
        (0, -1): (y_low, 0),
        (0, 0): (own, 0),
        (0, 1): (y_high, 0),
        (-1, 0): (z_low, 0),
        (1, 0): (z_high, 0),
        (-1, -1): (corner_low, 0),
        (1, -1): (corner_low, 48),
        (-1, 1): (corner_high, 0),
        (1, 1): (corner_high, 48),
    }


def size_pieces(refs):
    own, y_low, y_high, side, corner_low, corner_high = refs
    pieces = {(0, -1): (y_low, 0), (0, 0): (own, 0), (0, 1): (y_high, 0)}
    for z in (-1, 1):
        pieces.update({(z, -1): (corner_low, 0), (z, 0): (side, 0), (z, 1): (corner_high, 0)})
    return pieces


def lane_index():
    return lax.broadcasted_iota(jnp.int32, (8, 128), 1)


def x_up(v):
    return jnp.where((lane_index() & 63) == 63, pltpu.roll(v, 63, 1), pltpu.roll(v, 127, 1))


def x_down(v):
    return jnp.where((lane_index() & 63) == 0, pltpu.roll(v, 65, 1), pltpu.roll(v, 1, 1))


def z_up(v):
    turned = pltpu.roll(v, 64, 1)
    return jnp.where(lane_index() < 64, turned, pltpu.roll(turned, 4, 0))


def z_down(v):
    turned = pltpu.roll(v, 64, 1)
    return jnp.where(lane_index() < 64, pltpu.roll(turned, 4, 0), turned)


def y_up(v):
    return pltpu.roll(v, 7, 0)


def y_down(v):
    return pltpu.roll(v, 1, 0)


def spread(low, mid, high, slopes=True, values=True):
    bend = (low + high) - 2.0 * mid
    rise = high - low
    vals = slps = None
    if values:
        centre = mid + (2.0 * HALF_GAP * HALF_GAP) * bend
        lean = HALF_GAP * rise
        vals = (centre - lean, mid, centre + lean)
    if slopes:
        change = (4.0 * HALF_GAP) * bend
        slps = (rise - change, rise, rise + change)
    return vals, slps


def collect(vals, slps):
    bend = rise = mid = None
    if vals is not None:
        outer = vals[0] + vals[2]
        bend = (2.0 * HALF_GAP * HALF_GAP) * outer
        rise = HALF_GAP * (vals[2] - vals[0])
        mid = outer + vals[1]
    if slps is not None:
        slope_bend = (4.0 * HALF_GAP) * (slps[2] - slps[0])
        slope_rise = (slps[0] + slps[2]) + slps[1]
        bend = slope_bend if bend is None else bend + slope_bend
        rise = slope_rise if rise is None else rise + slope_rise
    twice = -2.0 * bend
    return bend - rise, twice if mid is None else mid + twice, bend + rise


def at_point(c, k, jz, jy, jx):
    row = (((jz * 3 + jy) * 3 + jx) * 9 + k) * 8
    return pl.ds(pl.multiple_of(row + c * 24, 8), 8)


def forward(c, local, out_ref):
    along_z = [[spread(local(0, y, x), local(1, y, x), local(2, y, x)) for x in range(3)] for y in range(3)]
    for jz in range(3):
        value = [[along_z[y][x][0][jz] for x in range(3)] for y in range(3)]
        slope = [[along_z[y][x][1][jz] for x in range(3)] for y in range(3)]
        plain = [spread(value[0][x], value[1][x], value[2][x]) for x in range(3)]
        steep = [spread(slope[0][x], slope[1][x], slope[2][x], slopes=False)[0] for x in range(3)]
        for jy in range(3):
            dx = spread(*(plain[x][0][jy] for x in range(3)), values=False)[1]
            dy = spread(*(plain[x][1][jy] for x in range(3)), slopes=False)[0]
            dz = spread(*(steep[x][jy] for x in range(3)), slopes=False)[0]
            for jx in range(3):
                for k, part in enumerate((dx, dy, dz)):
                    out_ref[at_point(c, k, jz, jy, jx), :] = part[jx]


def backward(c, from_ref, out_ref):
    planes = []
    for jz in range(3):
        lines = []
        for jy in range(3):
            dx, dy, dz = (
                tuple(from_ref[at_point(c, k, jz, jy, jx), :] for jx in range(3)) for k in range(3)
            )
            lines.append((collect(None, dx), collect(dy, None), collect(dz, None)))
        value = [
            collect(tuple(lines[jy][0][x] for jy in range(3)), tuple(lines[jy][1][x] for jy in range(3)))
            for x in range(3)
        ]
        slope = [collect(tuple(lines[jy][2][x] for jy in range(3)), None) for x in range(3)]
        planes.append((value, slope))
    whole = [
        [
            collect(
                tuple(planes[jz][0][x][y] for jz in range(3)), tuple(planes[jz][1][x][y] for jz in range(3))
            )
            for x in range(3)
        ]
        for y in range(3)
    ]
    folded_x = [[(whole[y][0][z] + x_down(whole[y][2][z]), whole[y][1][z]) for z in range(3)] for y in range(3)]
    for x in range(2):
        folded = [(folded_x[0][z][x] + y_down(folded_x[2][z][x]), folded_x[1][z][x]) for z in range(3)]
        for y in range(2):
            for z, node in enumerate((folded[0][y] + z_down(folded[2][y]), folded[1][y])):
                row = (z * 4 + y * 2 + x) * 8
                out_ref[pl.ds(pl.multiple_of(row + c * 64, 8), 8), :] = node


def symmetric(build):
    upper = {(k, l): build(k, l) for k in range(3) for l in range(k, 3)}
    return {(k, l): upper[min(k, l), max(k, l)] for k in range(3) for l in range(3)}


def inner(a, b):
    square = (a[0, 0] * b[0, 0] + a[1, 1] * b[1, 1]) + a[2, 2] * b[2, 2]
    cross = (a[0, 1] * b[0, 1] + a[0, 2] * b[0, 2]) + a[1, 2] * b[1, 2]
    return square + 2.0 * cross


def column_dot(a, b, k, l):
    return (a[0][k] * b[0][l] + a[1][k] * b[1][l]) + a[2][k] * b[2][l]


def load_tensor(ref, jz, jy, jx):
    tensor = [[ref[at_point(c, k, jz, jy, jx), :] for k in range(3)] for c in range(3)]
    return tensor


def jacobian_at(ref, jz, jy, jx):
    tensor = load_tensor(ref, jz, jy, jx)
    return [[tensor[c][k] + 1.0 if c == k else tensor[c][k] for k in range(3)] for c in range(3)]


def strain_of(jac, size):
    return symmetric(lambda k, l: column_dot(jac, jac, k, l) * size - (1.0 if k == l else 0.0))


def weight_at(jz, jy, jx):
    along_z = jnp.where(jz == 1, MIDDLE, OUTER).astype(jnp.float32)
    return along_z * ((MIDDLE if jy == 1 else OUTER) * (MIDDLE if jx == 1 else OUTER))


def newton_step(totals):
    _, linear, quadratic, cubic, quartic, floor = (totals[:, i : i + 1] for i in range(6))
    step = jnp.zeros_like(linear)
    for _ in range(4):
        slope = linear + step * (2.0 * quadratic + step * (3.0 * cubic + step * 4.0 * quartic))
        curvature = 2.0 * quadratic + step * (6.0 * cubic + step * 12.0 * quartic)
        step = step - slope / jnp.maximum(curvature, floor + 1e-06)
    return step


def add_up(terms_ref):
    return jnp.sum(terms_ref[...], axis=0, keepdims=True)


def ring(pieces, count, out_ref, out_at, z_shift, y_shift):
    low = lax.broadcasted_iota(jnp.int32, (count, 128), 1) < 64
    places = ((-1, 1), (0, 0), (0, 1), (1, 0)) if not y_shift else ((0, 0), (0, 1), (1, 0), (1, 1))
    for upper in range(2):
        for y, (piece_y, row) in enumerate(places):
            here, below, above = (
                ref[pl.ds(at + row, count, stride=2), :] for ref, at in (pieces[z, piece_y] for z in (0, -1, 1))
            )
            if z_shift:
                here = pltpu.roll(here, 64, 1)
                above = pltpu.roll(above, 64, 1)
                value = jnp.where(low, above, here) if upper else jnp.where(low, here, above)
            elif upper:
                value = jnp.where(low, above, below)
            else:
                value = here
            out_ref[pl.ds(out_at + upper * 4 + y, count, stride=8), :] = value


def pass_kernel(first, *refs):
    refs = list(refs)
    field_refs = [refs.pop(0) for _ in range(7)]
    if not first:
        shift_refs = [refs.pop(0) for _ in range(7)]
    sizes = size_pieces([refs.pop(0) for _ in range(6)])
    if first:
        move_ref, terms_out, nodes_ref, size_ref, jac_ref, part_ref, turn_ref = refs
        field = field_pieces(field_refs)
    else:
        terms_in, move_ref, terms_out, own_ref, nodes_ref, size_ref, jac_ref, part_ref, turn_ref, sum_ref = refs
        step = newton_step(add_up(terms_in))
        for i, (field_ref, shift_ref) in enumerate(zip(field_refs, shift_refs)):
            sum_ref[i, : field_ref.shape[0], :] = field_ref[...] + step * shift_ref[...]
        field = field_pieces([sum_ref.at[i] for i in range(7)])
        own_ref[...] = sum_ref[0, :48, :]
    for z_shift in range(2):
        for y_shift in range(2):
            ring(field, 24, nodes_ref, (z_shift * 2 + y_shift) * 192, z_shift, y_shift)
    ring(sizes, 27, size_ref, 0, 0, 0)

    def known(c):
        def local(z, y, x):
            row = ((z == 2) * 2 + (y == 2)) * 192 + ((z % 2) * 4 + (y % 2) * 2 + x % 2) * 8
            value = nodes_ref[pl.ds(pl.multiple_of(row + c * 64, 8), 8), :]
            return x_up(value) if x == 2 else value
        return local

    def sought(c):
        def local(z, y, x):
            row = ((z % 2) * 4 + (y % 2) * 2 + x % 2) * 8
            value = turn_ref[pl.ds(pl.multiple_of(row + c * 64, 8), 8), :]
            if x == 2:
                value = x_up(value)
            if y == 2:
                value = y_up(value)
            return z_up(value) if z == 2 else value
        return local

    def each(body):
        def run(i, carry):
            body(i)
            return carry
        lax.fori_loop(0, 3, run, 0)

    def size_at(jz, jy, jx):
        return size_ref[pl.ds(pl.multiple_of((jz * 9 + jy * 3 + jx) * 8, 8), 8), :]

    each(lambda c: forward(c, known(c), jac_ref))

    def stress(jz):
        for jy in range(3):
            for jx in range(3):
                jac = jacobian_at(jac_ref, jz, jy, jx)
                size = size_at(jz, jy, jx)
                strain = strain_of(jac, size)
                scale = size * (-4.0 * weight_at(jz, jy, jx))
                for c in range(3):
                    for k in range(3):
                        part = (strain[k, 0] * jac[c][0] + strain[k, 1] * jac[c][1]) + strain[k, 2] * jac[c][2]
                        part_ref[at_point(c, k, jz, jy, jx), :] = part * scale

    each(stress)
    each(lambda c: backward(c, part_ref, turn_ref))
    for row in range(2):
        move_ref[pl.ds(row, 24, stride=2), :] = turn_ref[pl.ds(row + 1, 24, stride=8), :]
    each(lambda c: forward(c, sought(c), part_ref))

    def line(jz, sums):
        for jy in range(3):
            for jx in range(3):
                jac = jacobian_at(jac_ref, jz, jy, jx)
                motion = load_tensor(part_ref, jz, jy, jx)
                size = size_at(jz, jy, jx)
                weight = weight_at(jz, jy, jx)
                zero = strain_of(jac, size)
                one = symmetric(lambda k, l: (column_dot(jac, motion, k, l) + column_dot(motion, jac, k, l)) * size)
                two = symmetric(lambda k, l: column_dot(motion, motion, k, l) * size)
                pairs = ((zero, zero), (zero, one), (zero, two), (one, two), (two, two), (one, one))
                sums = tuple(total + weight * inner(*pair) for total, pair in zip(sums, pairs))
        return sums

    sums = lax.fori_loop(0, 3, line, tuple(jnp.zeros((8, 128), jnp.float32) for _ in range(6)))
    sub = lax.broadcasted_iota(jnp.int32, (8, 128), 0)
    own = (sub == 1) | (sub == 2)
    zz, zo, zt, ot, tt, gn = (jnp.sum(jnp.where(own, total, 0.0), keepdims=True) for total in sums)
    lane = lax.broadcasted_iota(jnp.int32, (1, 128), 1)
    terms = jnp.zeros((1, 128), jnp.float32)
    for i, term in enumerate((zz, 2.0 * zo, gn + 2.0 * zt, 2.0 * ot, tt, gn)):
        terms = jnp.where(lane == i, term, terms)
    terms_out[...] = jnp.broadcast_to(terms, (SRC, 128))


def newton_pass(field, shift, sizes, terms):
    first = shift is None
    node = jax.ShapeDtypeStruct((48, 128), jnp.float32)
    outs = [node, jax.ShapeDtypeStruct((SRC, 128), jnp.float32)] + ([] if first else [node])
    scratch = [
        pltpu.VMEM((4 * 192, 128), jnp.float32),
        pltpu.VMEM((27 * 8, 128), jnp.float32),
        pltpu.VMEM((243 * 8, 128), jnp.float32),
        pltpu.VMEM((243 * 8, 128), jnp.float32),
        pltpu.VMEM((24 * 8, 128), jnp.float32),
    ] + ([] if first else [pltpu.VMEM((7, 96, 128), jnp.float32)])
    args = list(field) + ([] if first else list(shift)) + list(sizes) + ([] if first else [terms])
    return pl.pallas_call(
        functools.partial(pass_kernel, first),
        out_shape=outs,
        scratch_shapes=scratch,
        name="pass_one" if first else "pass_two",
    )(*args)


def interleave(back):
    row = lax.broadcasted_iota(jnp.int32, (128, 128), 0)
    col = lax.broadcasted_iota(jnp.int32, (128, 128), 1)
    if back:
        row, col = col, row
    return (col == (row & 1) * 64 + (row >> 1)).astype(jnp.float32)


def split_kernel(nodes_ref, out_ref, rows_ref):
    rows = nodes_ref[...].reshape(48, 128)
    rows_ref[...] = jnp.dot(rows, interleave(False), precision=lax.Precision.HIGHEST, preferred_element_type=jnp.float32)
    low = lax.broadcasted_iota(jnp.int32, (1, 128), 1) < 64
    for c in range(3):
        for az in range(2):
            for ay in range(2):
                for ey in range(2):
                    at = c * 16 + az * 4 + ey * 2 + ay
                    first = rows_ref[at : at + 1, :]
                    second = rows_ref[at + 8 : at + 9, :]
                    to = (c * 8 + az * 4 + ay * 2) * 2 + ey
                    out_ref[to : to + 1, :] = jnp.where(low, first, pltpu.roll(second, 64, 1))
                    out_ref[to + 2 : to + 3, :] = jnp.where(low, pltpu.roll(first, 64, 1), second)


def split_nodes(nodes):
    return pl.pallas_call(
        split_kernel,
        out_shape=jax.ShapeDtypeStruct((48, 128), jnp.float32),
        scratch_shapes=[pltpu.VMEM((48, 128), jnp.float32)],
        name="split_nodes",
    )(nodes)


def finish_kernel(own_ref, move_ref, first_ref, second_ref, out_ref, coeff_ref, rows_ref, new_ref):
    first = add_up(first_ref)
    second = add_up(second_ref)
    new_ref[...] = own_ref[...] + newton_step(second) * move_ref[...]
    low = lax.broadcasted_iota(jnp.int32, (1, 128), 1) < 64
    for c in range(3):
        for az in range(2):
            for ay in range(2):
                for ey in range(2):
                    at = (c * 8 + az * 4 + ay * 2) * 2 + ey
                    even = new_ref[at : at + 1, :]
                    odd = new_ref[at + 2 : at + 3, :]
                    to = c * 16 + az * 4 + ey * 2 + ay
                    rows_ref[to : to + 1, :] = jnp.where(low, even, pltpu.roll(odd, 64, 1))
                    rows_ref[to + 8 : to + 9, :] = jnp.where(low, pltpu.roll(even, 64, 1), odd)
    rows = jnp.dot(rows_ref[...], interleave(True), precision=lax.Precision.HIGHEST, preferred_element_type=jnp.float32)
    out_ref[...] = rows.reshape(3, 4, 4, 128)
    coeff_ref[0:1, :] = first[:, :5] * (1.0 / 32768.0)
    coeff_ref[1:2, :] = second[:, :5] * (1.0 / 32768.0)


def finish(own, move, first, second):
    return pl.pallas_call(
        finish_kernel,
        out_shape=[jax.ShapeDtypeStruct((3, 4, 4, 128), jnp.float32), jax.ShapeDtypeStruct((2, 5), jnp.float32)],
        scratch_shapes=[pltpu.VMEM((48, 128), jnp.float32), pltpu.VMEM((48, 128), jnp.float32)],
        name="finish",
    )(own, move, first, second)


def pack_kernel(elem_ref, coord_ref, out_ref):
    parts = [elem_ref[...].astype(jnp.float32)] + [coord_ref[j] for j in range(3)]
    for j, part in enumerate(parts):
        out_ref[:, 0, j * 128 : j * 128 + 128] = part[:128].T
    tails = jnp.concatenate([part[128:] for part in parts] + [jnp.zeros((96, 128), jnp.float32)], axis=0)
    out_ref[:, 0, 512:] = tails.T


def pack(elem, coord):
    return pl.pallas_call(
        pack_kernel, out_shape=jax.ShapeDtypeStruct((SRC, 1, 640), jnp.float32), name="pack"
    )(elem, coord)


def exchange(values):
    return lax.all_to_all(values, ("mesh", "bg"), split_axis=0, concat_axis=0, tiled=True)


def moved(values, axis, by):
    count = lax.axis_size(axis)
    return lax.ppermute(values, axis, [(i, (i - by) % count) for i in range(count)])


def around(block, merge):
    z_low, z_high = moved(block, "mesh", -1), moved(block, "mesh", 1)
    y_low, y_high = moved(block, "bg", -1), moved(block, "bg", 1)
    if merge:
        side = jnp.where(lax.broadcasted_iota(jnp.int32, block.shape, 1) < 64, z_high, z_low)
        return [block, y_low, y_high, side, moved(side, "bg", -1), moved(side, "bg", 1)]
    sides = jnp.concatenate([z_low, z_high], axis=0)
    return [block, y_low, y_high, z_low, z_high, moved(sides, "bg", -1), moved(sides, "bg", 1)]


def shards(displacement, bg_coef, query_elem, query_point, query_coord):
    asked = exchange(pack(query_elem[0].T, query_coord[0].transpose(1, 2, 0)))
    field = around(split_nodes(displacement), False)
    asked, field = lax.optimization_barrier((asked, field))
    found = exchange(lookup(asked, bg_coef))
    sizes = around(place(found, query_point[0].T), True)
    move, terms = newton_pass(field, None, sizes, None)
    first_terms = exchange(terms)
    last_move, last_terms, last_own = newton_pass(field, around(move, False), sizes, first_terms)
    return finish(last_own, last_move, first_terms, exchange(last_terms))


def solution(mesh):
    in_specs = (
        P(None, "mesh", "bg", None),
        P(None, ("mesh", "bg")),
        P(("mesh", "bg"), None, None),
        P(("mesh", "bg"), None, None),
        P(("mesh", "bg"), None, None, None),
    )
    out_specs = (P(None, "mesh", "bg", None), P())
    return jax.shard_map(shards, mesh=mesh, in_specs=in_specs, out_specs=out_specs, check_vma=False)
```

```python
import functools

import jax
import jax.numpy as jnp
import numpy as np
from jax import lax
from jax.experimental import pallas as pl
from jax.experimental.pallas import tpu as pltpu
from jax.sharding import PartitionSpec as P

SRC = 128
SLOTS = 136
TABLE = 16384
COLS = 256


GATHER_ROWS = 80
ROUNDS = 10


def in_vmem(count):
    return [pl.BlockSpec(memory_space=pltpu.VMEM) for _ in range(count)]


def call(kernel, outs, args, scratch, name):
    many = isinstance(outs, list)
    return pl.pallas_call(
        kernel,
        out_shape=outs,
        in_specs=in_vmem(len(args)),
        out_specs=in_vmem(len(outs)) if many else in_vmem(1)[0],
        scratch_shapes=scratch,
        name=name,
    )(*args)


def prepare_kernel(table_ref, split_ref, packed_ref, unit_ref):
    top = jnp.zeros((8, 128), jnp.float32)
    for block in range(TABLE // 128):
        top = jnp.maximum(top, jnp.abs(table_ref[:, block * 128 : block * 128 + 128]))
    top = jnp.maximum(jnp.max(top, keepdims=True), 1e-30)
    unit_ref[...] = jnp.broadcast_to(top * (1.0 / 32767.0), (8, 128))
    scale = 32767.0 / top

    def whole(values):
        return (values * scale + 32768.5).astype(jnp.int32) - 32768

    for block in range(TABLE // 256):
        low = table_ref[:, block * 128 : block * 128 + 128]
        high = table_ref[:, TABLE // 2 + block * 128 : TABLE // 2 + block * 128 + 128]
        packed_ref[:, block * 128 : block * 128 + 128] = (whole(high) << 16) | (whole(low) & 65535)
    for pair in range(TABLE // (2 * COLS)):
        start = pair * 2 * COLS
        rows = jnp.concatenate(
            [table_ref[:, start : start + COLS], table_ref[:, start + COLS : start + 2 * COLS]], axis=0
        )
        upper = rows.astype(jnp.bfloat16)
        split_ref[pair * 16 : pair * 16 + 16, :COLS] = upper
        split_ref[pair * 16 : pair * 16 + 16, COLS:] = (rows - upper.astype(jnp.float32)).astype(jnp.bfloat16)


def prepare(table):
    outs = [
        jax.ShapeDtypeStruct((8 * TABLE // COLS, 2 * COLS), jnp.bfloat16),
        jax.ShapeDtypeStruct((8, TABLE // 2), jnp.int32),
        jax.ShapeDtypeStruct((8, 128), jnp.float32),
    ]
    return call(prepare_kernel, outs, [table], [], "prepare")


def choose(leaf, masks, first, count):
    if count == 1:
        return leaf(first)
    half = count // 2
    mask = masks[half.bit_length() - 1]
    return jnp.where(mask, choose(leaf, masks, first + half, half), choose(leaf, masks, first, half))


def weigh(coef, x, y, z):
    corner = lax.broadcasted_iota(jnp.int32, coef.shape, 0)
    weight_x = jnp.where((corner & 1) == 1, x, 1.0 - x)
    weight_y = jnp.where((corner & 2) == 2, y, 1.0 - y)
    weight_z = jnp.where((corner & 4) == 4, z, 1.0 - z)
    lsize = jnp.sum(weight_x * weight_y * weight_z * coef, axis=0, keepdims=True)
    return jnp.exp(-2.0 * lsize)


def lookup_kernel(asked_ref, split_ref, packed_ref, unit_ref, found_ref, turned_ref, result_ref, column_ref):
    for j in range(4):
        turned_ref[j * SLOTS : j * SLOTS + 128, :] = asked_ref[:, 0, j * 128 : j * 128 + 128].T
    tails = asked_ref[:, 0, 512:].T
    for j in range(4):
        turned_ref[j * SLOTS + 128 : (j + 1) * SLOTS, :] = tails[j * 8 : j * 8 + 8]
    column_ref[...] = lax.broadcasted_iota(jnp.int32, (COLS, 128), 0).astype(jnp.float32).astype(jnp.bfloat16)
    one = jnp.ones((), jnp.bfloat16)
    zero = jnp.zeros((), jnp.bfloat16)

    def step(i, carry):
        base = pl.multiple_of(i * 8, 8)
        ids, xs, ys, zs = (turned_ref[pl.ds(pl.multiple_of(j * SLOTS + base, 8), 8), :] for j in range(4))
        ids = ids.astype(jnp.int32)
        unit = unit_ref[...]
        for r in range(8):
            own = jnp.broadcast_to(ids[r : r + 1], (8, 128))
            lane = own & 127
            masks = [(own & (128 << bit)) != 0 for bit in range(6)]

            def leaf(block):
                return jnp.take_along_axis(packed_ref[:, block * 128 : block * 128 + 128], lane, axis=1)

            word = choose(leaf, masks, 0, 64)
            whole = jnp.where((own & (TABLE // 2)) != 0, word, word << 16) >> 16
            coef = whole.astype(jnp.float32) * unit
            result_ref[pl.ds(base + r, 1), :] = weigh(coef, xs[r : r + 1], ys[r : r + 1], zs[r : r + 1])

        start = jnp.minimum(GATHER_ROWS + i * 6, SLOTS - 6)
        for pair in range(3):
            at = start + 2 * pair
            pair_ids, px, py, pz = (
                jnp.concatenate(
                    [turned_ref[pl.ds(j * SLOTS + at, 1), :], turned_ref[pl.ds(j * SLOTS + at + 1, 1), :]], axis=1
                )
                for j in range(4)
            )
            pair_ids = pair_ids.astype(jnp.int32)
            column = (pair_ids & (COLS - 1)).astype(jnp.float32).astype(jnp.bfloat16)
            chosen = jnp.concatenate(
                [
                    jnp.where(column_ref[...] == column[:, half * 128 : half * 128 + 128], one, zero)
                    for half in range(2)
                ],
                axis=1,
            )
            picked = jnp.dot(split_ref[:, :COLS], chosen, preferred_element_type=jnp.float32) + jnp.dot(
                split_ref[:, COLS:], chosen, preferred_element_type=jnp.float32
            )
            own = jnp.broadcast_to(pair_ids, (8, 256))
            masks = [(own & (COLS << bit)) != 0 for bit in range(6)]
            coef = choose(lambda row: picked[row * 8 : row * 8 + 8], masks, 0, 64)
            value = weigh(coef, px, py, pz)
            result_ref[pl.ds(at, 1), :] = value[:, :128]
            result_ref[pl.ds(at + 1, 1), :] = value[:, 128:]
        return carry

    lax.fori_loop(0, ROUNDS, step, 0)
    found_ref[:, 0, :128] = result_ref[:128, :].T
    found_ref[:, 0, 128:] = result_ref[128:, :].T


def lookup(asked, prepared):
    scratch = [
        pltpu.VMEM((4 * SLOTS, 128), jnp.float32),
        pltpu.VMEM((SLOTS, 128), jnp.float32),
        pltpu.VMEM((COLS, 128), jnp.bfloat16),
    ]
    out = jax.ShapeDtypeStruct((SRC, 1, SLOTS), jnp.float32)
    return call(lookup_kernel, out, [asked, *prepared], scratch, "lookup")


def place_kernel(found_ref, point_ref, size_ref, value_ref, row_ref, lane_ref, at_ref):
    value_ref[:128, :] = found_ref[:, 0, :128].T
    value_ref[128:, :] = found_ref[:, 0, 128:].T
    point = point_ref[...]
    line = (point * 10923) >> 21
    qx = point - line * 192
    qz = (line * 43) >> 8
    qy = line - qz * 6
    ex = (qx * 171) >> 9
    jx = qx - ex * 3
    ey = (qy * 11) >> 5
    jy = qy - ey * 3
    ez = (qz * 11) >> 5
    jz = qz - ez * 3
    row_ref[...] = (((jz * 3 + jy) * 3 + jx) * 2 + ey).astype(jnp.float32)
    lane_ref[...] = (ez * 64 + ex).astype(jnp.float32)
    at_ref[...] = lax.broadcasted_iota(jnp.int32, (128, 128), 0).astype(jnp.float32).astype(jnp.bfloat16)
    one = jnp.ones((), jnp.bfloat16)
    zero = jnp.zeros((), jnp.bfloat16)

    def step(i, total):
        base = pl.multiple_of(i * 8, 8)
        values = value_ref[pl.ds(base, 8), :]
        rows = row_ref[pl.ds(base, 8), :]
        lanes = lane_ref[pl.ds(base, 8), :]
        left, right = [], []
        for r in range(8):
            value = values[r : r + 1]
            upper = value.astype(jnp.bfloat16)
            lower = (value - upper.astype(jnp.float32)).astype(jnp.bfloat16)
            row = at_ref[:64, :] == rows[r : r + 1].astype(jnp.bfloat16)
            left.append(jnp.concatenate([jnp.where(row, upper, zero), jnp.where(row, lower, zero)], axis=0))
            right.append(jnp.where(at_ref[...] == lanes[r : r + 1].astype(jnp.bfloat16), one, zero))
        left = jnp.concatenate(left, axis=1)
        right = jnp.concatenate(right, axis=1)
        return total + lax.dot_general(left, right, (((1,), (1,)), ((), ())), preferred_element_type=jnp.float32)

    total = lax.fori_loop(0, SLOTS // 8, step, jnp.zeros((128, 128), jnp.float32))
    size_ref[...] = total[:56] + total[64:120]


def place(found, point):
    scratch = [pltpu.VMEM((SLOTS, 128), jnp.float32) for _ in range(3)] + [pltpu.VMEM((128, 128), jnp.bfloat16)]
    return call(place_kernel, jax.ShapeDtypeStruct((56, 128), jnp.float32), [found, point], scratch, "place")


HALF_GAP = float(np.sqrt(0.15))
OUTER, MIDDLE = 5.0 / 18.0, 8.0 / 18.0


def field_pieces(refs):
    return {(z, y): (refs[y], (z % 3) * 48) for z in (-1, 0, 1) for y in (-1, 0, 1)}


def size_pieces(refs):
    return {(z, y): (refs[y], 56 * abs(z)) for z in (-1, 0, 1) for y in (-1, 0, 1)}


def lane_index():
    return lax.broadcasted_iota(jnp.int32, (8, 128), 1)


def x_up(v):
    return jnp.where((lane_index() & 63) == 63, pltpu.roll(v, 63, 1), pltpu.roll(v, 127, 1))


def x_down(v):
    return jnp.where((lane_index() & 63) == 0, pltpu.roll(v, 65, 1), pltpu.roll(v, 1, 1))


def z_up(v):
    turned = pltpu.roll(v, 64, 1)
    return jnp.where(lane_index() < 64, turned, pltpu.roll(turned, 4, 0))


def z_down(v):
    turned = pltpu.roll(v, 64, 1)
    return jnp.where(lane_index() < 64, pltpu.roll(turned, 4, 0), turned)


def y_up(v):
    return pltpu.roll(v, 7, 0)


def y_down(v):
    return pltpu.roll(v, 1, 0)


def spread(low, mid, high, slopes=True, values=True):
    bend = (low + high) - 2.0 * mid
    rise = high - low
    vals = slps = None
    if values:
        centre = mid + (2.0 * HALF_GAP * HALF_GAP) * bend
        lean = HALF_GAP * rise
        vals = (centre - lean, mid, centre + lean)
    if slopes:
        change = (4.0 * HALF_GAP) * bend
        slps = (rise - change, rise, rise + change)
    return vals, slps


def collect(vals, slps):
    bend = rise = mid = None
    if vals is not None:
        outer = vals[0] + vals[2]
        bend = (2.0 * HALF_GAP * HALF_GAP) * outer
        rise = HALF_GAP * (vals[2] - vals[0])
        mid = outer + vals[1]
    if slps is not None:
        slope_bend = (4.0 * HALF_GAP) * (slps[2] - slps[0])
        slope_rise = (slps[0] + slps[2]) + slps[1]
        bend = slope_bend if bend is None else bend + slope_bend
        rise = slope_rise if rise is None else rise + slope_rise
    twice = -2.0 * bend
    return bend - rise, twice if mid is None else mid + twice, bend + rise


def at_point(c, k, jz, jy, jx):
    row = (((jz * 3 + jy) * 3 + jx) * 9 + k) * 8
    return pl.ds(pl.multiple_of(row + c * 24, 8), 8)


def forward(local, out_ref, at):
    along_z = [[spread(local(0, y, x), local(1, y, x), local(2, y, x)) for x in range(3)] for y in range(3)]
    for jz in range(3):
        value = [[along_z[y][x][0][jz] for x in range(3)] for y in range(3)]
        slope = [[along_z[y][x][1][jz] for x in range(3)] for y in range(3)]
        plain = [spread(value[0][x], value[1][x], value[2][x]) for x in range(3)]
        steep = [spread(slope[0][x], slope[1][x], slope[2][x], slopes=False)[0] for x in range(3)]
        for jy in range(3):
            dx = spread(*(plain[x][0][jy] for x in range(3)), values=False)[1]
            dy = spread(*(plain[x][1][jy] for x in range(3)), slopes=False)[0]
            dz = spread(*(steep[x][jy] for x in range(3)), slopes=False)[0]
            for jx in range(3):
                for k, part in enumerate((dx, dy, dz)):
                    out_ref[at(k, jz, jy, jx), :] = part[jx]


def backward(c, from_ref, out_ref):
    planes = []
    for jz in range(3):
        lines = []
        for jy in range(3):
            dx, dy, dz = (
                tuple(from_ref[at_point(c, k, jz, jy, jx), :] for jx in range(3)) for k in range(3)
            )
            lines.append((collect(None, dx), collect(dy, None), collect(dz, None)))
        value = [
            collect(tuple(lines[jy][0][x] for jy in range(3)), tuple(lines[jy][1][x] for jy in range(3)))
            for x in range(3)
        ]
        slope = [collect(tuple(lines[jy][2][x] for jy in range(3)), None) for x in range(3)]
        planes.append((value, slope))
    whole = [
        [
            collect(
                tuple(planes[jz][0][x][y] for jz in range(3)), tuple(planes[jz][1][x][y] for jz in range(3))
            )
            for x in range(3)
        ]
        for y in range(3)
    ]
    folded_x = [[(whole[y][0][z] + x_down(whole[y][2][z]), whole[y][1][z]) for z in range(3)] for y in range(3)]
    for x in range(2):
        folded = [(folded_x[0][z][x] + y_down(folded_x[2][z][x]), folded_x[1][z][x]) for z in range(3)]
        for y in range(2):
            for z, node in enumerate((folded[0][y] + z_down(folded[2][y]), folded[1][y])):
                row = (z * 4 + y * 2 + x) * 8
                out_ref[pl.ds(pl.multiple_of(row + c * 64, 8), 8), :] = node


def symmetric(build):
    upper = {(k, l): build(k, l) for k in range(3) for l in range(k, 3)}
    return {(k, l): upper[min(k, l), max(k, l)] for k in range(3) for l in range(3)}


def inner(a, b):
    square = (a[0, 0] * b[0, 0] + a[1, 1] * b[1, 1]) + a[2, 2] * b[2, 2]
    cross = (a[0, 1] * b[0, 1] + a[0, 2] * b[0, 2]) + a[1, 2] * b[1, 2]
    return square + 2.0 * cross


def column_dot(a, b, k, l):
    return (a[0][k] * b[0][l] + a[1][k] * b[1][l]) + a[2][k] * b[2][l]


def load_tensor(ref, jz, jy, jx):
    tensor = [[ref[at_point(c, k, jz, jy, jx), :] for k in range(3)] for c in range(3)]
    return tensor


def jacobian_at(ref, jz, jy, jx):
    tensor = load_tensor(ref, jz, jy, jx)
    return [[tensor[c][k] + 1.0 if c == k else tensor[c][k] for k in range(3)] for c in range(3)]


def strain_of(jac, size):
    return symmetric(lambda k, l: column_dot(jac, jac, k, l) * size - (1.0 if k == l else 0.0))


def weight_at(jz, jy, jx):
    along_z = jnp.where(jz == 1, MIDDLE, OUTER).astype(jnp.float32)
    return along_z * ((MIDDLE if jy == 1 else OUTER) * (MIDDLE if jx == 1 else OUTER))


def newton_step(totals):
    _, linear, quadratic, cubic, quartic, floor = (totals[:, i : i + 1] for i in range(6))
    step = jnp.zeros_like(linear)
    for _ in range(4):
        slope = linear + step * (2.0 * quadratic + step * (3.0 * cubic + step * 4.0 * quartic))
        curvature = 2.0 * quadratic + step * (6.0 * cubic + step * 12.0 * quartic)
        step = step - slope / jnp.maximum(curvature, floor + 1e-06)
    return step


def add_up(terms_ref):
    return jnp.sum(terms_ref[...], axis=0, keepdims=True)


def ring(pieces, count, out_ref, out_at, z_shift, y_shift):
    low = lax.broadcasted_iota(jnp.int32, (count, 128), 1) < 64
    places = ((-1, 1), (0, 0), (0, 1), (1, 0)) if not y_shift else ((0, 0), (0, 1), (1, 0), (1, 1))
    for upper in range(2):
        for y, (piece_y, row) in enumerate(places):
            here, below, above = (
                ref[pl.ds(at + row, count, stride=2), :] for ref, at in (pieces[z, piece_y] for z in (0, -1, 1))
            )
            if z_shift:
                here = pltpu.roll(here, 64, 1)
                above = pltpu.roll(above, 64, 1)
                value = jnp.where(low, above, here) if upper else jnp.where(low, here, above)
            elif upper:
                value = jnp.where(low, above, below)
            else:
                value = here
            out_ref[pl.ds(out_at + upper * 4 + y, count, stride=8), :] = value


def pass_kernel(first, *refs):
    refs = list(refs)
    field_refs = [refs.pop(0) for _ in range(3)]
    if not first:
        shift_refs = [refs.pop(0) for _ in range(3)]
    sizes = size_pieces([refs.pop(0) for _ in range(3)])
    if first:
        move_ref, terms_out, nodes_ref, size_ref, jac_ref, part_ref, turn_ref = refs
        field = field_pieces(field_refs)
    else:
        terms_in, move_ref, terms_out, own_ref, nodes_ref, size_ref, jac_ref, part_ref, turn_ref, sum_ref = refs
        step = newton_step(add_up(terms_in))
        for i, (field_ref, shift_ref) in enumerate(zip(field_refs, shift_refs)):
            sum_ref[i] = field_ref[...] + step * shift_ref[...]
        field = field_pieces([sum_ref.at[i] for i in range(3)])
        own_ref[...] = sum_ref[0, :48, :]
    for z_shift in range(2):
        for y_shift in range(2):
            ring(field, 24, nodes_ref, (z_shift * 2 + y_shift) * 192, z_shift, y_shift)
    ring(sizes, 27, size_ref, 0, 0, 0)

    def known(c):
        def local(z, y, x):
            row = ((z == 2) * 2 + (y == 2)) * 192 + ((z % 2) * 4 + (y % 2) * 2 + x % 2) * 8
            value = nodes_ref[pl.ds(pl.multiple_of(row + c * 64, 8), 8), :]
            return x_up(value) if x == 2 else value
        return local

    def packed(node, upper, shift):
        rows = [
            turn_ref[pl.ds(node * 8 + upper * 4 + 1 + shift + ey, 4, stride=64), :] for ey in range(2)
        ]
        return jnp.concatenate(rows, axis=0)

    def sought(z, y, x):
        node = (z % 2) * 4 + (y % 2) * 2 + x % 2
        shift = y // 2
        value = packed(node, 0, shift)
        if z == 2:
            turned = pltpu.roll(value, 64, 1)
            value = jnp.where(lane_index() < 64, turned, pltpu.roll(packed(node, 1, shift), 64, 1))
        return x_up(value) if x == 2 else value

    def each(body):
        def run(i, carry):
            body(i)
            return carry
        lax.fori_loop(0, 3, run, 0)

    def size_at(jz, jy, jx):
        return size_ref[pl.ds(pl.multiple_of((jz * 9 + jy * 3 + jx) * 8, 8), 8), :]

    each(lambda c: forward(known(c), jac_ref, functools.partial(at_point, c)))
    turn_ref[192:, :] = jnp.zeros((64, 128), jnp.float32)

    def stress(jz):
        for jy in range(3):
            for jx in range(3):
                jac = jacobian_at(jac_ref, jz, jy, jx)
                size = size_at(jz, jy, jx)
                strain = strain_of(jac, size)
                scale = size * (-4.0 * weight_at(jz, jy, jx))
                for c in range(3):
                    for k in range(3):
                        part = (strain[k, 0] * jac[c][0] + strain[k, 1] * jac[c][1]) + strain[k, 2] * jac[c][2]
                        part_ref[at_point(c, k, jz, jy, jx), :] = part * scale

    each(stress)
    each(lambda c: backward(c, part_ref, turn_ref))
    for row in range(2):
        move_ref[pl.ds(row, 24, stride=2), :] = turn_ref[pl.ds(row + 1, 24, stride=8), :]
    forward(sought, part_ref, lambda k, jz, jy, jx: pl.ds(((jz * 9 + jy * 3 + jx) * 3 + k) * 8, 8))

    sub = lax.broadcasted_iota(jnp.int32, (8, 128), 0)
    sums = [jnp.zeros((8, 128), jnp.float32) for _ in range(6)]
    for start, fresh in ((0, 0), (8, 8), (16, 16), (19, 24)):
        weight = jnp.zeros((8, 128), jnp.float32)
        for i in range(fresh - start, 8):
            point = start + i
            parts = [MIDDLE if (point // by) % 3 == 1 else OUTER for by in (9, 3, 1)]
            weight = jnp.where(sub == i, (parts[0] * parts[1]) * parts[2], weight)
        for ey in range(2):
            jac = [
                [jac_ref[pl.ds((start * 9 + c * 3 + k) * 8 + 1 + ey, 8, stride=72), :] for k in range(3)]
                for c in range(3)
            ]
            jac = [[jac[c][k] + 1.0 if c == k else jac[c][k] for k in range(3)] for c in range(3)]
            motion = [
                [part_ref[pl.ds((start * 3 + k) * 8 + ey * 4 + c, 8, stride=24), :] for k in range(3)]
                for c in range(3)
            ]
            size = size_ref[pl.ds(start * 8 + 1 + ey, 8, stride=8), :]
            zero = strain_of(jac, size)
            one = symmetric(lambda k, l: (column_dot(jac, motion, k, l) + column_dot(motion, jac, k, l)) * size)
            two = symmetric(lambda k, l: column_dot(motion, motion, k, l) * size)
            pairs = ((zero, zero), (zero, one), (zero, two), (one, two), (two, two), (one, one))
            sums = [total + weight * inner(*pair) for total, pair in zip(sums, pairs)]
    zz, zo, zt, ot, tt, gn = (jnp.sum(total, keepdims=True) for total in sums)
    lane = lax.broadcasted_iota(jnp.int32, (1, 128), 1)
    terms = jnp.zeros((1, 128), jnp.float32)
    for i, term in enumerate((zz, 2.0 * zo, gn + 2.0 * zt, 2.0 * ot, tt, gn)):
        terms = jnp.where(lane == i, term, terms)
    terms_out[...] = jnp.broadcast_to(terms, (SRC, 128))


def newton_pass(field, shift, sizes, terms):
    first = shift is None
    node = jax.ShapeDtypeStruct((48, 128), jnp.float32)
    outs = [node, jax.ShapeDtypeStruct((SRC, 128), jnp.float32)] + ([] if first else [node])
    scratch = [
        pltpu.VMEM((4 * 192, 128), jnp.float32),
        pltpu.VMEM((27 * 8, 128), jnp.float32),
        pltpu.VMEM((243 * 8, 128), jnp.float32),
        pltpu.VMEM((243 * 8, 128), jnp.float32),
        pltpu.VMEM((32 * 8, 128), jnp.float32),
    ] + ([] if first else [pltpu.VMEM((3, 144, 128), jnp.float32)])
    args = list(field) + ([] if first else list(shift)) + list(sizes) + ([] if first else [terms])
    return call(functools.partial(pass_kernel, first), outs, args, scratch, "pass_one" if first else "pass_two")


def interleave(back):
    row = lax.broadcasted_iota(jnp.int32, (128, 128), 0)
    col = lax.broadcasted_iota(jnp.int32, (128, 128), 1)
    if back:
        row, col = col, row
    return (col == (row & 1) * 64 + (row >> 1)).astype(jnp.float32)


def split_kernel(nodes_ref, out_ref, rows_ref):
    rows = nodes_ref[...].reshape(48, 128)
    rows_ref[...] = jnp.dot(rows, interleave(False), precision=lax.Precision.HIGHEST, preferred_element_type=jnp.float32)
    low = lax.broadcasted_iota(jnp.int32, (1, 128), 1) < 64
    for c in range(3):
        for az in range(2):
            for ay in range(2):
                for ey in range(2):
                    at = c * 16 + az * 4 + ey * 2 + ay
                    first = rows_ref[at : at + 1, :]
                    second = rows_ref[at + 8 : at + 9, :]
                    to = (c * 8 + az * 4 + ay * 2) * 2 + ey
                    out_ref[to : to + 1, :] = jnp.where(low, first, pltpu.roll(second, 64, 1))
                    out_ref[to + 2 : to + 3, :] = jnp.where(low, pltpu.roll(first, 64, 1), second)


def split_nodes(nodes):
    out = jax.ShapeDtypeStruct((48, 128), jnp.float32)
    return call(split_kernel, out, [nodes], [pltpu.VMEM((48, 128), jnp.float32)], "split_nodes")


def join_kernel(first_ref, second_ref, out_first_ref, out_second_ref, rows_ref):
    low = lax.broadcasted_iota(jnp.int32, (1, 128), 1) < 64
    for i, new_ref in enumerate((first_ref, second_ref)):
        for c in range(3):
            for az in range(2):
                for ay in range(2):
                    for ey in range(2):
                        at = (c * 8 + az * 4 + ay * 2) * 2 + ey
                        even = new_ref[at : at + 1, :]
                        odd = new_ref[at + 2 : at + 3, :]
                        to = i * 48 + c * 16 + az * 4 + ey * 2 + ay
                        rows_ref[to : to + 1, :] = jnp.where(low, even, pltpu.roll(odd, 64, 1))
                        rows_ref[to + 8 : to + 9, :] = jnp.where(low, pltpu.roll(even, 64, 1), odd)
    rows = jnp.dot(
        rows_ref[...], interleave(True), precision=lax.Precision.HIGHEST, preferred_element_type=jnp.float32
    )
    out_first_ref[...] = rows[:48].reshape(3, 4, 4, 128)
    out_second_ref[...] = rows[48:].reshape(3, 4, 4, 128)


def join_nodes(first, second):
    out = jax.ShapeDtypeStruct((3, 4, 4, 128), jnp.float32)
    return call(join_kernel, [out, out], [first, second], [pltpu.VMEM((96, 128), jnp.float32)], "join_nodes")


def finish_kernel(own_ref, move_ref, first_ref, second_ref, out_ref, coeff_ref):
    second = add_up(second_ref)
    step = newton_step(second)
    for c in range(3):
        for z in range(4):
            out_ref[c, z] = own_ref[c, z] + step * move_ref[c, z]
    coeff_ref[0:1, :] = add_up(first_ref)[:, :5] * (1.0 / 32768.0)
    coeff_ref[1:2, :] = second[:, :5] * (1.0 / 32768.0)


def finish(own, move, first, second):
    outs = [jax.ShapeDtypeStruct((3, 4, 4, 128), jnp.float32), jax.ShapeDtypeStruct((2, 5), jnp.float32)]
    return call(finish_kernel, outs, [own, move, first, second], [], "finish")


def pack_kernel(elem_ref, coord_ref, out_ref):
    parts = [elem_ref[...].astype(jnp.float32)] + [coord_ref[j] for j in range(3)]
    for j, part in enumerate(parts):
        out_ref[:, 0, j * 128 : j * 128 + 128] = part[:128].T
    tails = jnp.concatenate([part[128:] for part in parts] + [jnp.zeros((96, 128), jnp.float32)], axis=0)
    out_ref[:, 0, 512:] = tails.T


def pack(elem, coord):
    return call(pack_kernel, jax.ShapeDtypeStruct((SRC, 1, 640), jnp.float32), [elem, coord], [], "pack")


def exchange(values):
    return lax.all_to_all(values, ("mesh", "bg"), split_axis=0, concat_axis=0, tiled=True)


def moved(values, axis, by):
    count = lax.axis_size(axis)
    return lax.ppermute(values, axis, [(i, (i - by) % count) for i in range(count)])


def along_mesh(block, merge):
    low, high = moved(block, "mesh", -1), moved(block, "mesh", 1)
    if merge:
        sides = [jnp.where(lax.broadcasted_iota(jnp.int32, block.shape, 1) < 64, high, low)]
    else:
        sides = [high, low]
    return jnp.concatenate([block] + sides, axis=0)


def along_bg(rows):
    return [rows, moved(rows, "bg", 1), moved(rows, "bg", -1)]


def shards(displacement, bg_coef, query_elem, query_point, query_coord):
    asked = exchange(pack(query_elem[0].T, query_coord[0].transpose(1, 2, 0)))
    prepared = prepare(bg_coef)
    rows = along_mesh(split_nodes(displacement), False)
    asked, rows = lax.optimization_barrier((asked, rows))
    found = exchange(lookup(asked, prepared))
    field = along_bg(rows)
    found, field = lax.optimization_barrier((found, field))
    sizes = along_bg(along_mesh(place(found, query_point[0].T), True))
    move, terms = newton_pass(field, None, sizes, None)
    first_terms = exchange(terms)
    shift = along_bg(along_mesh(move, False))
    last_move, last_terms, last_own = newton_pass(field, shift, sizes, first_terms)
    own, move = join_nodes(last_own, last_move)
    return finish(own, move, first_terms, exchange(last_terms))


def solution(mesh):
    in_specs = (
        P(None, "mesh", "bg", None),
        P(None, ("mesh", "bg")),
        P(("mesh", "bg"), None, None),
        P(("mesh", "bg"), None, None),
        P(("mesh", "bg"), None, None, None),
    )
    out_specs = (P(None, "mesh", "bg", None), P())
    return jax.shard_map(shards, mesh=mesh, in_specs=in_specs, out_specs=out_specs, check_vma=False)
```

```python
import functools

import jax
import jax.numpy as jnp
import numpy as np
from jax import lax
from jax.experimental import pallas as pl
from jax.experimental.pallas import tpu as pltpu
from jax.sharding import PartitionSpec as P

SRC = 128
SLOTS = 136
TABLE = 16384
COLS = 256


GATHER_ROWS = 80
ROUNDS = 10


def in_vmem(count):
    return [pl.BlockSpec(memory_space=pltpu.VMEM) for _ in range(count)]


def call(kernel, outs, args, scratch, far=(), last=False):
    args = [a if i in far else pltpu.with_memory_space_constraint(a, pltpu.VMEM) for i, a in enumerate(args)]
    many = isinstance(outs, list)
    if not last:
        outs = [pltpu.VMEM(o.shape, o.dtype) for o in outs] if many else pltpu.VMEM(outs.shape, outs.dtype)
    return pl.pallas_call(
        kernel,
        out_shape=outs,
        in_specs=in_vmem(len(args)),
        out_specs=in_vmem(len(outs)) if many else in_vmem(1)[0],
        scratch_shapes=scratch,
    )(*args)


def prepare_kernel(table_ref, split_ref, packed_ref, unit_ref):
    top = jnp.zeros((8, 128), jnp.float32)
    for block in range(TABLE // 128):
        top = jnp.maximum(top, jnp.abs(table_ref[:, block * 128 : block * 128 + 128]))
    top = jnp.maximum(jnp.max(top, keepdims=True), 1e-30)
    unit_ref[...] = jnp.broadcast_to(top * (1.0 / 32767.0), (8, 128))
    scale = 32767.0 / top

    def whole(values):
        return (values * scale + 32768.5).astype(jnp.int32) - 32768

    for block in range(TABLE // 256):
        low = table_ref[:, block * 128 : block * 128 + 128]
        high = table_ref[:, TABLE // 2 + block * 128 : TABLE // 2 + block * 128 + 128]
        packed_ref[:, block * 128 : block * 128 + 128] = (whole(high) << 16) | (whole(low) & 65535)
    for pair in range(TABLE // (2 * COLS)):
        start = pair * 2 * COLS
        rows = jnp.concatenate(
            [table_ref[:, start : start + COLS], table_ref[:, start + COLS : start + 2 * COLS]], axis=0
        )
        upper = rows.astype(jnp.bfloat16)
        split_ref[pair * 16 : pair * 16 + 16, :COLS] = upper
        split_ref[pair * 16 : pair * 16 + 16, COLS:] = (rows - upper.astype(jnp.float32)).astype(jnp.bfloat16)


def prepare(table):
    outs = [
        jax.ShapeDtypeStruct((8 * TABLE // COLS, 2 * COLS), jnp.bfloat16),
        jax.ShapeDtypeStruct((8, TABLE // 2), jnp.int32),
        jax.ShapeDtypeStruct((8, 128), jnp.float32),
    ]
    return call(prepare_kernel, outs, [table], [], far=(0,))


def choose(leaf, masks, first, count):
    if count == 1:
        return leaf(first)
    half = count // 2
    mask = masks[half.bit_length() - 1]
    return jnp.where(mask, choose(leaf, masks, first + half, half), choose(leaf, masks, first, half))


def weigh(coef, x, y, z):
    corner = lax.broadcasted_iota(jnp.int32, coef.shape, 0)
    weight_x = jnp.where((corner & 1) == 1, x, 1.0 - x)
    weight_y = jnp.where((corner & 2) == 2, y, 1.0 - y)
    weight_z = jnp.where((corner & 4) == 4, z, 1.0 - z)
    lsize = jnp.sum(weight_x * weight_y * weight_z * coef, axis=0, keepdims=True)
    return jnp.exp(-2.0 * lsize)


def lookup_kernel(asked_ref, split_ref, packed_ref, unit_ref, found_ref, turned_ref, result_ref, column_ref):
    for j in range(4):
        turned_ref[j * SLOTS : j * SLOTS + 128, :] = asked_ref[:, 0, j * 128 : j * 128 + 128].T
    tails = asked_ref[:, 0, 512:].T
    for j in range(4):
        turned_ref[j * SLOTS + 128 : (j + 1) * SLOTS, :] = tails[j * 8 : j * 8 + 8]
    column_ref[...] = lax.broadcasted_iota(jnp.int32, (COLS, 128), 0).astype(jnp.float32).astype(jnp.bfloat16)
    one = jnp.ones((), jnp.bfloat16)
    zero = jnp.zeros((), jnp.bfloat16)

    def step(i, carry):
        base = pl.multiple_of(i * 8, 8)
        ids, xs, ys, zs = (turned_ref[pl.ds(pl.multiple_of(j * SLOTS + base, 8), 8), :] for j in range(4))
        ids = ids.astype(jnp.int32)
        unit = unit_ref[...]
        for r in range(8):
            own = jnp.broadcast_to(ids[r : r + 1], (8, 128))
            lane = own & 127
            masks = [(own & (128 << bit)) != 0 for bit in range(6)]

            def leaf(block):
                return jnp.take_along_axis(packed_ref[:, block * 128 : block * 128 + 128], lane, axis=1)

            word = choose(leaf, masks, 0, 64)
            whole = jnp.where((own & (TABLE // 2)) != 0, word, word << 16) >> 16
            coef = whole.astype(jnp.float32) * unit
            result_ref[pl.ds(base + r, 1), :] = weigh(coef, xs[r : r + 1], ys[r : r + 1], zs[r : r + 1])

        start = jnp.minimum(GATHER_ROWS + i * 6, SLOTS - 6)
        for pair in range(3):
            at = start + 2 * pair
            pair_ids, px, py, pz = (
                jnp.concatenate(
                    [turned_ref[pl.ds(j * SLOTS + at, 1), :], turned_ref[pl.ds(j * SLOTS + at + 1, 1), :]], axis=1
                )
                for j in range(4)
            )
            pair_ids = pair_ids.astype(jnp.int32)
            column = (pair_ids & (COLS - 1)).astype(jnp.float32).astype(jnp.bfloat16)
            chosen = jnp.concatenate(
                [
                    jnp.where(column_ref[...] == column[:, half * 128 : half * 128 + 128], one, zero)
                    for half in range(2)
                ],
                axis=1,
            )
            picked = jnp.dot(split_ref[:, :COLS], chosen, preferred_element_type=jnp.float32) + jnp.dot(
                split_ref[:, COLS:], chosen, preferred_element_type=jnp.float32
            )
            own = jnp.broadcast_to(pair_ids, (8, 256))
            masks = [(own & (COLS << bit)) != 0 for bit in range(6)]
            coef = choose(lambda row: picked[row * 8 : row * 8 + 8], masks, 0, 64)
            value = weigh(coef, px, py, pz)
            result_ref[pl.ds(at, 1), :] = value[:, :128]
            result_ref[pl.ds(at + 1, 1), :] = value[:, 128:]
        return carry

    lax.fori_loop(0, ROUNDS, step, 0)
    found_ref[:, 0, :128] = result_ref[:128, :].T
    found_ref[:, 0, 128:] = result_ref[128:, :].T


def lookup(asked, prepared):
    scratch = [
        pltpu.VMEM((4 * SLOTS, 128), jnp.float32),
        pltpu.VMEM((SLOTS, 128), jnp.float32),
        pltpu.VMEM((COLS, 128), jnp.bfloat16),
    ]
    out = jax.ShapeDtypeStruct((SRC, 1, SLOTS), jnp.float32)
    return call(lookup_kernel, out, [asked, *prepared], scratch)


def place_kernel(found_ref, point_ref, size_ref, value_ref, row_ref, lane_ref, at_ref):
    value_ref[:128, :] = found_ref[:, 0, :128].T
    value_ref[128:, :] = found_ref[:, 0, 128:].T
    point = point_ref[...]
    line = (point * 10923) >> 21
    qx = point - line * 192
    qz = (line * 43) >> 8
    qy = line - qz * 6
    ex = (qx * 171) >> 9
    jx = qx - ex * 3
    ey = (qy * 11) >> 5
    jy = qy - ey * 3
    ez = (qz * 11) >> 5
    jz = qz - ez * 3
    row_ref[...] = (((jz * 3 + jy) * 3 + jx) * 2 + ey).astype(jnp.float32)
    lane_ref[...] = (ez * 64 + ex).astype(jnp.float32)
    at_ref[...] = lax.broadcasted_iota(jnp.int32, (128, 128), 0).astype(jnp.float32).astype(jnp.bfloat16)
    one = jnp.ones((), jnp.bfloat16)
    zero = jnp.zeros((), jnp.bfloat16)

    def step(i, total):
        base = pl.multiple_of(i * 8, 8)
        values = value_ref[pl.ds(base, 8), :]
        rows = row_ref[pl.ds(base, 8), :]
        lanes = lane_ref[pl.ds(base, 8), :]
        left, right = [], []
        for r in range(8):
            value = values[r : r + 1]
            upper = value.astype(jnp.bfloat16)
            lower = (value - upper.astype(jnp.float32)).astype(jnp.bfloat16)
            row = at_ref[:64, :] == rows[r : r + 1].astype(jnp.bfloat16)
            left.append(jnp.concatenate([jnp.where(row, upper, zero), jnp.where(row, lower, zero)], axis=0))
            right.append(jnp.where(at_ref[...] == lanes[r : r + 1].astype(jnp.bfloat16), one, zero))
        left = jnp.concatenate(left, axis=1)
        right = jnp.concatenate(right, axis=1)
        return total + lax.dot_general(left, right, (((1,), (1,)), ((), ())), preferred_element_type=jnp.float32)

    total = lax.fori_loop(0, SLOTS // 8, step, jnp.zeros((128, 128), jnp.float32))
    size_ref[...] = total[:56] + total[64:120]


def place(found, point):
    scratch = [pltpu.VMEM((SLOTS, 128), jnp.float32) for _ in range(3)] + [pltpu.VMEM((128, 128), jnp.bfloat16)]
    return call(place_kernel, jax.ShapeDtypeStruct((56, 128), jnp.float32), [found, point], scratch, far=(1,))


HALF_GAP = float(np.sqrt(0.15))
OUTER, MIDDLE = 5.0 / 18.0, 8.0 / 18.0


def field_pieces(refs):
    return {(z, y): (refs[y], (z % 3) * 48) for z in (-1, 0, 1) for y in (-1, 0, 1)}


def size_pieces(refs):
    return {(z, y): (refs[y], 56 * abs(z)) for z in (-1, 0, 1) for y in (-1, 0, 1)}


def lane_index():
    return lax.broadcasted_iota(jnp.int32, (8, 128), 1)


def x_up(v):
    return jnp.where((lane_index() & 63) == 63, pltpu.roll(v, 63, 1), pltpu.roll(v, 127, 1))


def x_down(v):
    return jnp.where((lane_index() & 63) == 0, pltpu.roll(v, 65, 1), pltpu.roll(v, 1, 1))


def z_down(v):
    turned = pltpu.roll(v, 64, 1)
    return jnp.where(lane_index() < 64, pltpu.roll(turned, 4, 0), turned)


def y_down(v):
    return pltpu.roll(v, 1, 0)


def spread(low, mid, high, slopes=True, values=True):
    bend = (low + high) - 2.0 * mid
    rise = high - low
    vals = slps = None
    if values:
        centre = mid + (2.0 * HALF_GAP * HALF_GAP) * bend
        lean = HALF_GAP * rise
        vals = (centre - lean, mid, centre + lean)
    if slopes:
        change = (4.0 * HALF_GAP) * bend
        slps = (rise - change, rise, rise + change)
    return vals, slps


def collect(vals, slps):
    bend = rise = mid = None
    if vals is not None:
        outer = vals[0] + vals[2]
        bend = (2.0 * HALF_GAP * HALF_GAP) * outer
        rise = HALF_GAP * (vals[2] - vals[0])
        mid = outer + vals[1]
    if slps is not None:
        slope_bend = (4.0 * HALF_GAP) * (slps[2] - slps[0])
        slope_rise = (slps[0] + slps[2]) + slps[1]
        bend = slope_bend if bend is None else bend + slope_bend
        rise = slope_rise if rise is None else rise + slope_rise
    twice = -2.0 * bend
    return bend - rise, twice if mid is None else mid + twice, bend + rise


def at_point(c, k, jz, jy, jx):
    row = (((jz * 3 + jy) * 3 + jx) * 9 + k) * 8
    return pl.ds(pl.multiple_of(row + c * 24, 8), 8)


def forward(local, out_ref, at):
    along_z = [[spread(local(0, y, x), local(1, y, x), local(2, y, x)) for x in range(3)] for y in range(3)]
    for jz in range(3):
        value = [[along_z[y][x][0][jz] for x in range(3)] for y in range(3)]
        slope = [[along_z[y][x][1][jz] for x in range(3)] for y in range(3)]
        plain = [spread(value[0][x], value[1][x], value[2][x]) for x in range(3)]
        steep = [spread(slope[0][x], slope[1][x], slope[2][x], slopes=False)[0] for x in range(3)]
        for jy in range(3):
            dx = spread(*(plain[x][0][jy] for x in range(3)), values=False)[1]
            dy = spread(*(plain[x][1][jy] for x in range(3)), slopes=False)[0]
            dz = spread(*(steep[x][jy] for x in range(3)), slopes=False)[0]
            for jx in range(3):
                for k, part in enumerate((dx, dy, dz)):
                    out_ref[at(k, jz, jy, jx), :] = part[jx]


def backward(c, from_ref, out_ref):
    planes = []
    for jz in range(3):
        lines = []
        for jy in range(3):
            dx, dy, dz = (
                tuple(from_ref[at_point(c, k, jz, jy, jx), :] for jx in range(3)) for k in range(3)
            )
            lines.append((collect(None, dx), collect(dy, None), collect(dz, None)))
        value = [
            collect(tuple(lines[jy][0][x] for jy in range(3)), tuple(lines[jy][1][x] for jy in range(3)))
            for x in range(3)
        ]
        slope = [collect(tuple(lines[jy][2][x] for jy in range(3)), None) for x in range(3)]
        planes.append((value, slope))
    whole = [
        [
            collect(
                tuple(planes[jz][0][x][y] for jz in range(3)), tuple(planes[jz][1][x][y] for jz in range(3))
            )
            for x in range(3)
        ]
        for y in range(3)
    ]
    folded_x = [[(whole[y][0][z] + x_down(whole[y][2][z]), whole[y][1][z]) for z in range(3)] for y in range(3)]
    for x in range(2):
        folded = [(folded_x[0][z][x] + y_down(folded_x[2][z][x]), folded_x[1][z][x]) for z in range(3)]
        for y in range(2):
            for z, node in enumerate((folded[0][y] + z_down(folded[2][y]), folded[1][y])):
                row = (z * 4 + y * 2 + x) * 8
                out_ref[pl.ds(pl.multiple_of(row + c * 64, 8), 8), :] = node


def symmetric(build):
    upper = {(k, l): build(k, l) for k in range(3) for l in range(k, 3)}
    return {(k, l): upper[min(k, l), max(k, l)] for k in range(3) for l in range(3)}


def inner(a, b):
    square = (a[0, 0] * b[0, 0] + a[1, 1] * b[1, 1]) + a[2, 2] * b[2, 2]
    cross = (a[0, 1] * b[0, 1] + a[0, 2] * b[0, 2]) + a[1, 2] * b[1, 2]
    return square + 2.0 * cross


def column_dot(a, b, k, l):
    return (a[0][k] * b[0][l] + a[1][k] * b[1][l]) + a[2][k] * b[2][l]


def load_tensor(ref, jz, jy, jx):
    tensor = [[ref[at_point(c, k, jz, jy, jx), :] for k in range(3)] for c in range(3)]
    return tensor


def jacobian_at(ref, jz, jy, jx):
    tensor = load_tensor(ref, jz, jy, jx)
    return [[tensor[c][k] + 1.0 if c == k else tensor[c][k] for k in range(3)] for c in range(3)]


def strain_of(jac, size):
    return symmetric(lambda k, l: column_dot(jac, jac, k, l) * size - (1.0 if k == l else 0.0))


def weight_at(jz, jy, jx):
    along_z = jnp.where(jz == 1, MIDDLE, OUTER).astype(jnp.float32)
    return along_z * ((MIDDLE if jy == 1 else OUTER) * (MIDDLE if jx == 1 else OUTER))


def newton_step(totals):
    _, linear, quadratic, cubic, quartic, floor = (totals[:, i : i + 1] for i in range(6))
    step = jnp.zeros_like(linear)
    for _ in range(4):
        slope = linear + step * (2.0 * quadratic + step * (3.0 * cubic + step * 4.0 * quartic))
        curvature = 2.0 * quadratic + step * (6.0 * cubic + step * 12.0 * quartic)
        step = step - slope / jnp.maximum(curvature, floor + 1e-06)
    return step


def add_up(terms_ref):
    return jnp.sum(terms_ref[...], axis=0, keepdims=True)


def ring(pieces, count, out_ref, out_at, z_shift, y_shift):
    low = lax.broadcasted_iota(jnp.int32, (count, 128), 1) < 64
    places = ((-1, 1), (0, 0), (0, 1), (1, 0)) if not y_shift else ((0, 0), (0, 1), (1, 0), (1, 1))
    for upper in range(2):
        for y, (piece_y, row) in enumerate(places):
            here, below, above = (
                ref[pl.ds(at + row, count, stride=2), :] for ref, at in (pieces[z, piece_y] for z in (0, -1, 1))
            )
            if z_shift:
                here = pltpu.roll(here, 64, 1)
                above = pltpu.roll(above, 64, 1)
                value = jnp.where(low, above, here) if upper else jnp.where(low, here, above)
            elif upper:
                value = jnp.where(low, above, below)
            else:
                value = here
            out_ref[pl.ds(out_at + upper * 4 + y, count, stride=8), :] = value


def pass_kernel(first, *refs):
    refs = list(refs)
    field_refs = [refs.pop(0) for _ in range(3)]
    if not first:
        shift_refs = [refs.pop(0) for _ in range(3)]
    sizes = size_pieces([refs.pop(0) for _ in range(3)])
    if first:
        move_ref, terms_out, nodes_ref, size_ref, jac_ref, part_ref, turn_ref = refs
        field = field_pieces(field_refs)
    else:
        terms_in, move_ref, terms_out, own_ref, nodes_ref, size_ref, jac_ref, part_ref, turn_ref, sum_ref = refs
        step = newton_step(add_up(terms_in))
        for i, (field_ref, shift_ref) in enumerate(zip(field_refs, shift_refs)):
            sum_ref[i] = field_ref[...] + step * shift_ref[...]
        field = field_pieces([sum_ref.at[i] for i in range(3)])
        own_ref[...] = sum_ref[0, :48, :]
    for z_shift in range(2):
        for y_shift in range(2):
            ring(field, 24, nodes_ref, (z_shift * 2 + y_shift) * 192, z_shift, y_shift)
    ring(sizes, 27, size_ref, 0, 0, 0)

    def known(c):
        def local(z, y, x):
            row = ((z == 2) * 2 + (y == 2)) * 192 + ((z % 2) * 4 + (y % 2) * 2 + x % 2) * 8
            value = nodes_ref[pl.ds(pl.multiple_of(row + c * 64, 8), 8), :]
            return x_up(value) if x == 2 else value

        return local

    def packed(node, upper, shift):
        rows = [
            turn_ref[pl.ds(node * 8 + upper * 4 + 1 + shift + ey, 4, stride=64), :] for ey in range(2)
        ]
        return jnp.concatenate(rows, axis=0)

    def sought(z, y, x):
        node = (z % 2) * 4 + (y % 2) * 2 + x % 2
        shift = y // 2
        value = packed(node, 0, shift)
        if z == 2:
            turned = pltpu.roll(value, 64, 1)
            value = jnp.where(lane_index() < 64, turned, pltpu.roll(packed(node, 1, shift), 64, 1))
        return x_up(value) if x == 2 else value

    def each(body):
        def run(i, carry):
            body(i)
            return carry

        lax.fori_loop(0, 3, run, 0)

    def size_at(jz, jy, jx):
        return size_ref[pl.ds(pl.multiple_of((jz * 9 + jy * 3 + jx) * 8, 8), 8), :]

    each(lambda c: forward(known(c), jac_ref, functools.partial(at_point, c)))
    turn_ref[192:, :] = jnp.zeros((64, 128), jnp.float32)

    def stress(jz):
        for jy in range(3):
            for jx in range(3):
                jac = jacobian_at(jac_ref, jz, jy, jx)
                size = size_at(jz, jy, jx)
                strain = strain_of(jac, size)
                scale = size * (-4.0 * weight_at(jz, jy, jx))
                for c in range(3):
                    for k in range(3):
                        part = (strain[k, 0] * jac[c][0] + strain[k, 1] * jac[c][1]) + strain[k, 2] * jac[c][2]
                        part_ref[at_point(c, k, jz, jy, jx), :] = part * scale

    each(stress)
    each(lambda c: backward(c, part_ref, turn_ref))
    for row in range(2):
        move_ref[pl.ds(row, 24, stride=2), :] = turn_ref[pl.ds(row + 1, 24, stride=8), :]
    forward(sought, part_ref, lambda k, jz, jy, jx: pl.ds(((jz * 9 + jy * 3 + jx) * 3 + k) * 8, 8))

    sub = lax.broadcasted_iota(jnp.int32, (8, 128), 0)
    sums = [jnp.zeros((8, 128), jnp.float32) for _ in range(6)]
    for start, fresh in ((0, 0), (8, 8), (16, 16), (19, 24)):
        weight = jnp.zeros((8, 128), jnp.float32)
        for i in range(fresh - start, 8):
            point = start + i
            parts = [MIDDLE if (point // by) % 3 == 1 else OUTER for by in (9, 3, 1)]
            weight = jnp.where(sub == i, (parts[0] * parts[1]) * parts[2], weight)
        for ey in range(2):
            jac = [
                [jac_ref[pl.ds((start * 9 + c * 3 + k) * 8 + 1 + ey, 8, stride=72), :] for k in range(3)]
                for c in range(3)
            ]
            jac = [[jac[c][k] + 1.0 if c == k else jac[c][k] for k in range(3)] for c in range(3)]
            motion = [
                [part_ref[pl.ds((start * 3 + k) * 8 + ey * 4 + c, 8, stride=24), :] for k in range(3)]
                for c in range(3)
            ]
            size = size_ref[pl.ds(start * 8 + 1 + ey, 8, stride=8), :]
            zero = strain_of(jac, size)
            one = symmetric(lambda k, l: (column_dot(jac, motion, k, l) + column_dot(motion, jac, k, l)) * size)
            two = symmetric(lambda k, l: column_dot(motion, motion, k, l) * size)
            pairs = ((zero, zero), (zero, one), (zero, two), (one, two), (two, two), (one, one))
            sums = [total + weight * inner(*pair) for total, pair in zip(sums, pairs)]
    zz, zo, zt, ot, tt, gn = (jnp.sum(total, keepdims=True) for total in sums)
    lane = lax.broadcasted_iota(jnp.int32, (1, 128), 1)
    terms = jnp.zeros((1, 128), jnp.float32)
    for i, term in enumerate((zz, 2.0 * zo, gn + 2.0 * zt, 2.0 * ot, tt, gn)):
        terms = jnp.where(lane == i, term, terms)
    terms_out[...] = jnp.broadcast_to(terms, (SRC, 128))


def newton_pass(field, shift, sizes, terms):
    first = shift is None
    node = jax.ShapeDtypeStruct((48, 128), jnp.float32)
    outs = [node, jax.ShapeDtypeStruct((SRC, 128), jnp.float32)] + ([] if first else [node])
    scratch = [
        pltpu.VMEM((4 * 192, 128), jnp.float32),
        pltpu.VMEM((27 * 8, 128), jnp.float32),
        pltpu.VMEM((243 * 8, 128), jnp.float32),
        pltpu.VMEM((243 * 8, 128), jnp.float32),
        pltpu.VMEM((32 * 8, 128), jnp.float32),
    ] + ([] if first else [pltpu.VMEM((3, 144, 128), jnp.float32)])
    args = list(field) + ([] if first else list(shift)) + list(sizes) + ([] if first else [terms])
    return call(functools.partial(pass_kernel, first), outs, args, scratch)


def interleave(back):
    row = lax.broadcasted_iota(jnp.int32, (128, 128), 0)
    col = lax.broadcasted_iota(jnp.int32, (128, 128), 1)
    if back:
        row, col = col, row
    return (col == (row & 1) * 64 + (row >> 1)).astype(jnp.float32)


def split_kernel(nodes_ref, out_ref, rows_ref):
    rows = nodes_ref[...].reshape(48, 128)
    rows_ref[...] = jnp.dot(rows, interleave(False), precision=lax.Precision.HIGHEST, preferred_element_type=jnp.float32)
    low = lax.broadcasted_iota(jnp.int32, (1, 128), 1) < 64
    for c in range(3):
        for az in range(2):
            for ay in range(2):
                for ey in range(2):
                    at = c * 16 + az * 4 + ey * 2 + ay
                    first = rows_ref[at : at + 1, :]
                    second = rows_ref[at + 8 : at + 9, :]
                    to = (c * 8 + az * 4 + ay * 2) * 2 + ey
                    out_ref[to : to + 1, :] = jnp.where(low, first, pltpu.roll(second, 64, 1))
                    out_ref[to + 2 : to + 3, :] = jnp.where(low, pltpu.roll(first, 64, 1), second)


def split_nodes(nodes):
    out = jax.ShapeDtypeStruct((48, 128), jnp.float32)
    return call(split_kernel, out, [nodes], [pltpu.VMEM((48, 128), jnp.float32)], far=(0,))


def join_kernel(first_ref, second_ref, out_first_ref, out_second_ref, rows_ref):
    low = lax.broadcasted_iota(jnp.int32, (1, 128), 1) < 64
    for i, new_ref in enumerate((first_ref, second_ref)):
        for c in range(3):
            for az in range(2):
                for ay in range(2):
                    for ey in range(2):
                        at = (c * 8 + az * 4 + ay * 2) * 2 + ey
                        even = new_ref[at : at + 1, :]
                        odd = new_ref[at + 2 : at + 3, :]
                        to = i * 48 + c * 16 + az * 4 + ey * 2 + ay
                        rows_ref[to : to + 1, :] = jnp.where(low, even, pltpu.roll(odd, 64, 1))
                        rows_ref[to + 8 : to + 9, :] = jnp.where(low, pltpu.roll(even, 64, 1), odd)
    rows = jnp.dot(
        rows_ref[...], interleave(True), precision=lax.Precision.HIGHEST, preferred_element_type=jnp.float32
    )
    out_first_ref[...] = rows[:48].reshape(3, 4, 4, 128)
    out_second_ref[...] = rows[48:].reshape(3, 4, 4, 128)


def join_nodes(first, second):
    out = jax.ShapeDtypeStruct((3, 4, 4, 128), jnp.float32)
    return call(join_kernel, [out, out], [first, second], [pltpu.VMEM((96, 128), jnp.float32)])


def finish_kernel(own_ref, move_ref, first_ref, second_ref, out_ref, coeff_ref):
    second = add_up(second_ref)
    step = newton_step(second)
    for c in range(3):
        for z in range(4):
            out_ref[c, z] = own_ref[c, z] + step * move_ref[c, z]
    coeff_ref[0:1, :] = add_up(first_ref)[:, :5] * (1.0 / 32768.0)
    coeff_ref[1:2, :] = second[:, :5] * (1.0 / 32768.0)


def finish(own, move, first, second):
    outs = [jax.ShapeDtypeStruct((3, 4, 4, 128), jnp.float32), jax.ShapeDtypeStruct((2, 5), jnp.float32)]
    return call(finish_kernel, outs, [own, move, first, second], [], last=True)


def pack_kernel(elem_ref, coord_ref, out_ref):
    parts = [elem_ref[...].astype(jnp.float32)] + [coord_ref[j] for j in range(3)]
    for j, part in enumerate(parts):
        out_ref[:, 0, j * 128 : j * 128 + 128] = part[:128].T
    tails = jnp.concatenate([part[128:] for part in parts] + [jnp.zeros((96, 128), jnp.float32)], axis=0)
    out_ref[:, 0, 512:] = tails.T


def pack(elem, coord):
    return call(pack_kernel, jax.ShapeDtypeStruct((SRC, 1, 640), jnp.float32), [elem, coord], [], far=(0, 1))


def exchange(values):
    return lax.all_to_all(values, ("mesh", "bg"), split_axis=0, concat_axis=0, tiled=True)


def moved(values, axis, by):
    count = lax.axis_size(axis)
    return lax.ppermute(values, axis, [(i, (i - by) % count) for i in range(count)])


def along_mesh(block, merge):
    low, high = moved(block, "mesh", -1), moved(block, "mesh", 1)
    if merge:
        sides = [jnp.where(lax.broadcasted_iota(jnp.int32, block.shape, 1) < 64, high, low)]
    else:
        sides = [high, low]
    return jnp.concatenate([block] + sides, axis=0)


def along_bg(rows):
    return [rows, moved(rows, "bg", 1), moved(rows, "bg", -1)]


def shards(displacement, bg_coef, query_elem, query_point, query_coord):
    asked = exchange(pack(query_elem[0].T, query_coord[0].transpose(1, 2, 0)))
    own = split_nodes(displacement)
    asked, prepared, own = lax.optimization_barrier((asked, prepare(bg_coef), own))
    found, own = lax.optimization_barrier((lookup(asked, prepared), own))
    found = exchange(found)
    field = along_bg(along_mesh(own, False))
    found, field = lax.optimization_barrier((found, field))
    sizes = along_bg(along_mesh(place(found, query_point[0].T), True))
    move, terms = newton_pass(field, None, sizes, None)
    first_terms = exchange(terms)
    shift = along_bg(along_mesh(move, False))
    last_move, last_terms, last_own = newton_pass(field, shift, sizes, first_terms)
    own, move = join_nodes(last_own, last_move)
    last_terms = exchange(last_terms)
    return finish(own, move, first_terms, last_terms)


def solution(mesh):
    in_specs = (
        P(None, "mesh", "bg", None),
        P(None, ("mesh", "bg")),
        P(("mesh", "bg"), None, None),
        P(("mesh", "bg"), None, None),
        P(("mesh", "bg"), None, None, None),
    )
    out_specs = (P(None, "mesh", "bg", None), P())
    return jax.shard_map(shards, mesh=mesh, in_specs=in_specs, out_specs=out_specs, check_vma=False)
```

```python
import functools

import jax
import jax.numpy as jnp
import numpy as np
from jax import lax
from jax.experimental import pallas as pl
from jax.experimental.pallas import tpu as pltpu
from jax.sharding import PartitionSpec as P

SRC = 128
SLOTS = 136
TABLE = 16384
COLS = 256


GATHER_ROWS = 64
ROUNDS = 8


def in_vmem(count):
    return [pl.BlockSpec(memory_space=pltpu.VMEM) for _ in range(count)]


def call(kernel, outs, args, scratch, far=(), last=False):
    args = [a if i in far else pltpu.with_memory_space_constraint(a, pltpu.VMEM) for i, a in enumerate(args)]
    many = isinstance(outs, list)
    if not last:
        outs = [pltpu.VMEM(o.shape, o.dtype) for o in outs] if many else pltpu.VMEM(outs.shape, outs.dtype)
    return pl.pallas_call(
        kernel,
        out_shape=outs,
        in_specs=in_vmem(len(args)),
        out_specs=in_vmem(len(outs)) if many else in_vmem(1)[0],
        scratch_shapes=scratch,
    )(*args)


def prepare_kernel(table_ref, split_ref, packed_ref, unit_ref):
    top = jnp.zeros((8, 128), jnp.float32)
    for block in range(TABLE // 128):
        top = jnp.maximum(top, jnp.abs(table_ref[:, block * 128 : block * 128 + 128]))
    top = jnp.maximum(jnp.max(top, keepdims=True), 1e-30)
    unit_ref[...] = jnp.broadcast_to(top * (1.0 / 32767.0), (8, 128))
    scale = 32767.0 / top

    def whole(values):
        return (values * scale + 32768.5).astype(jnp.int32) - 32768

    for block in range(TABLE // 256):
        low = table_ref[:, block * 128 : block * 128 + 128]
        high = table_ref[:, TABLE // 2 + block * 128 : TABLE // 2 + block * 128 + 128]
        packed_ref[:, block * 128 : block * 128 + 128] = (whole(high) << 16) | (whole(low) & 65535)
    for pair in range(TABLE // (2 * COLS)):
        start = pair * 2 * COLS
        rows = jnp.concatenate(
            [table_ref[:, start : start + COLS], table_ref[:, start + COLS : start + 2 * COLS]], axis=0
        )
        upper = rows.astype(jnp.bfloat16)
        split_ref[pair * 16 : pair * 16 + 16, :COLS] = upper
        split_ref[pair * 16 : pair * 16 + 16, COLS:] = (rows - upper.astype(jnp.float32)).astype(jnp.bfloat16)


def prepare(table):
    outs = [
        jax.ShapeDtypeStruct((8 * TABLE // COLS, 2 * COLS), jnp.bfloat16),
        jax.ShapeDtypeStruct((8, TABLE // 2), jnp.int32),
        jax.ShapeDtypeStruct((8, 128), jnp.float32),
    ]
    return call(prepare_kernel, outs, [table], [], far=(0,))


def choose(leaf, masks, first, count):
    if count == 1:
        return leaf(first)
    half = count // 2
    mask = masks[half.bit_length() - 1]
    return jnp.where(mask, choose(leaf, masks, first + half, half), choose(leaf, masks, first, half))


def weigh(coef, x, y, z):
    corner = lax.broadcasted_iota(jnp.int32, coef.shape, 0)
    weight_x = jnp.where((corner & 1) == 1, x, 1.0 - x)
    weight_y = jnp.where((corner & 2) == 2, y, 1.0 - y)
    weight_z = jnp.where((corner & 4) == 4, z, 1.0 - z)
    lsize = jnp.sum(weight_x * weight_y * weight_z * coef, axis=0, keepdims=True)
    return jnp.exp(-2.0 * lsize)


def lookup_kernel(asked_ref, split_ref, packed_ref, unit_ref, found_ref, turned_ref, result_ref, column_ref):
    for j in range(4):
        turned_ref[j * SLOTS : j * SLOTS + 128, :] = asked_ref[:, 0, j * 128 : j * 128 + 128].T
    tails = asked_ref[:, 0, 512:].T
    for j in range(4):
        turned_ref[j * SLOTS + 128 : (j + 1) * SLOTS, :] = tails[j * 8 : j * 8 + 8]
    column_ref[...] = lax.broadcasted_iota(jnp.int32, (COLS, 128), 0).astype(jnp.float32).astype(jnp.bfloat16)
    one = jnp.ones((), jnp.bfloat16)
    zero = jnp.zeros((), jnp.bfloat16)

    def step(i, carry):
        base = pl.multiple_of(i * 8, 8)
        ids, xs, ys, zs = (turned_ref[pl.ds(pl.multiple_of(j * SLOTS + base, 8), 8), :] for j in range(4))
        ids = ids.astype(jnp.int32)
        unit = unit_ref[...]
        for r in range(8):
            own = jnp.broadcast_to(ids[r : r + 1], (8, 128))
            lane = own & 127
            masks = [(own & (128 << bit)) != 0 for bit in range(6)]

            def leaf(block):
                return jnp.take_along_axis(packed_ref[:, block * 128 : block * 128 + 128], lane, axis=1)

            word = choose(leaf, masks, 0, 64)
            whole = jnp.where((own & (TABLE // 2)) != 0, word, word << 16) >> 16
            coef = whole.astype(jnp.float32) * unit
            result_ref[pl.ds(base + r, 1), :] = weigh(coef, xs[r : r + 1], ys[r : r + 1], zs[r : r + 1])

        start = GATHER_ROWS + i * 9
        for pair in range(5):
            at = start + 2 * pair
            wide = 2 if pair < 4 else 1
            pair_ids, px, py, pz = (
                jnp.concatenate([turned_ref[pl.ds(j * SLOTS + at + k, 1), :] for k in range(wide)], axis=1)
                for j in range(4)
            )
            pair_ids = pair_ids.astype(jnp.int32)
            column = (pair_ids & (COLS - 1)).astype(jnp.float32).astype(jnp.bfloat16)
            chosen = jnp.concatenate(
                [
                    jnp.where(column_ref[...] == column[:, half * 128 : half * 128 + 128], one, zero)
                    for half in range(wide)
                ],
                axis=1,
            )
            picked = jnp.dot(split_ref[:, :COLS], chosen, preferred_element_type=jnp.float32) + jnp.dot(
                split_ref[:, COLS:], chosen, preferred_element_type=jnp.float32
            )
            own = jnp.broadcast_to(pair_ids, (8, 128 * wide))
            masks = [(own & (COLS << bit)) != 0 for bit in range(6)]
            coef = choose(lambda row: picked[row * 8 : row * 8 + 8], masks, 0, 64)
            value = weigh(coef, px, py, pz)
            for k in range(wide):
                result_ref[pl.ds(at + k, 1), :] = value[:, k * 128 : k * 128 + 128]
        return carry

    lax.fori_loop(0, ROUNDS, step, 0)
    found_ref[:, 0, :128] = result_ref[:128, :].T
    found_ref[:, 0, 128:] = result_ref[128:, :].T


def lookup(asked, prepared):
    scratch = [
        pltpu.VMEM((4 * SLOTS, 128), jnp.float32),
        pltpu.VMEM((SLOTS, 128), jnp.float32),
        pltpu.VMEM((COLS, 128), jnp.bfloat16),
    ]
    out = jax.ShapeDtypeStruct((SRC, 1, SLOTS), jnp.float32)
    return call(lookup_kernel, out, [asked, *prepared], scratch)


def place_kernel(found_ref, point_ref, size_ref, value_ref, row_ref, lane_ref, at_ref):
    value_ref[:128, :] = found_ref[:, 0, :128].T
    value_ref[128:, :] = found_ref[:, 0, 128:].T
    point = point_ref[...]
    line = (point * 10923) >> 21
    qx = point - line * 192
    qz = (line * 43) >> 8
    qy = line - qz * 6
    ex = (qx * 171) >> 9
    jx = qx - ex * 3
    ey = (qy * 11) >> 5
    jy = qy - ey * 3
    ez = (qz * 11) >> 5
    jz = qz - ez * 3
    row_ref[...] = (((jz * 3 + jy) * 3 + jx) * 2 + ey).astype(jnp.float32)
    lane_ref[...] = (ez * 64 + ex).astype(jnp.float32)
    at_ref[...] = lax.broadcasted_iota(jnp.int32, (128, 128), 0).astype(jnp.float32).astype(jnp.bfloat16)
    one = jnp.ones((), jnp.bfloat16)
    zero = jnp.zeros((), jnp.bfloat16)

    def step(i, total):
        values = value_ref[i * 8 : i * 8 + 8, :]
        rows = row_ref[i * 8 : i * 8 + 8, :]
        lanes = lane_ref[i * 8 : i * 8 + 8, :]
        left, right = [], []
        for r in range(8):
            value = values[r : r + 1]
            upper = value.astype(jnp.bfloat16)
            lower = (value - upper.astype(jnp.float32)).astype(jnp.bfloat16)
            row = at_ref[:64, :] == rows[r : r + 1].astype(jnp.bfloat16)
            left.append(jnp.concatenate([jnp.where(row, upper, zero), jnp.where(row, lower, zero)], axis=0))
            right.append(jnp.where(at_ref[...] == lanes[r : r + 1].astype(jnp.bfloat16), one, zero))
        left = jnp.concatenate(left, axis=1)
        right = jnp.concatenate(right, axis=1)
        return total + lax.dot_general(left, right, (((1,), (1,)), ((), ())), preferred_element_type=jnp.float32)

    total = jnp.zeros((128, 128), jnp.float32)
    for i in range(SLOTS // 8):
        total = step(i, total)
    size_ref[...] = total[:56] + total[64:120]


def place(found, point):
    scratch = [pltpu.VMEM((SLOTS, 128), jnp.float32) for _ in range(3)] + [pltpu.VMEM((128, 128), jnp.bfloat16)]
    return call(place_kernel, jax.ShapeDtypeStruct((56, 128), jnp.float32), [found, point], scratch, far=(1,))


HALF_GAP = float(np.sqrt(0.15))
OUTER, MIDDLE = 5.0 / 18.0, 8.0 / 18.0


def field_pieces(refs):
    return {(z, y): (refs[y], (z % 3) * 48) for z in (-1, 0, 1) for y in (-1, 0, 1)}


def size_pieces(refs):
    own, z_low, y_low, corner = refs
    return {(0, 0): own, (-1, 0): z_low, (0, -1): y_low, (-1, -1): corner}


def lane_index():
    return lax.broadcasted_iota(jnp.int32, (8, 128), 1)


def x_up(v):
    return jnp.where((lane_index() & 63) == 63, pltpu.roll(v, 63, 1), pltpu.roll(v, 127, 1))


def x_down(v):
    return jnp.where((lane_index() & 63) == 0, pltpu.roll(v, 65, 1), pltpu.roll(v, 1, 1))


def z_down(v):
    turned = pltpu.roll(v, 64, 1)
    return jnp.where(lane_index() < 64, pltpu.roll(turned, 4, 0), turned)


def y_down(v):
    return pltpu.roll(v, 1, 0)


def spread(low, mid, high, slopes=True, values=True):
    bend = (low + high) - 2.0 * mid
    rise = high - low
    vals = slps = None
    if values:
        centre = mid + (2.0 * HALF_GAP * HALF_GAP) * bend
        lean = HALF_GAP * rise
        vals = (centre - lean, mid, centre + lean)
    if slopes:
        change = (4.0 * HALF_GAP) * bend
        slps = (rise - change, rise, rise + change)
    return vals, slps


def collect(vals, slps):
    bend = rise = mid = None
    if vals is not None:
        outer = vals[0] + vals[2]
        bend = (2.0 * HALF_GAP * HALF_GAP) * outer
        rise = HALF_GAP * (vals[2] - vals[0])
        mid = outer + vals[1]
    if slps is not None:
        slope_bend = (4.0 * HALF_GAP) * (slps[2] - slps[0])
        slope_rise = (slps[0] + slps[2]) + slps[1]
        bend = slope_bend if bend is None else bend + slope_bend
        rise = slope_rise if rise is None else rise + slope_rise
    twice = -2.0 * bend
    return bend - rise, twice if mid is None else mid + twice, bend + rise


def at_point(c, k, jz, jy, jx):
    row = (((jz * 3 + jy) * 3 + jx) * 9 + k) * 8
    return pl.ds(pl.multiple_of(row + c * 24, 8), 8)


def forward(local, out_ref, at):
    along_z = [[spread(local(0, y, x), local(1, y, x), local(2, y, x)) for x in range(3)] for y in range(3)]
    for jz in range(3):
        value = [[along_z[y][x][0][jz] for x in range(3)] for y in range(3)]
        slope = [[along_z[y][x][1][jz] for x in range(3)] for y in range(3)]
        plain = [spread(value[0][x], value[1][x], value[2][x]) for x in range(3)]
        steep = [spread(slope[0][x], slope[1][x], slope[2][x], slopes=False)[0] for x in range(3)]
        for jy in range(3):
            dx = spread(*(plain[x][0][jy] for x in range(3)), values=False)[1]
            dy = spread(*(plain[x][1][jy] for x in range(3)), slopes=False)[0]
            dz = spread(*(steep[x][jy] for x in range(3)), slopes=False)[0]
            for jx in range(3):
                for k, part in enumerate((dx, dy, dz)):
                    out_ref[at(k, jz, jy, jx), :] = part[jx]


def backward(c, from_ref, out_ref):
    planes = []
    for jz in range(3):
        lines = []
        for jy in range(3):
            dx, dy, dz = (
                tuple(from_ref[at_point(c, k, jz, jy, jx), :] for jx in range(3)) for k in range(3)
            )
            lines.append((collect(None, dx), collect(dy, None), collect(dz, None)))
        value = [
            collect(tuple(lines[jy][0][x] for jy in range(3)), tuple(lines[jy][1][x] for jy in range(3)))
            for x in range(3)
        ]
        slope = [collect(tuple(lines[jy][2][x] for jy in range(3)), None) for x in range(3)]
        planes.append((value, slope))
    whole = [
        [
            collect(
                tuple(planes[jz][0][x][y] for jz in range(3)), tuple(planes[jz][1][x][y] for jz in range(3))
            )
            for x in range(3)
        ]
        for y in range(3)
    ]
    folded_x = [[(whole[y][0][z] + x_down(whole[y][2][z]), whole[y][1][z]) for z in range(3)] for y in range(3)]
    for x in range(2):
        folded = [(folded_x[0][z][x] + y_down(folded_x[2][z][x]), folded_x[1][z][x]) for z in range(3)]
        for y in range(2):
            for z, node in enumerate((folded[0][y] + z_down(folded[2][y]), folded[1][y])):
                row = (z * 4 + y * 2 + x) * 8
                out_ref[pl.ds(pl.multiple_of(row + c * 64, 8), 8), :] = node


def symmetric(build):
    upper = {(k, l): build(k, l) for k in range(3) for l in range(k, 3)}
    return {(k, l): upper[min(k, l), max(k, l)] for k in range(3) for l in range(3)}


def inner(a, b):
    square = (a[0, 0] * b[0, 0] + a[1, 1] * b[1, 1]) + a[2, 2] * b[2, 2]
    cross = (a[0, 1] * b[0, 1] + a[0, 2] * b[0, 2]) + a[1, 2] * b[1, 2]
    return square + 2.0 * cross


def column_dot(a, b, k, l):
    return (a[0][k] * b[0][l] + a[1][k] * b[1][l]) + a[2][k] * b[2][l]


def load_tensor(ref, jz, jy, jx):
    tensor = [[ref[at_point(c, k, jz, jy, jx), :] for k in range(3)] for c in range(3)]
    return tensor


def jacobian_at(ref, jz, jy, jx):
    tensor = load_tensor(ref, jz, jy, jx)
    return [[tensor[c][k] + 1.0 if c == k else tensor[c][k] for k in range(3)] for c in range(3)]


def strain_of(jac, size):
    return symmetric(lambda k, l: column_dot(jac, jac, k, l) * size - (1.0 if k == l else 0.0))


def weight_at(jz, jy, jx):
    along_z = jnp.where(jz == 1, MIDDLE, OUTER).astype(jnp.float32)
    return along_z * ((MIDDLE if jy == 1 else OUTER) * (MIDDLE if jx == 1 else OUTER))


def newton_step(totals):
    _, linear, quadratic, cubic, quartic, floor = (totals[:, i : i + 1] for i in range(6))
    step = jnp.zeros_like(linear)
    for _ in range(4):
        slope = linear + step * (2.0 * quadratic + step * (3.0 * cubic + step * 4.0 * quartic))
        curvature = 2.0 * quadratic + step * (6.0 * cubic + step * 12.0 * quartic)
        step = step - slope / jnp.maximum(curvature, floor + 1e-06)
    return step


def add_up(terms_ref):
    return jnp.sum(terms_ref[...], axis=0, keepdims=True)


def ring(pieces, count, out_ref, out_at, z_shift, y_shift):
    low = lax.broadcasted_iota(jnp.int32, (count, 128), 1) < 64
    places = ((-1, 1), (0, 0), (0, 1), (1, 0)) if y_shift else ((-1, 0), (-1, 1), (0, 0), (0, 1))
    for upper in range(2):
        for y, (piece_y, row) in enumerate(places):

            def piece(z):
                ref, at = pieces[z, piece_y]
                return ref[pl.ds(at + row, count, stride=2), :]

            value = piece(-upper)
            if z_shift:
                value = jnp.where(low, pltpu.roll(value, 64, 1), pltpu.roll(piece(1 - upper), 64, 1))
            out_ref[pl.ds(out_at + upper * 4 + y, count, stride=8), :] = value


def pass_kernel(first, *refs):
    refs = list(refs)
    field_refs = [refs.pop(0) for _ in range(3)]
    if not first:
        shift_refs = [refs.pop(0) for _ in range(3)]
    sizes = {at: (ref, 0) for at, ref in size_pieces([refs.pop(0) for _ in range(4)]).items()}
    if first:
        move_ref, terms_out, nodes_ref, size_ref, jac_ref, part_ref, turn_ref = refs
        field = field_pieces(field_refs)
    else:
        terms_in, move_ref, terms_out, own_ref, nodes_ref, size_ref, jac_ref, part_ref, turn_ref, sum_ref = refs
        step = newton_step(add_up(terms_in))
        for i, (field_ref, shift_ref) in enumerate(zip(field_refs, shift_refs)):
            sum_ref[i] = field_ref[...] + step * shift_ref[...]
        field = field_pieces([sum_ref.at[i] for i in range(3)])
        own_ref[...] = sum_ref[0, :48, :]
    for z_shift in range(2):
        for y_shift in range(2):
            ring(field, 24, nodes_ref, (z_shift * 2 + y_shift) * 192, z_shift, y_shift)
    ring(sizes, 27, size_ref, 0, 0, 0)

    def known(c):
        def local(z, y, x):
            row = ((z == 2) * 2 + (y == 2)) * 192 + ((z % 2) * 4 + (y % 2) * 2 + x % 2) * 8
            value = nodes_ref[pl.ds(pl.multiple_of(row + c * 64, 8), 8), :]
            return x_up(value) if x == 2 else value

        return local

    def packed(node, upper, shift):
        rows = [
            turn_ref[pl.ds(node * 8 + upper * 4 + 1 + shift + ey, 4, stride=64), :] for ey in range(2)
        ]
        return jnp.concatenate(rows, axis=0)

    def sought(z, y, x):
        node = (z % 2) * 4 + (y % 2) * 2 + x % 2
        shift = y // 2
        value = packed(node, 0, shift)
        if z == 2:
            value = pltpu.roll(value, 64, 1)
        else:
            value = jnp.where(lane_index() < 64, value, packed(node, 1, shift))
        return x_up(value) if x == 2 else value

    def each(body):
        def run(i, carry):
            body(i)
            return carry

        lax.fori_loop(0, 3, run, 0)

    def size_at(jz, jy, jx):
        return size_ref[pl.ds(pl.multiple_of((jz * 9 + jy * 3 + jx) * 8, 8), 8), :]

    each(lambda c: forward(known(c), jac_ref, functools.partial(at_point, c)))
    turn_ref[192:, :] = jnp.zeros((64, 128), jnp.float32)

    def stress(jz):
        for jy in range(3):
            for jx in range(3):
                jac = jacobian_at(jac_ref, jz, jy, jx)
                size = size_at(jz, jy, jx)
                strain = strain_of(jac, size)
                scale = size * (-4.0 * weight_at(jz, jy, jx))
                for c in range(3):
                    for k in range(3):
                        part = (strain[k, 0] * jac[c][0] + strain[k, 1] * jac[c][1]) + strain[k, 2] * jac[c][2]
                        part_ref[at_point(c, k, jz, jy, jx), :] = part * scale

    each(stress)
    each(lambda c: backward(c, part_ref, turn_ref))
    for row in range(2):
        move_ref[pl.ds(row, 24, stride=2), :] = turn_ref[pl.ds(row + 2, 24, stride=8), :]
    forward(sought, part_ref, lambda k, jz, jy, jx: pl.ds(((jz * 9 + jy * 3 + jx) * 3 + k) * 8, 8))

    def middle(ref, at, stride):
        return jnp.where(lane_index() < 64, ref[pl.ds(at, 8, stride=stride), :], ref[pl.ds(at + 4, 8, stride=stride), :])

    sub = lax.broadcasted_iota(jnp.int32, (8, 128), 0)
    sums = [jnp.zeros((8, 128), jnp.float32) for _ in range(6)]
    for start, fresh in ((0, 0), (8, 8), (16, 16), (19, 24)):
        weight = jnp.zeros((8, 128), jnp.float32)
        for i in range(fresh - start, 8):
            point = start + i
            parts = [MIDDLE if (point // by) % 3 == 1 else OUTER for by in (9, 3, 1)]
            weight = jnp.where(sub == i, (parts[0] * parts[1]) * parts[2], weight)
        for ey in range(2):
            jac = [
                [middle(jac_ref, (start * 9 + c * 3 + k) * 8 + 1 + ey, 72) for k in range(3)]
                for c in range(3)
            ]
            jac = [[jac[c][k] + 1.0 if c == k else jac[c][k] for k in range(3)] for c in range(3)]
            motion = [
                [part_ref[pl.ds((start * 3 + k) * 8 + ey * 4 + c, 8, stride=24), :] for k in range(3)]
                for c in range(3)
            ]
            size = middle(size_ref, start * 8 + 1 + ey, 8)
            zero = strain_of(jac, size)
            one = symmetric(lambda k, l: (column_dot(jac, motion, k, l) + column_dot(motion, jac, k, l)) * size)
            two = symmetric(lambda k, l: column_dot(motion, motion, k, l) * size)
            pairs = ((zero, zero), (zero, one), (zero, two), (one, two), (two, two), (one, one))
            sums = [total + weight * inner(*pair) for total, pair in zip(sums, pairs)]
    zz, zo, zt, ot, tt, gn = (jnp.sum(total, keepdims=True) for total in sums)
    lane = lax.broadcasted_iota(jnp.int32, (1, 128), 1)
    terms = jnp.zeros((1, 128), jnp.float32)
    for i, term in enumerate((zz, 2.0 * zo, gn + 2.0 * zt, 2.0 * ot, tt, gn)):
        terms = jnp.where(lane == i, term, terms)
    terms_out[...] = jnp.broadcast_to(terms, (SRC, 128))


def newton_pass(field, shift, sizes, terms):
    first = shift is None
    node = jax.ShapeDtypeStruct((48, 128), jnp.float32)
    outs = [node, jax.ShapeDtypeStruct((SRC, 128), jnp.float32)] + ([] if first else [node])
    scratch = [
        pltpu.VMEM((4 * 192, 128), jnp.float32),
        pltpu.VMEM((27 * 8, 128), jnp.float32),
        pltpu.VMEM((243 * 8, 128), jnp.float32),
        pltpu.VMEM((243 * 8, 128), jnp.float32),
        pltpu.VMEM((32 * 8, 128), jnp.float32),
    ] + ([] if first else [pltpu.VMEM((3, 144, 128), jnp.float32)])
    args = list(field) + ([] if first else list(shift)) + list(sizes) + ([] if first else [terms])
    return call(functools.partial(pass_kernel, first), outs, args, scratch)


def interleave(back):
    row = lax.broadcasted_iota(jnp.int32, (128, 128), 0)
    col = lax.broadcasted_iota(jnp.int32, (128, 128), 1)
    if back:
        row, col = col, row
    return (col == (row & 1) * 64 + (row >> 1)).astype(jnp.float32)


def split_kernel(nodes_ref, out_ref, rows_ref):
    rows = nodes_ref[...].reshape(48, 128)
    rows_ref[...] = jnp.dot(rows, interleave(False), precision=lax.Precision.HIGHEST, preferred_element_type=jnp.float32)
    low = lax.broadcasted_iota(jnp.int32, (1, 128), 1) < 64
    for c in range(3):
        for az in range(2):
            for ay in range(2):
                for ey in range(2):
                    at = c * 16 + az * 4 + ey * 2 + ay
                    first = rows_ref[at : at + 1, :]
                    second = rows_ref[at + 8 : at + 9, :]
                    to = (c * 8 + az * 4 + ay * 2) * 2 + ey
                    out_ref[to : to + 1, :] = jnp.where(low, first, pltpu.roll(second, 64, 1))
                    out_ref[to + 2 : to + 3, :] = jnp.where(low, pltpu.roll(first, 64, 1), second)


def split_nodes(nodes):
    out = jax.ShapeDtypeStruct((48, 128), jnp.float32)
    return call(split_kernel, out, [nodes], [pltpu.VMEM((48, 128), jnp.float32)], far=(0,))


def join_kernel(first_ref, second_ref, out_first_ref, out_second_ref, rows_ref):
    low = lax.broadcasted_iota(jnp.int32, (1, 128), 1) < 64
    for i, new_ref in enumerate((first_ref, second_ref)):
        for c in range(3):
            for az in range(2):
                for ay in range(2):
                    for ey in range(2):
                        at = (c * 8 + az * 4 + ay * 2) * 2 + ey
                        even = new_ref[at : at + 1, :]
                        odd = new_ref[at + 2 : at + 3, :]
                        to = i * 48 + c * 16 + az * 4 + ey * 2 + ay
                        rows_ref[to : to + 1, :] = jnp.where(low, even, pltpu.roll(odd, 64, 1))
                        rows_ref[to + 8 : to + 9, :] = jnp.where(low, pltpu.roll(even, 64, 1), odd)
    rows = jnp.dot(
        rows_ref[...], interleave(True), precision=lax.Precision.HIGHEST, preferred_element_type=jnp.float32
    )
    out_first_ref[...] = rows[:48].reshape(3, 4, 4, 128)
    out_second_ref[...] = rows[48:].reshape(3, 4, 4, 128)


def join_nodes(first, second):
    out = jax.ShapeDtypeStruct((3, 4, 4, 128), jnp.float32)
    return call(join_kernel, [out, out], [first, second], [pltpu.VMEM((96, 128), jnp.float32)])


def finish_kernel(own_ref, move_ref, first_ref, second_ref, out_ref, coeff_ref):
    second = add_up(second_ref)
    step = newton_step(second)
    for c in range(3):
        for z in range(4):
            out_ref[c, z] = own_ref[c, z] + step * move_ref[c, z]
    coeff_ref[0:1, :] = add_up(first_ref)[:, :5] * (1.0 / 32768.0)
    coeff_ref[1:2, :] = second[:, :5] * (1.0 / 32768.0)


def finish(own, move, first, second):
    outs = [jax.ShapeDtypeStruct((3, 4, 4, 128), jnp.float32), jax.ShapeDtypeStruct((2, 5), jnp.float32)]
    return call(finish_kernel, outs, [own, move, first, second], [], last=True)


def pack_kernel(elem_ref, coord_ref, out_ref):
    parts = [elem_ref[...].astype(jnp.float32)] + [coord_ref[j] for j in range(3)]
    for j, part in enumerate(parts):
        out_ref[:, 0, j * 128 : j * 128 + 128] = part[:128].T
    tails = jnp.concatenate([part[128:] for part in parts] + [jnp.zeros((96, 128), jnp.float32)], axis=0)
    out_ref[:, 0, 512:] = tails.T


def pack(elem, coord):
    return call(pack_kernel, jax.ShapeDtypeStruct((SRC, 1, 640), jnp.float32), [elem, coord], [], far=(0, 1))


def exchange(values):
    return lax.all_to_all(values, ("mesh", "bg"), split_axis=0, concat_axis=0, tiled=True)


def moved(values, axis, by):
    count = lax.axis_size(axis)
    return lax.ppermute(values, axis, [(i, (i - by) % count) for i in range(count)])


def along_mesh(block):
    return jnp.concatenate([block, moved(block, "mesh", 1), moved(block, "mesh", -1)], axis=0)


def from_below(block):
    mesh, bg = lax.axis_size("mesh"), lax.axis_size("bg")
    steps = [
        (z * bg + y, ((z + 1) % mesh) * bg + (y + 1) % bg) for z in range(mesh) for y in range(bg)
    ]
    return [block, moved(block, "mesh", -1), moved(block, "bg", -1), lax.ppermute(block, ("mesh", "bg"), steps)]


def along_bg(rows):
    return [rows, moved(rows, "bg", 1), moved(rows, "bg", -1)]


def shards(displacement, bg_coef, query_elem, query_point, query_coord):
    asked = exchange(pack(query_elem[0].T, query_coord[0].transpose(1, 2, 0)))
    own = split_nodes(displacement)
    rows = along_mesh(own)
    asked, prepared, rows = lax.optimization_barrier((asked, prepare(bg_coef), rows))
    found, rows = lax.optimization_barrier((lookup(asked, prepared), rows))
    found = exchange(found)
    field = along_bg(rows)
    found, field = lax.optimization_barrier((found, field))
    sizes = from_below(place(found, query_point[0].T))
    move, terms = newton_pass(field, None, sizes, None)
    first_terms = exchange(terms)
    shift = along_bg(along_mesh(move))
    last_move, last_terms, last_own = newton_pass(field, shift, sizes, first_terms)
    own, move = join_nodes(last_own, last_move)
    last_terms = exchange(last_terms)
    return finish(own, move, first_terms, last_terms)


def solution(mesh):
    in_specs = (
        P(None, "mesh", "bg", None),
        P(None, ("mesh", "bg")),
        P(("mesh", "bg"), None, None),
        P(("mesh", "bg"), None, None),
        P(("mesh", "bg"), None, None, None),
    )
    out_specs = (P(None, "mesh", "bg", None), P())
    return jax.shard_map(shards, mesh=mesh, in_specs=in_specs, out_specs=out_specs, check_vma=False)
```

```python
import functools

import jax
import jax.numpy as jnp
import numpy as np
from jax import lax
from jax.experimental import pallas as pl
from jax.experimental.pallas import tpu as pltpu
from jax.sharding import PartitionSpec as P

SRC = 128
SLOTS = 136
TABLE = 16384
COLS = 256


GATHER_ROWS = 64
ROUNDS = 8


def in_vmem(count):
    return [pl.BlockSpec(memory_space=pltpu.VMEM) for _ in range(count)]


def call(kernel, outs, args, scratch, far=(), last=False):
    args = [a if i in far else pltpu.with_memory_space_constraint(a, pltpu.VMEM) for i, a in enumerate(args)]
    many = isinstance(outs, list)
    if not last:
        outs = [pltpu.VMEM(o.shape, o.dtype) for o in outs] if many else pltpu.VMEM(outs.shape, outs.dtype)
    return pl.pallas_call(
        kernel,
        out_shape=outs,
        in_specs=in_vmem(len(args)),
        out_specs=in_vmem(len(outs)) if many else in_vmem(1)[0],
        scratch_shapes=scratch,
    )(*args)


def prepare_kernel(table_ref, split_ref, packed_ref, unit_ref):
    top = jnp.zeros((8, 128), jnp.float32)
    for block in range(TABLE // 128):
        top = jnp.maximum(top, jnp.abs(table_ref[:, block * 128 : block * 128 + 128]))
    top = jnp.maximum(jnp.max(top, keepdims=True), 1e-30)
    unit_ref[...] = jnp.broadcast_to(top * (1.0 / 32767.0), (8, 128))
    scale = 32767.0 / top

    def whole(values):
        return (values * scale + 32768.5).astype(jnp.int32) - 32768

    for block in range(TABLE // 256):
        low = table_ref[:, block * 128 : block * 128 + 128]
        high = table_ref[:, TABLE // 2 + block * 128 : TABLE // 2 + block * 128 + 128]
        packed_ref[:, block * 128 : block * 128 + 128] = (whole(high) << 16) | (whole(low) & 65535)
    for pair in range(TABLE // (2 * COLS)):
        start = pair * 2 * COLS
        rows = jnp.concatenate(
            [table_ref[:, start : start + COLS], table_ref[:, start + COLS : start + 2 * COLS]], axis=0
        )
        upper = rows.astype(jnp.bfloat16)
        split_ref[pair * 16 : pair * 16 + 16, :COLS] = upper
        split_ref[pair * 16 : pair * 16 + 16, COLS:] = (rows - upper.astype(jnp.float32)).astype(jnp.bfloat16)


def prepare(table):
    outs = [
        jax.ShapeDtypeStruct((8 * TABLE // COLS, 2 * COLS), jnp.bfloat16),
        jax.ShapeDtypeStruct((8, TABLE // 2), jnp.int32),
        jax.ShapeDtypeStruct((8, 128), jnp.float32),
    ]
    return call(prepare_kernel, outs, [table], [], far=(0,))


def choose(leaf, masks, first, count):
    if count == 1:
        return leaf(first)
    half = count // 2
    mask = masks[half.bit_length() - 1]
    return jnp.where(mask, choose(leaf, masks, first + half, half), choose(leaf, masks, first, half))


def weigh(coef, x, y, z):
    corner = lax.broadcasted_iota(jnp.int32, coef.shape, 0)
    weight_x = jnp.where((corner & 1) == 1, x, 1.0 - x)
    weight_y = jnp.where((corner & 2) == 2, y, 1.0 - y)
    weight_z = jnp.where((corner & 4) == 4, z, 1.0 - z)
    lsize = jnp.sum(weight_x * weight_y * weight_z * coef, axis=0, keepdims=True)
    return jnp.exp(-2.0 * lsize)


def lookup_kernel(asked_ref, split_ref, packed_ref, unit_ref, found_ref, turned_ref, result_ref, column_ref):
    for j in range(4):
        turned_ref[j * SLOTS : j * SLOTS + 128, :] = asked_ref[:, 0, j * 128 : j * 128 + 128].T
    tails = asked_ref[:, 0, 512:].T
    for j in range(4):
        turned_ref[j * SLOTS + 128 : (j + 1) * SLOTS, :] = tails[j * 8 : j * 8 + 8]
    column_ref[...] = lax.broadcasted_iota(jnp.int32, (COLS, 128), 0).astype(jnp.float32).astype(jnp.bfloat16)
    one = jnp.ones((), jnp.bfloat16)
    zero = jnp.zeros((), jnp.bfloat16)

    def step(i, carry):
        base = pl.multiple_of(i * 8, 8)
        ids, xs, ys, zs = (turned_ref[pl.ds(pl.multiple_of(j * SLOTS + base, 8), 8), :] for j in range(4))
        ids = ids.astype(jnp.int32)
        unit = unit_ref[...]
        for r in range(8):
            own = jnp.broadcast_to(ids[r : r + 1], (8, 128))
            lane = own & 127
            masks = [(own & (128 << bit)) != 0 for bit in range(6)]

            def leaf(block):
                return jnp.take_along_axis(packed_ref[:, block * 128 : block * 128 + 128], lane, axis=1)

            word = choose(leaf, masks, 0, 64)
            whole = jnp.where((own & (TABLE // 2)) != 0, word, word << 16) >> 16
            coef = whole.astype(jnp.float32) * unit
            result_ref[pl.ds(base + r, 1), :] = weigh(coef, xs[r : r + 1], ys[r : r + 1], zs[r : r + 1])

        start = GATHER_ROWS + i * 9
        for pair in range(5):
            at = start + 2 * pair
            wide = 2 if pair < 4 else 1
            pair_ids, px, py, pz = (
                jnp.concatenate([turned_ref[pl.ds(j * SLOTS + at + k, 1), :] for k in range(wide)], axis=1)
                for j in range(4)
            )
            pair_ids = pair_ids.astype(jnp.int32)
            column = (pair_ids & (COLS - 1)).astype(jnp.float32).astype(jnp.bfloat16)
            chosen = jnp.concatenate(
                [
                    jnp.where(column_ref[...] == column[:, half * 128 : half * 128 + 128], one, zero)
                    for half in range(wide)
                ],
                axis=1,
            )
            picked = jnp.dot(split_ref[:, :COLS], chosen, preferred_element_type=jnp.float32) + jnp.dot(
                split_ref[:, COLS:], chosen, preferred_element_type=jnp.float32
            )
            own = jnp.broadcast_to(pair_ids, (8, 128 * wide))
            masks = [(own & (COLS << bit)) != 0 for bit in range(6)]
            coef = choose(lambda row: picked[row * 8 : row * 8 + 8], masks, 0, 64)
            value = weigh(coef, px, py, pz)
            for k in range(wide):
                result_ref[pl.ds(at + k, 1), :] = value[:, k * 128 : k * 128 + 128]
        return carry

    lax.fori_loop(0, ROUNDS, step, 0)
    found_ref[:, 0, :128] = result_ref[:128, :].T
    found_ref[:, 0, 128:] = result_ref[128:, :].T


def lookup(asked, prepared):
    scratch = [
        pltpu.VMEM((4 * SLOTS, 128), jnp.float32),
        pltpu.VMEM((SLOTS, 128), jnp.float32),
        pltpu.VMEM((COLS, 128), jnp.bfloat16),
    ]
    out = jax.ShapeDtypeStruct((SRC, 1, SLOTS), jnp.float32)
    return call(lookup_kernel, out, [asked, *prepared], scratch)


def place_kernel(found_ref, point_ref, size_ref, value_ref, row_ref, lane_ref, at_ref):
    value_ref[:128, :] = found_ref[:, 0, :128].T
    value_ref[128:, :] = found_ref[:, 0, 128:].T
    point = point_ref[...]
    line = (point * 10923) >> 21
    qx = point - line * 192
    qz = (line * 43) >> 8
    qy = line - qz * 6
    ex = (qx * 171) >> 9
    jx = qx - ex * 3
    ey = (qy * 11) >> 5
    jy = qy - ey * 3
    ez = (qz * 11) >> 5
    jz = qz - ez * 3
    row_ref[...] = (((jz * 3 + jy) * 3 + jx) * 2 + ey).astype(jnp.float32)
    lane_ref[...] = (ez * 64 + ex).astype(jnp.float32)
    at_ref[...] = lax.broadcasted_iota(jnp.int32, (128, 128), 0).astype(jnp.float32).astype(jnp.bfloat16)
    one = jnp.ones((), jnp.bfloat16)
    zero = jnp.zeros((), jnp.bfloat16)

    def step(i, total):
        values = value_ref[i * 8 : i * 8 + 8, :]
        rows = row_ref[i * 8 : i * 8 + 8, :]
        lanes = lane_ref[i * 8 : i * 8 + 8, :]
        left, right = [], []
        for r in range(8):
            value = values[r : r + 1]
            upper = value.astype(jnp.bfloat16)
            lower = (value - upper.astype(jnp.float32)).astype(jnp.bfloat16)
            row = at_ref[:64, :] == rows[r : r + 1].astype(jnp.bfloat16)
            left.append(jnp.concatenate([jnp.where(row, upper, zero), jnp.where(row, lower, zero)], axis=0))
            right.append(jnp.where(at_ref[...] == lanes[r : r + 1].astype(jnp.bfloat16), one, zero))
        left = jnp.concatenate(left, axis=1)
        right = jnp.concatenate(right, axis=1)
        return total + lax.dot_general(left, right, (((1,), (1,)), ((), ())), preferred_element_type=jnp.float32)

    total = jnp.zeros((128, 128), jnp.float32)
    for i in range(SLOTS // 8):
        total = step(i, total)
    size_ref[...] = total[:56] + total[64:120]


def place(found, point):
    scratch = [pltpu.VMEM((SLOTS, 128), jnp.float32) for _ in range(3)] + [pltpu.VMEM((128, 128), jnp.bfloat16)]
    return call(place_kernel, jax.ShapeDtypeStruct((56, 128), jnp.float32), [found, point], scratch, far=(1,))


HALF_GAP = float(np.sqrt(0.15))
OUTER, MIDDLE = 5.0 / 18.0, 8.0 / 18.0


def field_pieces(refs):
    return {(z, y): (refs[y], (z % 3) * 48) for z in (-1, 0, 1) for y in (-1, 0, 1)}


def size_pieces(refs):
    own, z_low, y_low, corner = refs
    return {(0, 0): own, (-1, 0): z_low, (0, -1): y_low, (-1, -1): corner}


def lane_index():
    return lax.broadcasted_iota(jnp.int32, (8, 128), 1)


def x_up(v):
    return jnp.where((lane_index() & 63) == 63, pltpu.roll(v, 63, 1), pltpu.roll(v, 127, 1))


def x_down(v):
    return jnp.where((lane_index() & 63) == 0, pltpu.roll(v, 65, 1), pltpu.roll(v, 1, 1))


def z_down(v):
    turned = pltpu.roll(v, 64, 1)
    return jnp.where(lane_index() < 64, pltpu.roll(turned, 4, 0), turned)


def y_down(v):
    return pltpu.roll(v, 1, 0)


def spread(low, mid, high, slopes=True, values=True):
    bend = (low + high) - 2.0 * mid
    rise = high - low
    vals = slps = None
    if values:
        centre = mid + (2.0 * HALF_GAP * HALF_GAP) * bend
        lean = HALF_GAP * rise
        vals = (centre - lean, mid, centre + lean)
    if slopes:
        change = (4.0 * HALF_GAP) * bend
        slps = (rise - change, rise, rise + change)
    return vals, slps


def collect(vals, slps):
    bend = rise = mid = None
    if vals is not None:
        outer = vals[0] + vals[2]
        bend = (2.0 * HALF_GAP * HALF_GAP) * outer
        rise = HALF_GAP * (vals[2] - vals[0])
        mid = outer + vals[1]
    if slps is not None:
        slope_bend = (4.0 * HALF_GAP) * (slps[2] - slps[0])
        slope_rise = (slps[0] + slps[2]) + slps[1]
        bend = slope_bend if bend is None else bend + slope_bend
        rise = slope_rise if rise is None else rise + slope_rise
    twice = -2.0 * bend
    return bend - rise, twice if mid is None else mid + twice, bend + rise


def at_point(c, k, jz, jy, jx):
    row = (((jz * 3 + jy) * 3 + jx) * 9 + k) * 8
    return pl.ds(pl.multiple_of(row + c * 24, 8), 8)


def forward(local, out_ref, at):
    along_z = [[spread(local(0, y, x), local(1, y, x), local(2, y, x)) for x in range(3)] for y in range(3)]
    for jz in range(3):
        value = [[along_z[y][x][0][jz] for x in range(3)] for y in range(3)]
        slope = [[along_z[y][x][1][jz] for x in range(3)] for y in range(3)]
        plain = [spread(value[0][x], value[1][x], value[2][x]) for x in range(3)]
        steep = [spread(slope[0][x], slope[1][x], slope[2][x], slopes=False)[0] for x in range(3)]
        for jy in range(3):
            dx = spread(*(plain[x][0][jy] for x in range(3)), values=False)[1]
            dy = spread(*(plain[x][1][jy] for x in range(3)), slopes=False)[0]
            dz = spread(*(steep[x][jy] for x in range(3)), slopes=False)[0]
            for jx in range(3):
                for k, part in enumerate((dx, dy, dz)):
                    out_ref[at(k, jz, jy, jx), :] = part[jx]


def backward(c, from_ref, out_ref):
    planes = []
    for jz in range(3):
        lines = []
        for jy in range(3):
            dx, dy, dz = (
                tuple(from_ref[at_point(c, k, jz, jy, jx), :] for jx in range(3)) for k in range(3)
            )
            lines.append((collect(None, dx), collect(dy, None), collect(dz, None)))
        value = [
            collect(tuple(lines[jy][0][x] for jy in range(3)), tuple(lines[jy][1][x] for jy in range(3)))
            for x in range(3)
        ]
        slope = [collect(tuple(lines[jy][2][x] for jy in range(3)), None) for x in range(3)]
        planes.append((value, slope))
    whole = [
        [
            collect(
                tuple(planes[jz][0][x][y] for jz in range(3)), tuple(planes[jz][1][x][y] for jz in range(3))
            )
            for x in range(3)
        ]
        for y in range(3)
    ]
    folded_x = [[(whole[y][0][z] + x_down(whole[y][2][z]), whole[y][1][z]) for z in range(3)] for y in range(3)]
    for x in range(2):
        folded = [(folded_x[0][z][x] + y_down(folded_x[2][z][x]), folded_x[1][z][x]) for z in range(3)]
        for y in range(2):
            for z, node in enumerate((folded[0][y] + z_down(folded[2][y]), folded[1][y])):
                row = (z * 4 + y * 2 + x) * 8
                out_ref[pl.ds(pl.multiple_of(row + c * 64, 8), 8), :] = node


def symmetric(build):
    upper = {(k, l): build(k, l) for k in range(3) for l in range(k, 3)}
    return {(k, l): upper[min(k, l), max(k, l)] for k in range(3) for l in range(3)}


def inner(a, b):
    square = (a[0, 0] * b[0, 0] + a[1, 1] * b[1, 1]) + a[2, 2] * b[2, 2]
    cross = (a[0, 1] * b[0, 1] + a[0, 2] * b[0, 2]) + a[1, 2] * b[1, 2]
    return square + 2.0 * cross


def column_dot(a, b, k, l):
    return (a[0][k] * b[0][l] + a[1][k] * b[1][l]) + a[2][k] * b[2][l]


def load_tensor(ref, jz, jy, jx):
    tensor = [[ref[at_point(c, k, jz, jy, jx), :] for k in range(3)] for c in range(3)]
    return tensor


def jacobian_at(ref, jz, jy, jx):
    tensor = load_tensor(ref, jz, jy, jx)
    return [[tensor[c][k] + 1.0 if c == k else tensor[c][k] for k in range(3)] for c in range(3)]


def strain_of(jac, size):
    return symmetric(lambda k, l: column_dot(jac, jac, k, l) * size - (1.0 if k == l else 0.0))


def weight_at(jz, jy, jx):
    along_z = jnp.where(jz == 1, MIDDLE, OUTER).astype(jnp.float32)
    return along_z * ((MIDDLE if jy == 1 else OUTER) * (MIDDLE if jx == 1 else OUTER))


def newton_step(totals):
    _, linear, quadratic, cubic, quartic, floor = (totals[:, i : i + 1] for i in range(6))
    step = jnp.zeros_like(linear)
    for _ in range(4):
        slope = linear + step * (2.0 * quadratic + step * (3.0 * cubic + step * 4.0 * quartic))
        curvature = 2.0 * quadratic + step * (6.0 * cubic + step * 12.0 * quartic)
        step = step - slope / jnp.maximum(curvature, floor + 1e-06)
    return step


def add_up(terms_ref):
    return jnp.sum(terms_ref[...], axis=0, keepdims=True)


def ring(pieces, count, out_ref, out_at, z_shift, y_shift):
    low = lax.broadcasted_iota(jnp.int32, (count, 128), 1) < 64
    places = ((-1, 1), (0, 0), (0, 1), (1, 0)) if y_shift else ((-1, 0), (-1, 1), (0, 0), (0, 1))
    for upper in range(2):
        for y, (piece_y, row) in enumerate(places):

            def piece(z):
                ref, at = pieces[z, piece_y]
                return ref[pl.ds(at + row, count, stride=2), :]

            value = piece(-upper)
            if z_shift:
                value = jnp.where(low, pltpu.roll(value, 64, 1), pltpu.roll(piece(1 - upper), 64, 1))
            out_ref[pl.ds(out_at + upper * 4 + y, count, stride=8), :] = value


def pass_kernel(first, *refs):
    refs = list(refs)
    field_refs = [refs.pop(0) for _ in range(3)]
    if not first:
        shift_refs = [refs.pop(0) for _ in range(3)]
    sizes = {at: (ref, 0) for at, ref in size_pieces([refs.pop(0) for _ in range(4)]).items()}
    if first:
        move_ref, terms_out, nodes_ref, size_ref, jac_ref, part_ref, turn_ref = refs
        field = field_pieces(field_refs)
    else:
        terms_in, move_ref, terms_out, own_ref, nodes_ref, size_ref, jac_ref, part_ref, turn_ref, sum_ref = refs
        step = newton_step(add_up(terms_in))
        for i, (field_ref, shift_ref) in enumerate(zip(field_refs, shift_refs)):
            sum_ref[i] = field_ref[...] + step * shift_ref[...]
        field = field_pieces([sum_ref.at[i] for i in range(3)])
        own_ref[...] = sum_ref[0, :48, :]
    for z_shift in range(2):
        for y_shift in range(2):
            ring(field, 24, nodes_ref, (z_shift * 2 + y_shift) * 192, z_shift, y_shift)
    ring(sizes, 27, size_ref, 0, 0, 0)

    def known(c):
        def local(z, y, x):
            row = ((z == 2) * 2 + (y == 2)) * 192 + ((z % 2) * 4 + (y % 2) * 2 + x % 2) * 8
            value = nodes_ref[pl.ds(pl.multiple_of(row + c * 64, 8), 8), :]
            return x_up(value) if x == 2 else value

        return local

    def packed(node, upper, shift):
        rows = [
            turn_ref[pl.ds(node * 8 + upper * 4 + 1 + shift + ey, 4, stride=64), :] for ey in range(2)
        ]
        return jnp.concatenate(rows, axis=0)

    def sought(z, y, x):
        node = (z % 2) * 4 + (y % 2) * 2 + x % 2
        shift = y // 2
        value = packed(node, 0, shift)
        if z == 2:
            value = pltpu.roll(value, 64, 1)
        else:
            value = jnp.where(lane_index() < 64, value, packed(node, 1, shift))
        return x_up(value) if x == 2 else value

    def each(body):
        def run(i, carry):
            body(i)
            return carry

        lax.fori_loop(0, 3, run, 0)

    def size_at(jz, jy, jx):
        return size_ref[pl.ds(pl.multiple_of((jz * 9 + jy * 3 + jx) * 8, 8), 8), :]

    each(lambda c: forward(known(c), jac_ref, functools.partial(at_point, c)))
    turn_ref[192:, :] = jnp.zeros((64, 128), jnp.float32)

    def stress(jz):
        for jy in range(3):
            for jx in range(3):
                jac = jacobian_at(jac_ref, jz, jy, jx)
                size = size_at(jz, jy, jx)
                strain = strain_of(jac, size)
                scale = size * (-4.0 * weight_at(jz, jy, jx))
                for c in range(3):
                    for k in range(3):
                        part = (strain[k, 0] * jac[c][0] + strain[k, 1] * jac[c][1]) + strain[k, 2] * jac[c][2]
                        part_ref[at_point(c, k, jz, jy, jx), :] = part * scale

    each(stress)
    each(lambda c: backward(c, part_ref, turn_ref))
    for row in range(2):
        move_ref[pl.ds(row, 24, stride=2), :] = turn_ref[pl.ds(row + 2, 24, stride=8), :]
    forward(sought, part_ref, lambda k, jz, jy, jx: pl.ds(((jz * 9 + jy * 3 + jx) * 3 + k) * 8, 8))

    def middle(ref, at, stride):
        return jnp.where(lane_index() < 64, ref[pl.ds(at, 8, stride=stride), :], ref[pl.ds(at + 4, 8, stride=stride), :])

    sub = lax.broadcasted_iota(jnp.int32, (8, 128), 0)
    sums = [jnp.zeros((8, 128), jnp.float32) for _ in range(6)]
    for start, fresh in ((0, 0), (8, 8), (16, 16), (19, 24)):
        weight = jnp.zeros((8, 128), jnp.float32)
        for i in range(fresh - start, 8):
            point = start + i
            parts = [MIDDLE if (point // by) % 3 == 1 else OUTER for by in (9, 3, 1)]
            weight = jnp.where(sub == i, (parts[0] * parts[1]) * parts[2], weight)
        for ey in range(2):
            jac = [
                [middle(jac_ref, (start * 9 + c * 3 + k) * 8 + 1 + ey, 72) for k in range(3)]
                for c in range(3)
            ]
            jac = [[jac[c][k] + 1.0 if c == k else jac[c][k] for k in range(3)] for c in range(3)]
            motion = [
                [part_ref[pl.ds((start * 3 + k) * 8 + ey * 4 + c, 8, stride=24), :] for k in range(3)]
                for c in range(3)
            ]
            size = middle(size_ref, start * 8 + 1 + ey, 8)
            zero = strain_of(jac, size)
            one = symmetric(lambda k, l: (column_dot(jac, motion, k, l) + column_dot(motion, jac, k, l)) * size)
            two = symmetric(lambda k, l: column_dot(motion, motion, k, l) * size)
            pairs = ((zero, zero), (zero, one), (zero, two), (one, two), (two, two), (one, one))
            sums = [total + weight * inner(*pair) for total, pair in zip(sums, pairs)]
    zz, zo, zt, ot, tt, gn = (jnp.sum(total, keepdims=True) for total in sums)
    lane = lax.broadcasted_iota(jnp.int32, (1, 128), 1)
    terms = jnp.zeros((1, 128), jnp.float32)
    for i, term in enumerate((zz, 2.0 * zo, gn + 2.0 * zt, 2.0 * ot, tt, gn)):
        terms = jnp.where(lane == i, term, terms)
    terms_out[...] = jnp.broadcast_to(terms, (SRC, 128))


def newton_pass(field, shift, sizes, terms):
    first = shift is None
    node = jax.ShapeDtypeStruct((48, 128), jnp.float32)
    outs = [node, jax.ShapeDtypeStruct((SRC, 128), jnp.float32)] + ([] if first else [node])
    scratch = [
        pltpu.VMEM((4 * 192, 128), jnp.float32),
        pltpu.VMEM((27 * 8, 128), jnp.float32),
        pltpu.VMEM((243 * 8, 128), jnp.float32),
        pltpu.VMEM((243 * 8, 128), jnp.float32),
        pltpu.VMEM((32 * 8, 128), jnp.float32),
    ] + ([] if first else [pltpu.VMEM((3, 144, 128), jnp.float32)])
    args = list(field) + ([] if first else list(shift)) + list(sizes) + ([] if first else [terms])
    return call(functools.partial(pass_kernel, first), outs, args, scratch)


def interleave(back):
    row = lax.broadcasted_iota(jnp.int32, (128, 128), 0)
    col = lax.broadcasted_iota(jnp.int32, (128, 128), 1)
    if back:
        row, col = col, row
    return (col == (row & 1) * 64 + (row >> 1)).astype(jnp.float32)


def split_kernel(nodes_ref, out_ref, rows_ref):
    rows = nodes_ref[...].reshape(48, 128)
    rows_ref[...] = jnp.dot(rows, interleave(False), precision=lax.Precision.HIGHEST, preferred_element_type=jnp.float32)
    low = lax.broadcasted_iota(jnp.int32, (1, 128), 1) < 64
    for c in range(3):
        for az in range(2):
            for ay in range(2):
                for ey in range(2):
                    at = c * 16 + az * 4 + ey * 2 + ay
                    first = rows_ref[at : at + 1, :]
                    second = rows_ref[at + 8 : at + 9, :]
                    to = (c * 8 + az * 4 + ay * 2) * 2 + ey
                    out_ref[to : to + 1, :] = jnp.where(low, first, pltpu.roll(second, 64, 1))
                    out_ref[to + 2 : to + 3, :] = jnp.where(low, pltpu.roll(first, 64, 1), second)


def split_nodes(nodes):
    out = jax.ShapeDtypeStruct((48, 128), jnp.float32)
    return call(split_kernel, out, [nodes], [pltpu.VMEM((48, 128), jnp.float32)], far=(0,))


def join_kernel(first_ref, second_ref, out_first_ref, out_second_ref, rows_ref):
    low = lax.broadcasted_iota(jnp.int32, (1, 128), 1) < 64
    for i, new_ref in enumerate((first_ref, second_ref)):
        for c in range(3):
            for az in range(2):
                for ay in range(2):
                    for ey in range(2):
                        at = (c * 8 + az * 4 + ay * 2) * 2 + ey
                        even = new_ref[at : at + 1, :]
                        odd = new_ref[at + 2 : at + 3, :]
                        to = i * 48 + c * 16 + az * 4 + ey * 2 + ay
                        rows_ref[to : to + 1, :] = jnp.where(low, even, pltpu.roll(odd, 64, 1))
                        rows_ref[to + 8 : to + 9, :] = jnp.where(low, pltpu.roll(even, 64, 1), odd)
    rows = jnp.dot(
        rows_ref[...], interleave(True), precision=lax.Precision.HIGHEST, preferred_element_type=jnp.float32
    )
    out_first_ref[...] = rows[:48].reshape(3, 4, 4, 128)
    out_second_ref[...] = rows[48:].reshape(3, 4, 4, 128)


def join_nodes(first, second):
    out = jax.ShapeDtypeStruct((3, 4, 4, 128), jnp.float32)
    return call(join_kernel, [out, out], [first, second], [pltpu.VMEM((96, 128), jnp.float32)])


def finish_kernel(own_ref, move_ref, first_ref, second_ref, out_ref, coeff_ref):
    second = add_up(second_ref)
    step = newton_step(second)
    for c in range(3):
        for z in range(4):
            out_ref[c, z] = own_ref[c, z] + step * move_ref[c, z]
    coeff_ref[0:1, :] = add_up(first_ref)[:, :5] * (1.0 / 32768.0)
    coeff_ref[1:2, :] = second[:, :5] * (1.0 / 32768.0)


def finish(own, move, first, second):
    outs = [jax.ShapeDtypeStruct((3, 4, 4, 128), jnp.float32), jax.ShapeDtypeStruct((2, 5), jnp.float32)]
    return call(finish_kernel, outs, [own, move, first, second], [], last=True)


def pack_kernel(elem_ref, coord_ref, out_ref):
    parts = [elem_ref[...].astype(jnp.float32)] + [coord_ref[j] for j in range(3)]
    for j, part in enumerate(parts):
        out_ref[:, 0, j * 128 : j * 128 + 128] = part[:128].T
    tails = jnp.concatenate([part[128:] for part in parts] + [jnp.zeros((96, 128), jnp.float32)], axis=0)
    out_ref[:, 0, 512:] = tails.T


def pack(elem, coord):
    return call(pack_kernel, jax.ShapeDtypeStruct((SRC, 1, 640), jnp.float32), [elem, coord], [], far=(0, 1))


def exchange(values):
    return lax.all_to_all(values, ("mesh", "bg"), split_axis=0, concat_axis=0, tiled=True)


def moved(values, axis, by):
    count = lax.axis_size(axis)
    return lax.ppermute(values, axis, [(i, (i - by) % count) for i in range(count)])


def along_mesh(block):
    return jnp.concatenate([block, moved(block, "mesh", 1), moved(block, "mesh", -1)], axis=0)


def from_below(block):
    mesh, bg = lax.axis_size("mesh"), lax.axis_size("bg")
    steps = [
        (z * bg + y, ((z + 1) % mesh) * bg + (y + 1) % bg) for z in range(mesh) for y in range(bg)
    ]
    return [block, moved(block, "mesh", -1), moved(block, "bg", -1), lax.ppermute(block, ("mesh", "bg"), steps)]


def along_bg(rows):
    return [rows, moved(rows, "bg", 1), moved(rows, "bg", -1)]


def shards(displacement, bg_coef, query_elem, query_point, query_coord):
    asked = exchange(pack(query_elem[0].T, query_coord[0].transpose(1, 2, 0)))
    own = split_nodes(displacement)
    rows = along_mesh(own)
    asked, prepared = lax.optimization_barrier((asked, prepare(bg_coef)))
    found = lookup(asked, prepared)
    found = exchange(found)
    field = along_bg(rows)
    sizes = place(found, query_point[0].T)
    sizes = from_below(sizes)
    move, terms = newton_pass(field, None, sizes, None)
    first_terms = exchange(terms)
    shift = along_bg(along_mesh(move))
    last_move, last_terms, last_own = newton_pass(field, shift, sizes, first_terms)
    own, move = join_nodes(last_own, last_move)
    last_terms = exchange(last_terms)
    return finish(own, move, first_terms, last_terms)


def solution(mesh):
    in_specs = (
        P(None, "mesh", "bg", None),
        P(None, ("mesh", "bg")),
        P(("mesh", "bg"), None, None),
        P(("mesh", "bg"), None, None),
        P(("mesh", "bg"), None, None, None),
    )
    out_specs = (P(None, "mesh", "bg", None), P())
    return jax.shard_map(shards, mesh=mesh, in_specs=in_specs, out_specs=out_specs, check_vma=False)
```

```python
import functools

import jax
import jax.numpy as jnp
import numpy as np
from jax import lax
from jax.experimental import pallas as pl
from jax.experimental.pallas import tpu as pltpu
from jax.sharding import PartitionSpec as P

SRC = 128
SLOTS = 136
TABLE = 16384
COLS = 256


GATHER_ROWS = 64
ROUNDS = 8


def in_vmem(count):
    return [pl.BlockSpec(memory_space=pltpu.VMEM) for _ in range(count)]


def call(kernel, outs, args, scratch, far=(), last=False):
    args = [a if i in far else pltpu.with_memory_space_constraint(a, pltpu.VMEM) for i, a in enumerate(args)]
    many = isinstance(outs, list)
    if not last:
        outs = [pltpu.VMEM(o.shape, o.dtype) for o in outs] if many else pltpu.VMEM(outs.shape, outs.dtype)
    return pl.pallas_call(
        kernel,
        out_shape=outs,
        in_specs=in_vmem(len(args)),
        out_specs=in_vmem(len(outs)) if many else in_vmem(1)[0],
        scratch_shapes=scratch,
    )(*args)


def prepare_kernel(table_ref, split_ref, packed_ref, unit_ref):
    top = jnp.zeros((8, 128), jnp.float32)
    for block in range(TABLE // 128):
        top = jnp.maximum(top, jnp.abs(table_ref[:, block * 128 : block * 128 + 128]))
    top = jnp.maximum(jnp.max(top, keepdims=True), 1e-30)
    unit_ref[...] = jnp.broadcast_to(top * (1.0 / 32767.0), (8, 128))
    scale = 32767.0 / top

    def whole(values):
        return (values * scale + 32768.5).astype(jnp.int32) - 32768

    for block in range(TABLE // 256):
        low = table_ref[:, block * 128 : block * 128 + 128]
        high = table_ref[:, TABLE // 2 + block * 128 : TABLE // 2 + block * 128 + 128]
        packed_ref[:, block * 128 : block * 128 + 128] = (whole(high) << 16) | (whole(low) & 65535)
    for pair in range(TABLE // (2 * COLS)):
        start = pair * 2 * COLS
        rows = jnp.concatenate(
            [table_ref[:, start : start + COLS], table_ref[:, start + COLS : start + 2 * COLS]], axis=0
        )
        upper = rows.astype(jnp.bfloat16)
        split_ref[pair * 16 : pair * 16 + 16, :COLS] = upper
        split_ref[pair * 16 : pair * 16 + 16, COLS:] = (rows - upper.astype(jnp.float32)).astype(jnp.bfloat16)


def prepare(table):
    outs = [
        jax.ShapeDtypeStruct((8 * TABLE // COLS, 2 * COLS), jnp.bfloat16),
        jax.ShapeDtypeStruct((8, TABLE // 2), jnp.int32),
        jax.ShapeDtypeStruct((8, 128), jnp.float32),
    ]
    return call(prepare_kernel, outs, [table], [], far=(0,))


def choose(leaf, masks, first, count):
    if count == 1:
        return leaf(first)
    half = count // 2
    mask = masks[half.bit_length() - 1]
    return jnp.where(mask, choose(leaf, masks, first + half, half), choose(leaf, masks, first, half))


def weigh(coef, x, y, z):
    corner = lax.broadcasted_iota(jnp.int32, coef.shape, 0)
    weight_x = jnp.where((corner & 1) == 1, x, 1.0 - x)
    weight_y = jnp.where((corner & 2) == 2, y, 1.0 - y)
    weight_z = jnp.where((corner & 4) == 4, z, 1.0 - z)
    lsize = jnp.sum(weight_x * weight_y * weight_z * coef, axis=0, keepdims=True)
    return jnp.exp(-2.0 * lsize)


def lookup_kernel(asked_ref, split_ref, packed_ref, unit_ref, found_ref, turned_ref, result_ref, column_ref):
    for j in range(4):
        turned_ref[j * SLOTS : j * SLOTS + 128, :] = asked_ref[:, 0, j * 128 : j * 128 + 128].T
    tails = asked_ref[:, 0, 512:].T
    for j in range(4):
        turned_ref[j * SLOTS + 128 : (j + 1) * SLOTS, :] = tails[j * 8 : j * 8 + 8]
    column_ref[...] = lax.broadcasted_iota(jnp.int32, (COLS, 128), 0).astype(jnp.float32).astype(jnp.bfloat16)
    one = jnp.ones((), jnp.bfloat16)
    zero = jnp.zeros((), jnp.bfloat16)

    def step(i, carry):
        base = pl.multiple_of(i * 8, 8)
        ids, xs, ys, zs = (turned_ref[pl.ds(pl.multiple_of(j * SLOTS + base, 8), 8), :] for j in range(4))
        ids = ids.astype(jnp.int32)
        unit = unit_ref[...]
        for r in range(8):
            own = jnp.broadcast_to(ids[r : r + 1], (8, 128))
            lane = own & 127
            masks = [(own & (128 << bit)) != 0 for bit in range(6)]

            def leaf(block):
                return jnp.take_along_axis(packed_ref[:, block * 128 : block * 128 + 128], lane, axis=1)

            word = choose(leaf, masks, 0, 64)
            whole = jnp.where((own & (TABLE // 2)) != 0, word, word << 16) >> 16
            coef = whole.astype(jnp.float32) * unit
            result_ref[pl.ds(base + r, 1), :] = weigh(coef, xs[r : r + 1], ys[r : r + 1], zs[r : r + 1])

        start = GATHER_ROWS + i * 9
        for pair in range(5):
            at = start + 2 * pair
            wide = 2 if pair < 4 else 1
            pair_ids, px, py, pz = (
                jnp.concatenate([turned_ref[pl.ds(j * SLOTS + at + k, 1), :] for k in range(wide)], axis=1)
                for j in range(4)
            )
            pair_ids = pair_ids.astype(jnp.int32)
            column = (pair_ids & (COLS - 1)).astype(jnp.float32).astype(jnp.bfloat16)
            chosen = jnp.concatenate(
                [
                    jnp.where(column_ref[...] == column[:, half * 128 : half * 128 + 128], one, zero)
                    for half in range(wide)
                ],
                axis=1,
            )
            picked = jnp.dot(split_ref[:, :COLS], chosen, preferred_element_type=jnp.float32) + jnp.dot(
                split_ref[:, COLS:], chosen, preferred_element_type=jnp.float32
            )
            own = jnp.broadcast_to(pair_ids, (8, 128 * wide))
            masks = [(own & (COLS << bit)) != 0 for bit in range(6)]
            coef = choose(lambda row: picked[row * 8 : row * 8 + 8], masks, 0, 64)
            value = weigh(coef, px, py, pz)
            for k in range(wide):
                result_ref[pl.ds(at + k, 1), :] = value[:, k * 128 : k * 128 + 128]
        return carry

    lax.fori_loop(0, ROUNDS, step, 0)
    found_ref[:, 0, :128] = result_ref[:128, :].T
    found_ref[:, 0, 128:] = result_ref[128:, :].T


def lookup(asked, prepared):
    scratch = [
        pltpu.VMEM((4 * SLOTS, 128), jnp.float32),
        pltpu.VMEM((SLOTS, 128), jnp.float32),
        pltpu.VMEM((COLS, 128), jnp.bfloat16),
    ]
    out = jax.ShapeDtypeStruct((SRC, 1, SLOTS), jnp.float32)
    return call(lookup_kernel, out, [asked, *prepared], scratch)


def place_kernel(found_ref, point_ref, size_ref, value_ref, row_ref, lane_ref, at_ref):
    value_ref[:128, :] = found_ref[:, 0, :128].T
    value_ref[128:, :] = found_ref[:, 0, 128:].T
    point = point_ref[...]
    line = (point * 10923) >> 21
    qx = point - line * 192
    qz = (line * 43) >> 8
    qy = line - qz * 6
    ex = (qx * 171) >> 9
    jx = qx - ex * 3
    ey = (qy * 11) >> 5
    jy = qy - ey * 3
    ez = (qz * 11) >> 5
    jz = qz - ez * 3
    row_ref[...] = (((jz * 3 + jy) * 3 + jx) * 2 + ey).astype(jnp.float32)
    lane_ref[...] = (ez * 64 + ex).astype(jnp.float32)
    at_ref[...] = lax.broadcasted_iota(jnp.int32, (128, 128), 0).astype(jnp.float32).astype(jnp.bfloat16)
    one = jnp.ones((), jnp.bfloat16)
    zero = jnp.zeros((), jnp.bfloat16)

    def step(i, total):
        values = value_ref[i * 8 : i * 8 + 8, :]
        rows = row_ref[i * 8 : i * 8 + 8, :]
        lanes = lane_ref[i * 8 : i * 8 + 8, :]
        left, right = [], []
        for r in range(8):
            value = values[r : r + 1]
            upper = value.astype(jnp.bfloat16)
            lower = (value - upper.astype(jnp.float32)).astype(jnp.bfloat16)
            row = at_ref[:64, :] == rows[r : r + 1].astype(jnp.bfloat16)
            left.append(jnp.concatenate([jnp.where(row, upper, zero), jnp.where(row, lower, zero)], axis=0))
            right.append(jnp.where(at_ref[...] == lanes[r : r + 1].astype(jnp.bfloat16), one, zero))
        left = jnp.concatenate(left, axis=1)
        right = jnp.concatenate(right, axis=1)
        return total + lax.dot_general(left, right, (((1,), (1,)), ((), ())), preferred_element_type=jnp.float32)

    total = jnp.zeros((128, 128), jnp.float32)
    for i in range(SLOTS // 8):
        total = step(i, total)
    size_ref[...] = total[:56] + total[64:120]


def place(found, point):
    scratch = [pltpu.VMEM((SLOTS, 128), jnp.float32) for _ in range(3)] + [pltpu.VMEM((128, 128), jnp.bfloat16)]
    return call(place_kernel, jax.ShapeDtypeStruct((56, 128), jnp.float32), [found, point], scratch, far=(1,))


HALF_GAP = float(np.sqrt(0.15))
OUTER, MIDDLE = 5.0 / 18.0, 8.0 / 18.0


def field_pieces(refs):
    return {(z, y): (refs[y], (z % 3) * 48) for z in (-1, 0, 1) for y in (-1, 0, 1)}


def size_pieces(refs):
    own, z_low, y_low, corner = refs
    return {(0, 0): own, (-1, 0): z_low, (0, -1): y_low, (-1, -1): corner}


def lane_index():
    return lax.broadcasted_iota(jnp.int32, (8, 128), 1)


def x_up(v):
    return jnp.where((lane_index() & 63) == 63, pltpu.roll(v, 63, 1), pltpu.roll(v, 127, 1))


def x_down(v):
    return jnp.where((lane_index() & 63) == 0, pltpu.roll(v, 65, 1), pltpu.roll(v, 1, 1))


def z_down(v):
    turned = pltpu.roll(v, 64, 1)
    return jnp.where(lane_index() < 64, pltpu.roll(turned, 4, 0), turned)


def y_down(v):
    return pltpu.roll(v, 1, 0)


def spread(low, mid, high, slopes=True, values=True):
    bend = (low + high) - 2.0 * mid
    rise = high - low
    vals = slps = None
    if values:
        centre = mid + (2.0 * HALF_GAP * HALF_GAP) * bend
        lean = HALF_GAP * rise
        vals = (centre - lean, mid, centre + lean)
    if slopes:
        change = (4.0 * HALF_GAP) * bend
        slps = (rise - change, rise, rise + change)
    return vals, slps


def collect(vals, slps):
    bend = rise = mid = None
    if vals is not None:
        outer = vals[0] + vals[2]
        bend = (2.0 * HALF_GAP * HALF_GAP) * outer
        rise = HALF_GAP * (vals[2] - vals[0])
        mid = outer + vals[1]
    if slps is not None:
        slope_bend = (4.0 * HALF_GAP) * (slps[2] - slps[0])
        slope_rise = (slps[0] + slps[2]) + slps[1]
        bend = slope_bend if bend is None else bend + slope_bend
        rise = slope_rise if rise is None else rise + slope_rise
    twice = -2.0 * bend
    return bend - rise, twice if mid is None else mid + twice, bend + rise


def at_point(c, k, jz, jy, jx):
    row = (((jz * 3 + jy) * 3 + jx) * 9 + k) * 8
    return pl.ds(pl.multiple_of(row + c * 24, 8), 8)


def forward(local, out_ref, at):
    along_z = [[spread(local(0, y, x), local(1, y, x), local(2, y, x)) for x in range(3)] for y in range(3)]
    for jz in range(3):
        value = [[along_z[y][x][0][jz] for x in range(3)] for y in range(3)]
        slope = [[along_z[y][x][1][jz] for x in range(3)] for y in range(3)]
        plain = [spread(value[0][x], value[1][x], value[2][x]) for x in range(3)]
        steep = [spread(slope[0][x], slope[1][x], slope[2][x], slopes=False)[0] for x in range(3)]
        for jy in range(3):
            dx = spread(*(plain[x][0][jy] for x in range(3)), values=False)[1]
            dy = spread(*(plain[x][1][jy] for x in range(3)), slopes=False)[0]
            dz = spread(*(steep[x][jy] for x in range(3)), slopes=False)[0]
            for jx in range(3):
                for k, part in enumerate((dx, dy, dz)):
                    out_ref[at(k, jz, jy, jx), :] = part[jx]


def backward(c, from_ref, out_ref):
    planes = []
    for jz in range(3):
        lines = []
        for jy in range(3):
            dx, dy, dz = (
                tuple(from_ref[at_point(c, k, jz, jy, jx), :] for jx in range(3)) for k in range(3)
            )
            lines.append((collect(None, dx), collect(dy, None), collect(dz, None)))
        value = [
            collect(tuple(lines[jy][0][x] for jy in range(3)), tuple(lines[jy][1][x] for jy in range(3)))
            for x in range(3)
        ]
        slope = [collect(tuple(lines[jy][2][x] for jy in range(3)), None) for x in range(3)]
        planes.append((value, slope))
    whole = [
        [
            collect(
                tuple(planes[jz][0][x][y] for jz in range(3)), tuple(planes[jz][1][x][y] for jz in range(3))
            )
            for x in range(3)
        ]
        for y in range(3)
    ]
    folded_x = [[(whole[y][0][z] + x_down(whole[y][2][z]), whole[y][1][z]) for z in range(3)] for y in range(3)]
    for x in range(2):
        folded = [(folded_x[0][z][x] + y_down(folded_x[2][z][x]), folded_x[1][z][x]) for z in range(3)]
        for y in range(2):
            for z, node in enumerate((folded[0][y] + z_down(folded[2][y]), folded[1][y])):
                row = (z * 4 + y * 2 + x) * 8
                out_ref[pl.ds(pl.multiple_of(row + c * 64, 8), 8), :] = node


def symmetric(build):
    upper = {(k, l): build(k, l) for k in range(3) for l in range(k, 3)}
    return {(k, l): upper[min(k, l), max(k, l)] for k in range(3) for l in range(3)}


def inner(a, b):
    square = (a[0, 0] * b[0, 0] + a[1, 1] * b[1, 1]) + a[2, 2] * b[2, 2]
    cross = (a[0, 1] * b[0, 1] + a[0, 2] * b[0, 2]) + a[1, 2] * b[1, 2]
    return square + 2.0 * cross


def column_dot(a, b, k, l):
    return (a[0][k] * b[0][l] + a[1][k] * b[1][l]) + a[2][k] * b[2][l]


def load_tensor(ref, jz, jy, jx):
    tensor = [[ref[at_point(c, k, jz, jy, jx), :] for k in range(3)] for c in range(3)]
    return tensor


def jacobian_at(ref, jz, jy, jx):
    tensor = load_tensor(ref, jz, jy, jx)
    return [[tensor[c][k] + 1.0 if c == k else tensor[c][k] for k in range(3)] for c in range(3)]


def strain_of(jac, size):
    return symmetric(lambda k, l: column_dot(jac, jac, k, l) * size - (1.0 if k == l else 0.0))


def weight_at(jz, jy, jx):
    along_z = jnp.where(jz == 1, MIDDLE, OUTER).astype(jnp.float32)
    return along_z * ((MIDDLE if jy == 1 else OUTER) * (MIDDLE if jx == 1 else OUTER))


def newton_step(totals):
    _, linear, quadratic, cubic, quartic, floor = (totals[:, i : i + 1] for i in range(6))
    step = jnp.zeros_like(linear)
    for _ in range(4):
        slope = linear + step * (2.0 * quadratic + step * (3.0 * cubic + step * 4.0 * quartic))
        curvature = 2.0 * quadratic + step * (6.0 * cubic + step * 12.0 * quartic)
        step = step - slope / jnp.maximum(curvature, floor + 1e-06)
    return step


def add_up(terms_ref):
    return jnp.sum(terms_ref[...], axis=0, keepdims=True)


def ring(pieces, count, out_ref, out_at, z_shift, y_shift):
    low = lax.broadcasted_iota(jnp.int32, (count, 128), 1) < 64
    places = ((-1, 1), (0, 0), (0, 1), (1, 0)) if y_shift else ((-1, 0), (-1, 1), (0, 0), (0, 1))
    for upper in range(2):
        for y, (piece_y, row) in enumerate(places):

            def piece(z):
                ref, at = pieces[z, piece_y]
                return ref[pl.ds(at + row, count, stride=2), :]

            value = piece(-upper)
            if z_shift:
                value = jnp.where(low, pltpu.roll(value, 64, 1), pltpu.roll(piece(1 - upper), 64, 1))
            out_ref[pl.ds(out_at + upper * 4 + y, count, stride=8), :] = value


def each(body):
    def run(i, carry):
        body(i)
        return carry

    lax.fori_loop(0, 3, run, 0)


def jacobians(field, nodes_ref, jac_ref):
    for z_shift in range(2):
        for y_shift in range(2):
            ring(field, 24, nodes_ref, (z_shift * 2 + y_shift) * 192, z_shift, y_shift)

    def known(c):
        def local(z, y, x):
            row = ((z == 2) * 2 + (y == 2)) * 192 + ((z % 2) * 4 + (y % 2) * 2 + x % 2) * 8
            value = nodes_ref[pl.ds(pl.multiple_of(row + c * 64, 8), 8), :]
            return x_up(value) if x == 2 else value

        return local

    each(lambda c: forward(known(c), jac_ref, functools.partial(at_point, c)))


def descend(size_ref, jac_ref, part_ref, turn_ref, move_ref):
    def size_at(jz, jy, jx):
        return size_ref[pl.ds(pl.multiple_of((jz * 9 + jy * 3 + jx) * 8, 8), 8), :]

    turn_ref[192:, :] = jnp.zeros((64, 128), jnp.float32)

    def stress(jz):
        for jy in range(3):
            for jx in range(3):
                jac = jacobian_at(jac_ref, jz, jy, jx)
                size = size_at(jz, jy, jx)
                strain = strain_of(jac, size)
                scale = size * (-4.0 * weight_at(jz, jy, jx))
                for c in range(3):
                    for k in range(3):
                        part = (strain[k, 0] * jac[c][0] + strain[k, 1] * jac[c][1]) + strain[k, 2] * jac[c][2]
                        part_ref[at_point(c, k, jz, jy, jx), :] = part * scale

    each(stress)
    each(lambda c: backward(c, part_ref, turn_ref))
    for row in range(2):
        move_ref[pl.ds(row, 24, stride=2), :] = turn_ref[pl.ds(row + 2, 24, stride=8), :]


def line_sums(size_ref, jac_ref, part_ref, turn_ref, terms_out):
    def packed(node, upper, shift):
        rows = [
            turn_ref[pl.ds(node * 8 + upper * 4 + 1 + shift + ey, 4, stride=64), :] for ey in range(2)
        ]
        return jnp.concatenate(rows, axis=0)

    def sought(z, y, x):
        node = (z % 2) * 4 + (y % 2) * 2 + x % 2
        shift = y // 2
        value = packed(node, 0, shift)
        if z == 2:
            value = pltpu.roll(value, 64, 1)
        else:
            value = jnp.where(lane_index() < 64, value, packed(node, 1, shift))
        return x_up(value) if x == 2 else value

    forward(sought, part_ref, lambda k, jz, jy, jx: pl.ds(((jz * 9 + jy * 3 + jx) * 3 + k) * 8, 8))

    def middle(ref, at, stride):
        return jnp.where(lane_index() < 64, ref[pl.ds(at, 8, stride=stride), :], ref[pl.ds(at + 4, 8, stride=stride), :])

    sub = lax.broadcasted_iota(jnp.int32, (8, 128), 0)
    sums = [jnp.zeros((8, 128), jnp.float32) for _ in range(6)]
    for start, fresh in ((0, 0), (8, 8), (16, 16), (19, 24)):
        weight = jnp.zeros((8, 128), jnp.float32)
        for i in range(fresh - start, 8):
            point = start + i
            parts = [MIDDLE if (point // by) % 3 == 1 else OUTER for by in (9, 3, 1)]
            weight = jnp.where(sub == i, (parts[0] * parts[1]) * parts[2], weight)
        for ey in range(2):
            jac = [
                [middle(jac_ref, (start * 9 + c * 3 + k) * 8 + 1 + ey, 72) for k in range(3)]
                for c in range(3)
            ]
            jac = [[jac[c][k] + 1.0 if c == k else jac[c][k] for k in range(3)] for c in range(3)]
            motion = [
                [part_ref[pl.ds((start * 3 + k) * 8 + ey * 4 + c, 8, stride=24), :] for k in range(3)]
                for c in range(3)
            ]
            size = middle(size_ref, start * 8 + 1 + ey, 8)
            zero = strain_of(jac, size)
            one = symmetric(lambda k, l: (column_dot(jac, motion, k, l) + column_dot(motion, jac, k, l)) * size)
            two = symmetric(lambda k, l: column_dot(motion, motion, k, l) * size)
            pairs = ((zero, zero), (zero, one), (zero, two), (one, two), (two, two), (one, one))
            sums = [total + weight * inner(*pair) for total, pair in zip(sums, pairs)]
    zz, zo, zt, ot, tt, gn = (jnp.sum(total, keepdims=True) for total in sums)
    lane = lax.broadcasted_iota(jnp.int32, (1, 128), 1)
    terms = jnp.zeros((1, 128), jnp.float32)
    for i, term in enumerate((zz, 2.0 * zo, gn + 2.0 * zt, 2.0 * ot, tt, gn)):
        terms = jnp.where(lane == i, term, terms)
    terms_out[...] = jnp.broadcast_to(terms, (SRC, 128))


def jacobian_kernel(*refs):
    jacobians(field_pieces(refs[:3]), refs[4], refs[3])


def descent_kernel(jac_ref, own, z_low, y_low, corner, move_ref, turn_ref, size_ref, part_ref):
    sizes = {at: (ref, 0) for at, ref in size_pieces([own, z_low, y_low, corner]).items()}
    ring(sizes, 27, size_ref, 0, 0, 0)
    descend(size_ref, jac_ref, part_ref, turn_ref, move_ref)


def line_kernel(jac_ref, turn_ref, size_ref, terms_out, part_ref):
    line_sums(size_ref, jac_ref, part_ref, turn_ref, terms_out)


def second_kernel(*refs):
    field_refs, shift_refs = refs[:3], refs[3:6]
    size_ref, terms_in, move_ref, terms_out, own_ref, nodes_ref, jac_ref, part_ref, turn_ref, sum_ref = refs[6:]
    step = newton_step(add_up(terms_in))
    for i, (field_ref, shift_ref) in enumerate(zip(field_refs, shift_refs)):
        sum_ref[i] = field_ref[...] + step * shift_ref[...]
    own_ref[...] = sum_ref[0, :48, :]
    jacobians(field_pieces([sum_ref.at[i] for i in range(3)]), nodes_ref, jac_ref)
    descend(size_ref, jac_ref, part_ref, turn_ref, move_ref)
    line_sums(size_ref, jac_ref, part_ref, turn_ref, terms_out)


NODE = jax.ShapeDtypeStruct((48, 128), jnp.float32)
TERMS = jax.ShapeDtypeStruct((SRC, 128), jnp.float32)
NODES_ROWS, JAC_ROWS, TURN_ROWS, SIZE_ROWS = 4 * 192, 243 * 8, 32 * 8, 27 * 8


def rows_of(count):
    return jax.ShapeDtypeStruct((count, 128), jnp.float32)


def scratch_of(count):
    return pltpu.VMEM((count, 128), jnp.float32)


def first_jacobians(field):
    return call(jacobian_kernel, rows_of(JAC_ROWS), field, [scratch_of(NODES_ROWS)])


def first_descent(jac, sizes):
    outs = [NODE, rows_of(TURN_ROWS), rows_of(SIZE_ROWS)]
    return call(descent_kernel, outs, [jac, *sizes], [scratch_of(JAC_ROWS)])


def first_line(jac, turn, size):
    return call(line_kernel, TERMS, [jac, turn, size], [scratch_of(81 * 8)])


def second_pass(field, shift, size, terms):
    scratch = [scratch_of(rows) for rows in (NODES_ROWS, JAC_ROWS, JAC_ROWS, TURN_ROWS)]
    scratch.append(pltpu.VMEM((3, 144, 128), jnp.float32))
    return call(second_kernel, [NODE, TERMS, NODE], [*field, *shift, size, terms], scratch)


def interleave(back):
    row = lax.broadcasted_iota(jnp.int32, (128, 128), 0)
    col = lax.broadcasted_iota(jnp.int32, (128, 128), 1)
    if back:
        row, col = col, row
    return (col == (row & 1) * 64 + (row >> 1)).astype(jnp.float32)


def split_kernel(nodes_ref, out_ref, rows_ref):
    rows = nodes_ref[...].reshape(48, 128)
    rows_ref[...] = jnp.dot(rows, interleave(False), precision=lax.Precision.HIGHEST, preferred_element_type=jnp.float32)
    low = lax.broadcasted_iota(jnp.int32, (1, 128), 1) < 64
    for c in range(3):
        for az in range(2):
            for ay in range(2):
                for ey in range(2):
                    at = c * 16 + az * 4 + ey * 2 + ay
                    first = rows_ref[at : at + 1, :]
                    second = rows_ref[at + 8 : at + 9, :]
                    to = (c * 8 + az * 4 + ay * 2) * 2 + ey
                    out_ref[to : to + 1, :] = jnp.where(low, first, pltpu.roll(second, 64, 1))
                    out_ref[to + 2 : to + 3, :] = jnp.where(low, pltpu.roll(first, 64, 1), second)


def split_nodes(nodes):
    out = jax.ShapeDtypeStruct((48, 128), jnp.float32)
    return call(split_kernel, out, [nodes], [pltpu.VMEM((48, 128), jnp.float32)], far=(0,))


def join_kernel(first_ref, second_ref, out_first_ref, out_second_ref, rows_ref):
    low = lax.broadcasted_iota(jnp.int32, (1, 128), 1) < 64
    for i, new_ref in enumerate((first_ref, second_ref)):
        for c in range(3):
            for az in range(2):
                for ay in range(2):
                    for ey in range(2):
                        at = (c * 8 + az * 4 + ay * 2) * 2 + ey
                        even = new_ref[at : at + 1, :]
                        odd = new_ref[at + 2 : at + 3, :]
                        to = i * 48 + c * 16 + az * 4 + ey * 2 + ay
                        rows_ref[to : to + 1, :] = jnp.where(low, even, pltpu.roll(odd, 64, 1))
                        rows_ref[to + 8 : to + 9, :] = jnp.where(low, pltpu.roll(even, 64, 1), odd)
    rows = jnp.dot(
        rows_ref[...], interleave(True), precision=lax.Precision.HIGHEST, preferred_element_type=jnp.float32
    )
    out_first_ref[...] = rows[:48].reshape(3, 4, 4, 128)
    out_second_ref[...] = rows[48:].reshape(3, 4, 4, 128)


def join_nodes(first, second):
    out = jax.ShapeDtypeStruct((3, 4, 4, 128), jnp.float32)
    return call(join_kernel, [out, out], [first, second], [pltpu.VMEM((96, 128), jnp.float32)])


def finish_kernel(own_ref, move_ref, first_ref, second_ref, out_ref, coeff_ref):
    second = add_up(second_ref)
    step = newton_step(second)
    for c in range(3):
        for z in range(4):
            out_ref[c, z] = own_ref[c, z] + step * move_ref[c, z]
    coeff_ref[0:1, :] = add_up(first_ref)[:, :5] * (1.0 / 32768.0)
    coeff_ref[1:2, :] = second[:, :5] * (1.0 / 32768.0)


def finish(own, move, first, second):
    outs = [jax.ShapeDtypeStruct((3, 4, 4, 128), jnp.float32), jax.ShapeDtypeStruct((2, 5), jnp.float32)]
    return call(finish_kernel, outs, [own, move, first, second], [], last=True)


def pack_kernel(elem_ref, coord_ref, out_ref):
    parts = [elem_ref[...].astype(jnp.float32)] + [coord_ref[j] for j in range(3)]
    for j, part in enumerate(parts):
        out_ref[:, 0, j * 128 : j * 128 + 128] = part[:128].T
    tails = jnp.concatenate([part[128:] for part in parts] + [jnp.zeros((96, 128), jnp.float32)], axis=0)
    out_ref[:, 0, 512:] = tails.T


def pack(elem, coord):
    return call(pack_kernel, jax.ShapeDtypeStruct((SRC, 1, 640), jnp.float32), [elem, coord], [], far=(0, 1))


def exchange(values):
    return lax.all_to_all(values, ("mesh", "bg"), split_axis=0, concat_axis=0, tiled=True)


def moved(values, axis, by):
    count = lax.axis_size(axis)
    return lax.ppermute(values, axis, [(i, (i - by) % count) for i in range(count)])


def along_mesh(block):
    return jnp.concatenate([block, moved(block, "mesh", 1), moved(block, "mesh", -1)], axis=0)


def from_below(block):
    mesh, bg = lax.axis_size("mesh"), lax.axis_size("bg")
    steps = [
        (z * bg + y, ((z + 1) % mesh) * bg + (y + 1) % bg) for z in range(mesh) for y in range(bg)
    ]
    return [block, moved(block, "mesh", -1), moved(block, "bg", -1), lax.ppermute(block, ("mesh", "bg"), steps)]


def along_bg(rows):
    return [rows, moved(rows, "bg", 1), moved(rows, "bg", -1)]


def shards(displacement, bg_coef, query_elem, query_point, query_coord):
    asked = exchange(pack(query_elem[0].T, query_coord[0].transpose(1, 2, 0)))
    own = split_nodes(displacement)
    rows = along_mesh(own)
    asked, prepared = lax.optimization_barrier((asked, prepare(bg_coef)))
    found = lookup(asked, prepared)
    found = exchange(found)
    field = along_bg(rows)
    sizes = place(found, query_point[0].T)
    sizes = from_below(sizes)
    jac = first_jacobians(field)
    move, turn, size = first_descent(jac, sizes)
    rows = along_mesh(move)
    terms = first_line(jac, turn, size)
    first_terms = exchange(terms)
    shift = along_bg(rows)
    last_move, last_terms, last_own = second_pass(field, shift, size, first_terms)
    own, move = join_nodes(last_own, last_move)
    last_terms = exchange(last_terms)
    return finish(own, move, first_terms, last_terms)


def solution(mesh):
    in_specs = (
        P(None, "mesh", "bg", None),
        P(None, ("mesh", "bg")),
        P(("mesh", "bg"), None, None),
        P(("mesh", "bg"), None, None),
        P(("mesh", "bg"), None, None, None),
    )
    out_specs = (P(None, "mesh", "bg", None), P())
    return jax.shard_map(shards, mesh=mesh, in_specs=in_specs, out_specs=out_specs, check_vma=False)
```

```python
import functools

import jax
import jax.numpy as jnp
import numpy as np
from jax import lax
from jax.experimental import pallas as pl
from jax.experimental.pallas import tpu as pltpu
from jax.sharding import PartitionSpec as P

SRC = 128
SLOTS = 136
TABLE = 16384
COLS = 256


GATHER_ROWS = 64
ROUNDS = 8


def in_vmem(count):
    return [pl.BlockSpec(memory_space=pltpu.VMEM) for _ in range(count)]


def call(kernel, outs, args, scratch, far=(), last=False):
    args = [a if i in far else pltpu.with_memory_space_constraint(a, pltpu.VMEM) for i, a in enumerate(args)]
    many = isinstance(outs, list)
    if not last:
        outs = [pltpu.VMEM(o.shape, o.dtype) for o in outs] if many else pltpu.VMEM(outs.shape, outs.dtype)
    return pl.pallas_call(
        kernel,
        out_shape=outs,
        in_specs=in_vmem(len(args)),
        out_specs=in_vmem(len(outs)) if many else in_vmem(1)[0],
        scratch_shapes=scratch,
    )(*args)


def prepare_kernel(table_ref, split_ref, packed_ref, unit_ref):
    top = jnp.zeros((8, 128), jnp.float32)
    for block in range(TABLE // 128):
        top = jnp.maximum(top, jnp.abs(table_ref[:, block * 128 : block * 128 + 128]))
    top = jnp.maximum(jnp.max(top, keepdims=True), 1e-30)
    unit_ref[...] = jnp.broadcast_to(top * (1.0 / 32767.0), (8, 128))
    scale = 32767.0 / top

    def whole(values):
        return (values * scale + 32768.5).astype(jnp.int32) - 32768

    for block in range(TABLE // 256):
        low = table_ref[:, block * 128 : block * 128 + 128]
        high = table_ref[:, TABLE // 2 + block * 128 : TABLE // 2 + block * 128 + 128]
        packed_ref[:, block * 128 : block * 128 + 128] = (whole(high) << 16) | (whole(low) & 65535)
    for pair in range(TABLE // (2 * COLS)):
        start = pair * 2 * COLS
        rows = jnp.concatenate(
            [table_ref[:, start : start + COLS], table_ref[:, start + COLS : start + 2 * COLS]], axis=0
        )
        upper = rows.astype(jnp.bfloat16)
        split_ref[pair * 16 : pair * 16 + 16, :COLS] = upper
        split_ref[pair * 16 : pair * 16 + 16, COLS:] = (rows - upper.astype(jnp.float32)).astype(jnp.bfloat16)


def prepare(table):
    outs = [
        jax.ShapeDtypeStruct((8 * TABLE // COLS, 2 * COLS), jnp.bfloat16),
        jax.ShapeDtypeStruct((8, TABLE // 2), jnp.int32),
        jax.ShapeDtypeStruct((8, 128), jnp.float32),
    ]
    return call(prepare_kernel, outs, [table], [], far=(0,))


def choose(leaf, masks, first, count):
    if count == 1:
        return leaf(first)
    half = count // 2
    mask = masks[half.bit_length() - 1]
    return jnp.where(mask, choose(leaf, masks, first + half, half), choose(leaf, masks, first, half))


def weigh(coef, x, y, z):
    corner = lax.broadcasted_iota(jnp.int32, coef.shape, 0)
    weight_x = jnp.where((corner & 1) == 1, x, 1.0 - x)
    weight_y = jnp.where((corner & 2) == 2, y, 1.0 - y)
    weight_z = jnp.where((corner & 4) == 4, z, 1.0 - z)
    lsize = jnp.sum(weight_x * weight_y * weight_z * coef, axis=0, keepdims=True)
    return jnp.exp(-2.0 * lsize)


def lookup_kernel(asked_ref, split_ref, packed_ref, unit_ref, found_ref, turned_ref, result_ref, column_ref):
    for j in range(4):
        turned_ref[j * SLOTS : j * SLOTS + 128, :] = asked_ref[:, 0, j * 128 : j * 128 + 128].T
    tails = asked_ref[:, 0, 512:].T
    for j in range(4):
        turned_ref[j * SLOTS + 128 : (j + 1) * SLOTS, :] = tails[j * 8 : j * 8 + 8]
    column_ref[...] = lax.broadcasted_iota(jnp.int32, (COLS, 128), 0).astype(jnp.float32).astype(jnp.bfloat16)
    one = jnp.ones((), jnp.bfloat16)
    zero = jnp.zeros((), jnp.bfloat16)

    def step(i, carry):
        base = pl.multiple_of(i * 8, 8)
        ids, xs, ys, zs = (turned_ref[pl.ds(pl.multiple_of(j * SLOTS + base, 8), 8), :] for j in range(4))
        ids = ids.astype(jnp.int32)
        unit = unit_ref[...]
        for r in range(8):
            own = jnp.broadcast_to(ids[r : r + 1], (8, 128))
            lane = own & 127
            masks = [(own & (128 << bit)) != 0 for bit in range(6)]

            def leaf(block):
                return jnp.take_along_axis(packed_ref[:, block * 128 : block * 128 + 128], lane, axis=1)

            word = choose(leaf, masks, 0, 64)
            whole = jnp.where((own & (TABLE // 2)) != 0, word, word << 16) >> 16
            coef = whole.astype(jnp.float32) * unit
            result_ref[pl.ds(base + r, 1), :] = weigh(coef, xs[r : r + 1], ys[r : r + 1], zs[r : r + 1])

        start = GATHER_ROWS + i * 9
        for pair in range(5):
            at = start + 2 * pair
            wide = 2 if pair < 4 else 1
            pair_ids, px, py, pz = (
                jnp.concatenate([turned_ref[pl.ds(j * SLOTS + at + k, 1), :] for k in range(wide)], axis=1)
                for j in range(4)
            )
            pair_ids = pair_ids.astype(jnp.int32)
            column = (pair_ids & (COLS - 1)).astype(jnp.float32).astype(jnp.bfloat16)
            chosen = jnp.concatenate(
                [
                    jnp.where(column_ref[...] == column[:, half * 128 : half * 128 + 128], one, zero)
                    for half in range(wide)
                ],
                axis=1,
            )
            picked = jnp.dot(split_ref[:, :COLS], chosen, preferred_element_type=jnp.float32) + jnp.dot(
                split_ref[:, COLS:], chosen, preferred_element_type=jnp.float32
            )
            own = jnp.broadcast_to(pair_ids, (8, 128 * wide))
            masks = [(own & (COLS << bit)) != 0 for bit in range(6)]
            coef = choose(lambda row: picked[row * 8 : row * 8 + 8], masks, 0, 64)
            value = weigh(coef, px, py, pz)
            for k in range(wide):
                result_ref[pl.ds(at + k, 1), :] = value[:, k * 128 : k * 128 + 128]
        return carry

    lax.fori_loop(0, ROUNDS, step, 0)
    found_ref[:, 0, :128] = result_ref[:128, :].T
    found_ref[:, 0, 128:] = result_ref[128:, :].T


def lookup(asked, prepared):
    scratch = [
        pltpu.VMEM((4 * SLOTS, 128), jnp.float32),
        pltpu.VMEM((SLOTS, 128), jnp.float32),
        pltpu.VMEM((COLS, 128), jnp.bfloat16),
    ]
    out = jax.ShapeDtypeStruct((SRC, 1, SLOTS), jnp.float32)
    return call(lookup_kernel, out, [asked, *prepared], scratch)


def place_kernel(found_ref, point_ref, size_ref, value_ref, row_ref, lane_ref, at_ref):
    value_ref[:128, :] = found_ref[:, 0, :128].T
    value_ref[128:, :] = found_ref[:, 0, 128:].T
    point = point_ref[...]
    line = (point * 10923) >> 21
    qx = point - line * 192
    qz = (line * 43) >> 8
    qy = line - qz * 6
    ex = (qx * 171) >> 9
    jx = qx - ex * 3
    ey = (qy * 11) >> 5
    jy = qy - ey * 3
    ez = (qz * 11) >> 5
    jz = qz - ez * 3
    row_ref[...] = (((jz * 3 + jy) * 3 + jx) * 2 + ey).astype(jnp.float32)
    lane_ref[...] = (ez * 64 + ex).astype(jnp.float32)
    at_ref[...] = lax.broadcasted_iota(jnp.int32, (128, 128), 0).astype(jnp.float32).astype(jnp.bfloat16)
    one = jnp.ones((), jnp.bfloat16)
    zero = jnp.zeros((), jnp.bfloat16)

    def step(i, total):
        values = value_ref[i * 8 : i * 8 + 8, :]
        rows = row_ref[i * 8 : i * 8 + 8, :]
        lanes = lane_ref[i * 8 : i * 8 + 8, :]
        left, right = [], []
        for r in range(8):
            value = values[r : r + 1]
            upper = value.astype(jnp.bfloat16)
            lower = (value - upper.astype(jnp.float32)).astype(jnp.bfloat16)
            row = at_ref[:64, :] == rows[r : r + 1].astype(jnp.bfloat16)
            left.append(jnp.concatenate([jnp.where(row, upper, zero), jnp.where(row, lower, zero)], axis=0))
            right.append(jnp.where(at_ref[...] == lanes[r : r + 1].astype(jnp.bfloat16), one, zero))
        left = jnp.concatenate(left, axis=1)
        right = jnp.concatenate(right, axis=1)
        return total + lax.dot_general(left, right, (((1,), (1,)), ((), ())), preferred_element_type=jnp.float32)

    total = jnp.zeros((128, 128), jnp.float32)
    for i in range(SLOTS // 8):
        total = step(i, total)
    size_ref[...] = total[:56] + total[64:120]


def place(found, point):
    scratch = [pltpu.VMEM((SLOTS, 128), jnp.float32) for _ in range(3)] + [pltpu.VMEM((128, 128), jnp.bfloat16)]
    return call(place_kernel, jax.ShapeDtypeStruct((56, 128), jnp.float32), [found, point], scratch, far=(1,))


HALF_GAP = float(np.sqrt(0.15))
OUTER, MIDDLE = 5.0 / 18.0, 8.0 / 18.0


def field_pieces(refs):
    return {(z, y): (refs[y], (z % 3) * 48) for z in (-1, 0, 1) for y in (-1, 0, 1)}


def size_pieces(refs):
    own, z_low, y_low, corner = refs
    return {(0, 0): own, (-1, 0): z_low, (0, -1): y_low, (-1, -1): corner}


def lane_index():
    return lax.broadcasted_iota(jnp.int32, (8, 128), 1)


def x_up(v):
    return jnp.where((lane_index() & 63) == 63, pltpu.roll(v, 63, 1), pltpu.roll(v, 127, 1))


def x_down(v):
    return jnp.where((lane_index() & 63) == 0, pltpu.roll(v, 65, 1), pltpu.roll(v, 1, 1))


def z_down(v):
    turned = pltpu.roll(v, 64, 1)
    return jnp.where(lane_index() < 64, pltpu.roll(turned, 4, 0), turned)


def y_down(v):
    return pltpu.roll(v, 1, 0)


def spread(low, mid, high, slopes=True, values=True):
    bend = (low + high) - 2.0 * mid
    rise = high - low
    vals = slps = None
    if values:
        centre = mid + (2.0 * HALF_GAP * HALF_GAP) * bend
        lean = HALF_GAP * rise
        vals = (centre - lean, mid, centre + lean)
    if slopes:
        change = (4.0 * HALF_GAP) * bend
        slps = (rise - change, rise, rise + change)
    return vals, slps


def collect(vals, slps):
    bend = rise = mid = None
    if vals is not None:
        outer = vals[0] + vals[2]
        bend = (2.0 * HALF_GAP * HALF_GAP) * outer
        rise = HALF_GAP * (vals[2] - vals[0])
        mid = outer + vals[1]
    if slps is not None:
        slope_bend = (4.0 * HALF_GAP) * (slps[2] - slps[0])
        slope_rise = (slps[0] + slps[2]) + slps[1]
        bend = slope_bend if bend is None else bend + slope_bend
        rise = slope_rise if rise is None else rise + slope_rise
    twice = -2.0 * bend
    return bend - rise, twice if mid is None else mid + twice, bend + rise


def at_point(c, k, jz, jy, jx):
    row = (((jz * 3 + jy) * 3 + jx) * 9 + k) * 8
    return pl.ds(pl.multiple_of(row + c * 24, 8), 8)


def forward(local, out_ref, at):
    along_z = [[spread(local(0, y, x), local(1, y, x), local(2, y, x)) for x in range(3)] for y in range(3)]
    for jz in range(3):
        value = [[along_z[y][x][0][jz] for x in range(3)] for y in range(3)]
        slope = [[along_z[y][x][1][jz] for x in range(3)] for y in range(3)]
        plain = [spread(value[0][x], value[1][x], value[2][x]) for x in range(3)]
        steep = [spread(slope[0][x], slope[1][x], slope[2][x], slopes=False)[0] for x in range(3)]
        for jy in range(3):
            dx = spread(*(plain[x][0][jy] for x in range(3)), values=False)[1]
            dy = spread(*(plain[x][1][jy] for x in range(3)), slopes=False)[0]
            dz = spread(*(steep[x][jy] for x in range(3)), slopes=False)[0]
            for jx in range(3):
                for k, part in enumerate((dx, dy, dz)):
                    out_ref[at(k, jz, jy, jx), :] = part[jx]


def backward(c, from_ref, out_ref):
    planes = []
    for jz in range(3):
        lines = []
        for jy in range(3):
            dx, dy, dz = (
                tuple(from_ref[at_point(c, k, jz, jy, jx), :] for jx in range(3)) for k in range(3)
            )
            lines.append((collect(None, dx), collect(dy, None), collect(dz, None)))
        value = [
            collect(tuple(lines[jy][0][x] for jy in range(3)), tuple(lines[jy][1][x] for jy in range(3)))
            for x in range(3)
        ]
        slope = [collect(tuple(lines[jy][2][x] for jy in range(3)), None) for x in range(3)]
        planes.append((value, slope))
    whole = [
        [
            collect(
                tuple(planes[jz][0][x][y] for jz in range(3)), tuple(planes[jz][1][x][y] for jz in range(3))
            )
            for x in range(3)
        ]
        for y in range(3)
    ]
    folded_x = [[(whole[y][0][z] + x_down(whole[y][2][z]), whole[y][1][z]) for z in range(3)] for y in range(3)]
    for x in range(2):
        folded = [(folded_x[0][z][x] + y_down(folded_x[2][z][x]), folded_x[1][z][x]) for z in range(3)]
        for y in range(2):
            for z, node in enumerate((folded[0][y] + z_down(folded[2][y]), folded[1][y])):
                row = (z * 4 + y * 2 + x) * 8
                out_ref[pl.ds(pl.multiple_of(row + c * 64, 8), 8), :] = node


def symmetric(build):
    upper = {(k, l): build(k, l) for k in range(3) for l in range(k, 3)}
    return {(k, l): upper[min(k, l), max(k, l)] for k in range(3) for l in range(3)}


def inner(a, b):
    square = (a[0, 0] * b[0, 0] + a[1, 1] * b[1, 1]) + a[2, 2] * b[2, 2]
    cross = (a[0, 1] * b[0, 1] + a[0, 2] * b[0, 2]) + a[1, 2] * b[1, 2]
    return square + 2.0 * cross


def column_dot(a, b, k, l):
    return (a[0][k] * b[0][l] + a[1][k] * b[1][l]) + a[2][k] * b[2][l]


def load_tensor(ref, jz, jy, jx):
    tensor = [[ref[at_point(c, k, jz, jy, jx), :] for k in range(3)] for c in range(3)]
    return tensor


def jacobian_at(ref, jz, jy, jx):
    tensor = load_tensor(ref, jz, jy, jx)
    return [[tensor[c][k] + 1.0 if c == k else tensor[c][k] for k in range(3)] for c in range(3)]


def strain_of(jac, size):
    return symmetric(lambda k, l: column_dot(jac, jac, k, l) * size - (1.0 if k == l else 0.0))


def weight_at(jz, jy, jx):
    along_z = jnp.where(jz == 1, MIDDLE, OUTER).astype(jnp.float32)
    return along_z * ((MIDDLE if jy == 1 else OUTER) * (MIDDLE if jx == 1 else OUTER))


def newton_step(totals):
    _, linear, quadratic, cubic, quartic, floor = (jnp.broadcast_to(totals[:, i : i + 1], (8, 128)) for i in range(6))
    step = jnp.zeros_like(linear)
    for _ in range(4):
        slope = linear + step * (2.0 * quadratic + step * (3.0 * cubic + step * 4.0 * quartic))
        curvature = 2.0 * quadratic + step * (6.0 * cubic + step * 12.0 * quartic)
        step = step - slope / jnp.maximum(curvature, floor + 1e-06)
    return step


def add_up(terms_ref):
    return jnp.sum(terms_ref[...], axis=0, keepdims=True)


def ring(pieces, count, out_ref, out_at, z_shift, y_shift):
    low = lax.broadcasted_iota(jnp.int32, (count, 128), 1) < 64
    places = ((-1, 1), (0, 0), (0, 1), (1, 0)) if y_shift else ((-1, 0), (-1, 1), (0, 0), (0, 1))
    for upper in range(2):
        for y, (piece_y, row) in enumerate(places):

            def piece(z):
                ref, at = pieces[z, piece_y]
                return ref[pl.ds(at + row, count, stride=2), :]

            value = piece(-upper)
            if z_shift:
                value = jnp.where(low, pltpu.roll(value, 64, 1), pltpu.roll(piece(1 - upper), 64, 1))
            out_ref[pl.ds(out_at + upper * 4 + y, count, stride=8), :] = value


def each(body):
    def run(i, carry):
        body(i)
        return carry

    lax.fori_loop(0, 3, run, 0)


def jacobians(field, nodes_ref, jac_ref):
    for z_shift in range(2):
        for y_shift in range(2):
            ring(field, 24, nodes_ref, (z_shift * 2 + y_shift) * 192, z_shift, y_shift)

    def known(c):
        def local(z, y, x):
            row = ((z == 2) * 2 + (y == 2)) * 192 + ((z % 2) * 4 + (y % 2) * 2 + x % 2) * 8
            value = nodes_ref[pl.ds(pl.multiple_of(row + c * 64, 8), 8), :]
            return x_up(value) if x == 2 else value

        return local

    each(lambda c: forward(known(c), jac_ref, functools.partial(at_point, c)))


def descend(size_ref, jac_ref, part_ref, turn_ref, move_ref):
    def size_at(jz, jy, jx):
        return size_ref[pl.ds(pl.multiple_of((jz * 9 + jy * 3 + jx) * 8, 8), 8), :]

    turn_ref[192:, :] = jnp.zeros((64, 128), jnp.float32)

    def stress(jz):
        for jy in range(3):
            for jx in range(3):
                jac = jacobian_at(jac_ref, jz, jy, jx)
                size = size_at(jz, jy, jx)
                strain = strain_of(jac, size)
                scale = size * (-4.0 * weight_at(jz, jy, jx))
                for c in range(3):
                    for k in range(3):
                        part = (strain[k, 0] * jac[c][0] + strain[k, 1] * jac[c][1]) + strain[k, 2] * jac[c][2]
                        part_ref[at_point(c, k, jz, jy, jx), :] = part * scale

    each(stress)
    each(lambda c: backward(c, part_ref, turn_ref))
    for row in range(2):
        move_ref[pl.ds(row, 24, stride=2), :] = turn_ref[pl.ds(row + 2, 24, stride=8), :]


def line_sums(size_ref, jac_ref, part_ref, turn_ref, terms_out):
    def packed(node, upper, shift):
        rows = [
            turn_ref[pl.ds(node * 8 + upper * 4 + 1 + shift + ey, 4, stride=64), :] for ey in range(2)
        ]
        return jnp.concatenate(rows, axis=0)

    def sought(z, y, x):
        node = (z % 2) * 4 + (y % 2) * 2 + x % 2
        shift = y // 2
        value = packed(node, 0, shift)
        if z == 2:
            value = pltpu.roll(value, 64, 1)
        else:
            value = jnp.where(lane_index() < 64, value, packed(node, 1, shift))
        return x_up(value) if x == 2 else value

    forward(sought, part_ref, lambda k, jz, jy, jx: pl.ds(((jz * 9 + jy * 3 + jx) * 3 + k) * 8, 8))

    def middle(ref, at, stride):
        return jnp.where(lane_index() < 64, ref[pl.ds(at, 8, stride=stride), :], ref[pl.ds(at + 4, 8, stride=stride), :])

    sub = lax.broadcasted_iota(jnp.int32, (8, 128), 0)
    sums = [jnp.zeros((8, 128), jnp.float32) for _ in range(6)]
    for start, fresh in ((0, 0), (8, 8), (16, 16), (19, 24)):
        weight = jnp.zeros((8, 128), jnp.float32)
        for i in range(fresh - start, 8):
            point = start + i
            parts = [MIDDLE if (point // by) % 3 == 1 else OUTER for by in (9, 3, 1)]
            weight = jnp.where(sub == i, (parts[0] * parts[1]) * parts[2], weight)
        for ey in range(2):
            jac = [
                [middle(jac_ref, (start * 9 + c * 3 + k) * 8 + 1 + ey, 72) for k in range(3)]
                for c in range(3)
            ]
            jac = [[jac[c][k] + 1.0 if c == k else jac[c][k] for k in range(3)] for c in range(3)]
            motion = [
                [part_ref[pl.ds((start * 3 + k) * 8 + ey * 4 + c, 8, stride=24), :] for k in range(3)]
                for c in range(3)
            ]
            size = middle(size_ref, start * 8 + 1 + ey, 8)
            zero = strain_of(jac, size)
            one = symmetric(lambda k, l: (column_dot(jac, motion, k, l) + column_dot(motion, jac, k, l)) * size)
            two = symmetric(lambda k, l: column_dot(motion, motion, k, l) * size)
            pairs = ((zero, zero), (zero, one), (zero, two), (one, two), (two, two), (one, one))
            sums = [total + weight * inner(*pair) for total, pair in zip(sums, pairs)]
    zz, zo, zt, ot, tt, gn = (jnp.sum(total, keepdims=True) for total in sums)
    lane = lax.broadcasted_iota(jnp.int32, (1, 128), 1)
    terms = jnp.zeros((1, 128), jnp.float32)
    for i, term in enumerate((zz, 2.0 * zo, gn + 2.0 * zt, 2.0 * ot, tt, gn)):
        terms = jnp.where(lane == i, term, terms)
    terms_out[...] = jnp.broadcast_to(terms, (SRC, 128))


def jacobian_kernel(*refs):
    jacobians(field_pieces(refs[:3]), refs[4], refs[3])


def descent_kernel(jac_ref, own, z_low, y_low, corner, move_ref, turn_ref, size_ref, part_ref):
    sizes = {at: (ref, 0) for at, ref in size_pieces([own, z_low, y_low, corner]).items()}
    ring(sizes, 27, size_ref, 0, 0, 0)
    descend(size_ref, jac_ref, part_ref, turn_ref, move_ref)


def line_kernel(jac_ref, turn_ref, size_ref, terms_out, part_ref):
    line_sums(size_ref, jac_ref, part_ref, turn_ref, terms_out)


def second_kernel(before_ref, drift_ref, size_ref, terms_in, move_ref, terms_out, step_ref, jac_ref, part_ref, turn_ref):
    step = newton_step(add_up(terms_in))
    step_ref[...] = step
    for row in range(0, JAC_ROWS, 8):
        rows = slice(row, row + 8)
        jac_ref[rows, :] = before_ref[rows, :] + step * drift_ref[rows, :]
    descend(size_ref, jac_ref, part_ref, turn_ref, move_ref)
    line_sums(size_ref, jac_ref, part_ref, turn_ref, terms_out)


NODE = jax.ShapeDtypeStruct((48, 128), jnp.float32)
TERMS = jax.ShapeDtypeStruct((SRC, 128), jnp.float32)
NODES_ROWS, JAC_ROWS, TURN_ROWS, SIZE_ROWS = 4 * 192, 243 * 8, 32 * 8, 27 * 8


def rows_of(count):
    return jax.ShapeDtypeStruct((count, 128), jnp.float32)


def scratch_of(count):
    return pltpu.VMEM((count, 128), jnp.float32)


def all_jacobians(field):
    return call(jacobian_kernel, rows_of(JAC_ROWS), field, [scratch_of(NODES_ROWS)])


def first_descent(jac, sizes):
    outs = [NODE, rows_of(TURN_ROWS), rows_of(SIZE_ROWS)]
    return call(descent_kernel, outs, [jac, *sizes], [scratch_of(JAC_ROWS)])


def first_line(jac, turn, size):
    return call(line_kernel, TERMS, [jac, turn, size], [scratch_of(81 * 8)])


def second_pass(jac, drift, size, terms):
    scratch = [scratch_of(rows) for rows in (JAC_ROWS, JAC_ROWS, TURN_ROWS)]
    return call(second_kernel, [NODE, TERMS, rows_of(8)], [jac, drift, size, terms], scratch)


def interleave(back):
    row = lax.broadcasted_iota(jnp.int32, (128, 128), 0)
    col = lax.broadcasted_iota(jnp.int32, (128, 128), 1)
    if back:
        row, col = col, row
    return (col == (row & 1) * 64 + (row >> 1)).astype(jnp.float32)


def split_kernel(nodes_ref, out_ref, rows_ref):
    rows = nodes_ref[...].reshape(48, 128)
    rows_ref[...] = jnp.dot(rows, interleave(False), precision=lax.Precision.HIGHEST, preferred_element_type=jnp.float32)
    low = lax.broadcasted_iota(jnp.int32, (1, 128), 1) < 64
    for c in range(3):
        for az in range(2):
            for ay in range(2):
                for ey in range(2):
                    at = c * 16 + az * 4 + ey * 2 + ay
                    first = rows_ref[at : at + 1, :]
                    second = rows_ref[at + 8 : at + 9, :]
                    to = (c * 8 + az * 4 + ay * 2) * 2 + ey
                    out_ref[to : to + 1, :] = jnp.where(low, first, pltpu.roll(second, 64, 1))
                    out_ref[to + 2 : to + 3, :] = jnp.where(low, pltpu.roll(first, 64, 1), second)


def split_nodes(nodes):
    out = jax.ShapeDtypeStruct((48, 128), jnp.float32)
    return call(split_kernel, out, [nodes], [pltpu.VMEM((48, 128), jnp.float32)], far=(0,))


def join_kernel(count, *refs):
    rows_ref = refs[-1]
    low = lax.broadcasted_iota(jnp.int32, (1, 128), 1) < 64
    for i, new_ref in enumerate(refs[:count]):
        for c in range(3):
            for az in range(2):
                for ay in range(2):
                    for ey in range(2):
                        at = (c * 8 + az * 4 + ay * 2) * 2 + ey
                        even = new_ref[at : at + 1, :]
                        odd = new_ref[at + 2 : at + 3, :]
                        to = i * 48 + c * 16 + az * 4 + ey * 2 + ay
                        rows_ref[to : to + 1, :] = jnp.where(low, even, pltpu.roll(odd, 64, 1))
                        rows_ref[to + 8 : to + 9, :] = jnp.where(low, pltpu.roll(even, 64, 1), odd)
    rows = jnp.dot(
        rows_ref[...], interleave(True), precision=lax.Precision.HIGHEST, preferred_element_type=jnp.float32
    )
    for i, out_ref in enumerate(refs[count : 2 * count]):
        out_ref[...] = rows[i * 48 : i * 48 + 48].reshape(3, 4, 4, 128)


def join_nodes(*nodes):
    outs = [jax.ShapeDtypeStruct((3, 4, 4, 128), jnp.float32) for _ in nodes]
    kernel = functools.partial(join_kernel, len(nodes))
    return call(kernel, outs, list(nodes), [scratch_of(48 * len(nodes))])


def finish_kernel(own_ref, first_move_ref, last_move_ref, step_ref, first_ref, second_ref, out_ref, coeff_ref):
    second = add_up(second_ref)
    step = newton_step(second)[:4]
    first_step = step_ref[:4, :]
    for c in range(3):
        for z in range(4):
            field = own_ref[c, z] + first_step * first_move_ref[c, z]
            out_ref[c, z] = field + step * last_move_ref[c, z]
    coeff_ref[0:1, :] = add_up(first_ref)[:, :5] * (1.0 / 32768.0)
    coeff_ref[1:2, :] = second[:, :5] * (1.0 / 32768.0)


def finish(*args):
    outs = [jax.ShapeDtypeStruct((3, 4, 4, 128), jnp.float32), jax.ShapeDtypeStruct((2, 5), jnp.float32)]
    return call(finish_kernel, outs, list(args), [], last=True)


def pack_kernel(elem_ref, coord_ref, out_ref):
    parts = [elem_ref[...].astype(jnp.float32)] + [coord_ref[j] for j in range(3)]
    for j, part in enumerate(parts):
        out_ref[:, 0, j * 128 : j * 128 + 128] = part[:128].T
    tails = jnp.concatenate([part[128:] for part in parts] + [jnp.zeros((96, 128), jnp.float32)], axis=0)
    out_ref[:, 0, 512:] = tails.T


def pack(elem, coord):
    return call(pack_kernel, jax.ShapeDtypeStruct((SRC, 1, 640), jnp.float32), [elem, coord], [], far=(0, 1))


def exchange(values):
    return lax.all_to_all(values, ("mesh", "bg"), split_axis=0, concat_axis=0, tiled=True)


def moved(values, axis, by):
    count = lax.axis_size(axis)
    return lax.ppermute(values, axis, [(i, (i - by) % count) for i in range(count)])


def along_mesh(block):
    return jnp.concatenate([block, moved(block, "mesh", 1), moved(block, "mesh", -1)], axis=0)


def from_below(block):
    mesh, bg = lax.axis_size("mesh"), lax.axis_size("bg")
    steps = [
        (z * bg + y, ((z + 1) % mesh) * bg + (y + 1) % bg) for z in range(mesh) for y in range(bg)
    ]
    return [block, moved(block, "mesh", -1), moved(block, "bg", -1), lax.ppermute(block, ("mesh", "bg"), steps)]


def along_bg(rows):
    return [rows, moved(rows, "bg", 1), moved(rows, "bg", -1)]


def shards(displacement, bg_coef, query_elem, query_point, query_coord):
    asked = exchange(pack(query_elem[0].T, query_coord[0].transpose(1, 2, 0)))
    own = split_nodes(displacement)
    rows = along_mesh(own)
    asked, prepared = lax.optimization_barrier((asked, prepare(bg_coef)))
    found = lookup(asked, prepared)
    found = exchange(found)
    field = along_bg(rows)
    sizes = place(found, query_point[0].T)
    sizes = from_below(sizes)
    jac = all_jacobians(field)
    move, turn, size = first_descent(jac, sizes)
    rows = along_mesh(move)
    terms = first_line(jac, turn, size)
    first_terms = exchange(terms)
    shift = along_bg(rows)
    drift = all_jacobians(shift)
    last_move, last_terms, step = second_pass(jac, drift, size, first_terms)
    last_terms = exchange(last_terms)
    nodes = join_nodes(own, move, last_move)
    return finish(*nodes, step, first_terms, last_terms)


def solution(mesh):
    in_specs = (
        P(None, "mesh", "bg", None),
        P(None, ("mesh", "bg")),
        P(("mesh", "bg"), None, None),
        P(("mesh", "bg"), None, None),
        P(("mesh", "bg"), None, None, None),
    )
    out_specs = (P(None, "mesh", "bg", None), P())
    return jax.shard_map(shards, mesh=mesh, in_specs=in_specs, out_specs=out_specs, check_vma=False)
```

```python
import functools

import jax
import jax.numpy as jnp
import numpy as np
from jax import lax
from jax.experimental import pallas as pl
from jax.experimental.pallas import tpu as pltpu
from jax.sharding import PartitionSpec as P

SRC = 128
SLOTS = 136
TABLE = 16384
COLS = 256


ROUNDS = 2
GATHERED = 36
PAIRS = 16


def in_vmem(count):
    return [pl.BlockSpec(memory_space=pltpu.VMEM) for _ in range(count)]


def call(kernel, outs, args, scratch, far=(), last=False):
    args = [a if i in far else pltpu.with_memory_space_constraint(a, pltpu.VMEM) for i, a in enumerate(args)]
    many = isinstance(outs, list)
    if not last:
        outs = [pltpu.VMEM(o.shape, o.dtype) for o in outs] if many else pltpu.VMEM(outs.shape, outs.dtype)
    return pl.pallas_call(
        kernel,
        out_shape=outs,
        in_specs=in_vmem(len(args)),
        out_specs=in_vmem(len(outs)) if many else in_vmem(1)[0],
        scratch_shapes=scratch,
    )(*args)


def prepare_kernel(table_ref, split_ref, packed_ref, unit_ref):
    top = jnp.zeros((8, 128), jnp.float32)
    for block in range(TABLE // 128):
        top = jnp.maximum(top, jnp.abs(table_ref[:, block * 128 : block * 128 + 128]))
    top = jnp.maximum(jnp.max(top, keepdims=True), 1e-30)
    unit_ref[...] = jnp.broadcast_to(top * (1.0 / 32767.0), (8, 128))
    scale = 32767.0 / top

    def whole(values):
        return (values * scale + 32768.5).astype(jnp.int32) - 32768

    for block in range(TABLE // 256):
        low = table_ref[:, block * 128 : block * 128 + 128]
        high = table_ref[:, TABLE // 2 + block * 128 : TABLE // 2 + block * 128 + 128]
        packed_ref[:, block * 128 : block * 128 + 128] = (whole(high) << 16) | (whole(low) & 65535)
    for pair in range(TABLE // (2 * COLS)):
        start = pair * 2 * COLS
        rows = jnp.concatenate(
            [table_ref[:, start : start + COLS], table_ref[:, start + COLS : start + 2 * COLS]], axis=0
        )
        upper = rows.astype(jnp.bfloat16)
        split_ref[pair * 16 : pair * 16 + 16, :COLS] = upper
        split_ref[pair * 16 : pair * 16 + 16, COLS:] = (rows - upper.astype(jnp.float32)).astype(jnp.bfloat16)


def prepare(table):
    outs = [
        jax.ShapeDtypeStruct((8 * TABLE // COLS, 2 * COLS), jnp.bfloat16),
        jax.ShapeDtypeStruct((8, TABLE // 2), jnp.int32),
        jax.ShapeDtypeStruct((8, 128), jnp.float32),
    ]
    return call(prepare_kernel, outs, [table], [], far=(0,))


def choose(leaf, masks, first, count):
    if count == 1:
        return leaf(first)
    half = count // 2
    mask = masks[half.bit_length() - 1]
    return jnp.where(mask, choose(leaf, masks, first + half, half), choose(leaf, masks, first, half))


def tall(row):
    return jnp.broadcast_to(row, (16, 128)).astype(jnp.bfloat16)


def at_rows(index_ref, count, row, *values):
    index = tall(row)
    zero = jnp.zeros((16, 128), jnp.bfloat16)
    masks = [index_ref[at : at + 16, :] == index for at in range(0, count, 16)]
    return jnp.concatenate([jnp.where(mask, value, zero) for value in values for mask in masks], axis=0)


def weigh(coef, x, y, z):
    corner = lax.broadcasted_iota(jnp.int32, coef.shape, 0)
    weight_x = jnp.where((corner & 1) == 1, x, 1.0 - x)
    weight_y = jnp.where((corner & 2) == 2, y, 1.0 - y)
    weight_z = jnp.where((corner & 4) == 4, z, 1.0 - z)
    lsize = jnp.sum(weight_x * weight_y * weight_z * coef, axis=0, keepdims=True)
    return jnp.exp(-2.0 * lsize)


def lookup_kernel(asked_ref, split_ref, packed_ref, unit_ref, found_ref, turned_ref, result_ref, column_ref):
    for j in range(4):
        turned_ref[j * SLOTS : j * SLOTS + 128, :] = asked_ref[:, 0, j * 128 : j * 128 + 128].T
    tails = asked_ref[:, 0, 512:].T
    for j in range(4):
        turned_ref[j * SLOTS + 128 : (j + 1) * SLOTS, :] = tails[j * 8 : j * 8 + 8]
    column_ref[...] = lax.broadcasted_iota(jnp.int32, (COLS, 128), 0).astype(jnp.float32).astype(jnp.bfloat16)

    def step(i, carry):
        unit = unit_ref[...]
        for r in range(GATHERED):
            at = i * GATHERED + r
            ids, x, y, z = (turned_ref[pl.ds(j * SLOTS + at, 1), :] for j in range(4))
            own = jnp.broadcast_to(ids.astype(jnp.int32), (8, 128))
            lane = own & 127
            masks = [(own & (128 << bit)) != 0 for bit in range(6)]

            def leaf(block):
                return jnp.take_along_axis(packed_ref[:, block * 128 : block * 128 + 128], lane, axis=1)

            word = choose(leaf, masks, 0, 64)
            whole = jnp.where((own & (TABLE // 2)) != 0, word, word << 16) >> 16
            coef = whole.astype(jnp.float32) * unit
            result_ref[pl.ds(at, 1), :] = weigh(coef, x, y, z)

        for pair in range(PAIRS):
            at = ROUNDS * GATHERED + (i * PAIRS + pair) * 2
            pair_ids, px, py, pz = (
                jnp.concatenate([turned_ref[pl.ds(j * SLOTS + at + k, 1), :] for k in range(2)], axis=1)
                for j in range(4)
            )
            pair_ids = pair_ids.astype(jnp.int32)
            column = (pair_ids & (COLS - 1)).astype(jnp.float32)
            ones = jnp.ones((16, 128), jnp.bfloat16)
            chosen = jnp.concatenate(
                [at_rows(column_ref, COLS, column[:, k * 128 : k * 128 + 128], ones) for k in range(2)], axis=1
            )
            picked = jnp.dot(split_ref[:, :COLS], chosen, preferred_element_type=jnp.float32) + jnp.dot(
                split_ref[:, COLS:], chosen, preferred_element_type=jnp.float32
            )
            own = jnp.broadcast_to(pair_ids, (8, 256))
            masks = [(own & (COLS << bit)) != 0 for bit in range(6)]
            coef = choose(lambda row: picked[row * 8 : row * 8 + 8], masks, 0, 64)
            value = weigh(coef, px, py, pz)
            for k in range(2):
                result_ref[pl.ds(at + k, 1), :] = value[:, k * 128 : k * 128 + 128]
        return carry

    lax.fori_loop(0, ROUNDS, step, 0)
    found_ref[:, 0, :128] = result_ref[:128, :].T
    found_ref[:, 0, 128:] = result_ref[128:, :].T


def lookup(asked, prepared):
    scratch = [
        pltpu.VMEM((4 * SLOTS, 128), jnp.float32),
        pltpu.VMEM((SLOTS, 128), jnp.float32),
        pltpu.VMEM((COLS, 128), jnp.bfloat16),
    ]
    out = jax.ShapeDtypeStruct((SRC, 1, SLOTS), jnp.float32)
    return call(lookup_kernel, out, [asked, *prepared], scratch)


def place_kernel(found_ref, point_ref, size_ref, value_ref, row_ref, lane_ref, at_ref):
    value_ref[:128, :] = found_ref[:, 0, :128].T
    value_ref[128:, :] = found_ref[:, 0, 128:].T
    point = point_ref[...]
    line = (point * 10923) >> 21
    qx = point - line * 192
    qz = (line * 43) >> 8
    qy = line - qz * 6
    ex = (qx * 171) >> 9
    jx = qx - ex * 3
    ey = (qy * 11) >> 5
    jy = qy - ey * 3
    ez = (qz * 11) >> 5
    jz = qz - ez * 3
    row_ref[...] = (((jz * 3 + jy) * 3 + jx) * 2 + ey).astype(jnp.float32)
    lane_ref[...] = (ez * 64 + ex).astype(jnp.float32)
    at_ref[...] = lax.broadcasted_iota(jnp.int32, (128, 128), 0).astype(jnp.float32).astype(jnp.bfloat16)
    ones = jnp.ones((16, 128), jnp.bfloat16)

    def step(i, total):
        values = value_ref[i * 8 : i * 8 + 8, :]
        rows = row_ref[i * 8 : i * 8 + 8, :]
        lanes = lane_ref[i * 8 : i * 8 + 8, :]
        left, right = [], []
        for r in range(8):
            value = values[r : r + 1]
            upper = tall(value)
            lower = tall(value - upper[:1].astype(jnp.float32))
            left.append(at_rows(at_ref, 64, rows[r : r + 1], upper, lower))
            right.append(at_rows(at_ref, 128, lanes[r : r + 1], ones))
        left = jnp.concatenate(left, axis=1)
        right = jnp.concatenate(right, axis=1)
        return total + lax.dot_general(left, right, (((1,), (1,)), ((), ())), preferred_element_type=jnp.float32)

    total = jnp.zeros((128, 128), jnp.float32)
    for i in range(SLOTS // 8):
        total = step(i, total)
    size_ref[...] = total[:56] + total[64:120]


def place(found, point):
    scratch = [pltpu.VMEM((SLOTS, 128), jnp.float32) for _ in range(3)] + [pltpu.VMEM((128, 128), jnp.bfloat16)]
    return call(place_kernel, jax.ShapeDtypeStruct((56, 128), jnp.float32), [found, point], scratch, far=(1,))


HALF_GAP = float(np.sqrt(0.15))
OUTER, MIDDLE = 5.0 / 18.0, 8.0 / 18.0


def field_pieces(refs):
    return {(z, y): (refs[y], (z % 3) * 48) for z in (-1, 0, 1) for y in (-1, 0, 1)}


def size_pieces(refs):
    own, z_low, y_low, corner = refs
    return {(0, 0): own, (-1, 0): z_low, (0, -1): y_low, (-1, -1): corner}


def lane_index():
    return lax.broadcasted_iota(jnp.int32, (8, 128), 1)


def x_up(v):
    return jnp.where((lane_index() & 63) == 63, pltpu.roll(v, 63, 1), pltpu.roll(v, 127, 1))


def x_down(v):
    return jnp.where((lane_index() & 63) == 0, pltpu.roll(v, 65, 1), pltpu.roll(v, 1, 1))


def z_down(v):
    turned = pltpu.roll(v, 64, 1)
    return jnp.where(lane_index() < 64, pltpu.roll(turned, 4, 0), turned)


def y_down(v):
    return pltpu.roll(v, 1, 0)


def spread(low, mid, high, slopes=True, values=True):
    bend = (low + high) - 2.0 * mid
    rise = high - low
    vals = slps = None
    if values:
        centre = mid + (2.0 * HALF_GAP * HALF_GAP) * bend
        lean = HALF_GAP * rise
        vals = (centre - lean, mid, centre + lean)
    if slopes:
        change = (4.0 * HALF_GAP) * bend
        slps = (rise - change, rise, rise + change)
    return vals, slps


def collect(vals, slps):
    bend = rise = mid = None
    if vals is not None:
        outer = vals[0] + vals[2]
        bend = (2.0 * HALF_GAP * HALF_GAP) * outer
        rise = HALF_GAP * (vals[2] - vals[0])
        mid = outer + vals[1]
    if slps is not None:
        slope_bend = (4.0 * HALF_GAP) * (slps[2] - slps[0])
        slope_rise = (slps[0] + slps[2]) + slps[1]
        bend = slope_bend if bend is None else bend + slope_bend
        rise = slope_rise if rise is None else rise + slope_rise
    twice = -2.0 * bend
    return bend - rise, twice if mid is None else mid + twice, bend + rise


def at_point(c, k, jz, jy, jx):
    row = (((jz * 3 + jy) * 3 + jx) * 9 + k) * 8
    return pl.ds(row + c * 24, 8)


def forward(local, out_ref, at):
    along_z = [[spread(local(0, y, x), local(1, y, x), local(2, y, x)) for x in range(3)] for y in range(3)]
    for jz in range(3):
        value = [[along_z[y][x][0][jz] for x in range(3)] for y in range(3)]
        slope = [[along_z[y][x][1][jz] for x in range(3)] for y in range(3)]
        plain = [spread(value[0][x], value[1][x], value[2][x]) for x in range(3)]
        steep = [spread(slope[0][x], slope[1][x], slope[2][x], slopes=False)[0] for x in range(3)]
        for jy in range(3):
            dx = spread(*(plain[x][0][jy] for x in range(3)), values=False)[1]
            dy = spread(*(plain[x][1][jy] for x in range(3)), slopes=False)[0]
            dz = spread(*(steep[x][jy] for x in range(3)), slopes=False)[0]
            for jx in range(3):
                for k, part in enumerate((dx, dy, dz)):
                    out_ref[at(k, jz, jy, jx), :] = part[jx]


def backward(c, from_ref, out_ref):
    planes = []
    for jz in range(3):
        lines = []
        for jy in range(3):
            dx, dy, dz = (
                tuple(from_ref[at_point(c, k, jz, jy, jx), :] for jx in range(3)) for k in range(3)
            )
            lines.append((collect(None, dx), collect(dy, None), collect(dz, None)))
        value = [
            collect(tuple(lines[jy][0][x] for jy in range(3)), tuple(lines[jy][1][x] for jy in range(3)))
            for x in range(3)
        ]
        slope = [collect(tuple(lines[jy][2][x] for jy in range(3)), None) for x in range(3)]
        planes.append((value, slope))
    whole = [
        [
            collect(
                tuple(planes[jz][0][x][y] for jz in range(3)), tuple(planes[jz][1][x][y] for jz in range(3))
            )
            for x in range(3)
        ]
        for y in range(3)
    ]
    folded_x = [[(whole[y][0][z] + x_down(whole[y][2][z]), whole[y][1][z]) for z in range(3)] for y in range(3)]
    for x in range(2):
        folded = [(folded_x[0][z][x] + y_down(folded_x[2][z][x]), folded_x[1][z][x]) for z in range(3)]
        for y in range(2):
            for z, node in enumerate((folded[0][y] + z_down(folded[2][y]), folded[1][y])):
                row = (z * 4 + y * 2 + x) * 8
                out_ref[pl.ds(row + c * 64, 8), :] = node


def symmetric(build):
    upper = {(k, l): build(k, l) for k in range(3) for l in range(k, 3)}
    return {(k, l): upper[min(k, l), max(k, l)] for k in range(3) for l in range(3)}


def inner(a, b):
    square = (a[0, 0] * b[0, 0] + a[1, 1] * b[1, 1]) + a[2, 2] * b[2, 2]
    cross = (a[0, 1] * b[0, 1] + a[0, 2] * b[0, 2]) + a[1, 2] * b[1, 2]
    return square + 2.0 * cross


def column_dot(a, b, k, l):
    return (a[0][k] * b[0][l] + a[1][k] * b[1][l]) + a[2][k] * b[2][l]


def load_tensor(ref, jz, jy, jx):
    tensor = [[ref[at_point(c, k, jz, jy, jx), :] for k in range(3)] for c in range(3)]
    return tensor


def jacobian_at(ref, jz, jy, jx):
    tensor = load_tensor(ref, jz, jy, jx)
    return [[tensor[c][k] + 1.0 if c == k else tensor[c][k] for k in range(3)] for c in range(3)]


def strain_of(jac, size):
    return symmetric(lambda k, l: column_dot(jac, jac, k, l) * size - (1.0 if k == l else 0.0))


def weight_at(jz, jy, jx):
    along_z = MIDDLE if jz == 1 else OUTER
    return along_z * ((MIDDLE if jy == 1 else OUTER) * (MIDDLE if jx == 1 else OUTER))


def newton_step(totals):
    _, linear, quadratic, cubic, quartic, floor = (jnp.broadcast_to(totals[:, i : i + 1], (8, 128)) for i in range(6))
    step = jnp.zeros_like(linear)
    for _ in range(4):
        slope = linear + step * (2.0 * quadratic + step * (3.0 * cubic + step * 4.0 * quartic))
        curvature = 2.0 * quadratic + step * (6.0 * cubic + step * 12.0 * quartic)
        step = step - slope / jnp.maximum(curvature, floor + 1e-06)
    return step


def add_up(terms_ref):
    return jnp.sum(terms_ref[...], axis=0, keepdims=True)


def ring(pieces, count, out_ref, out_at, z_shift, y_shift):
    low = lax.broadcasted_iota(jnp.int32, (count, 128), 1) < 64
    places = ((-1, 1), (0, 0), (0, 1), (1, 0)) if y_shift else ((-1, 0), (-1, 1), (0, 0), (0, 1))
    for upper in range(2):
        for y, (piece_y, row) in enumerate(places):

            def piece(z):
                ref, at = pieces[z, piece_y]
                return ref[pl.ds(at + row, count, stride=2), :]

            value = piece(-upper)
            if z_shift:
                value = jnp.where(low, pltpu.roll(value, 64, 1), pltpu.roll(piece(1 - upper), 64, 1))
            out_ref[pl.ds(out_at + upper * 4 + y, count, stride=8), :] = value


def each(body):
    for i in range(3):
        body(i)


def jacobians(field, nodes_ref, jac_ref):
    for z_shift in range(2):
        for y_shift in range(2):
            ring(field, 24, nodes_ref, (z_shift * 2 + y_shift) * 192, z_shift, y_shift)

    def known(c):
        def local(z, y, x):
            row = ((z == 2) * 2 + (y == 2)) * 192 + ((z % 2) * 4 + (y % 2) * 2 + x % 2) * 8
            value = nodes_ref[pl.ds(row + c * 64, 8), :]
            return x_up(value) if x == 2 else value

        return local

    each(lambda c: forward(known(c), jac_ref, functools.partial(at_point, c)))


def descend(size_ref, jac_ref, part_ref, turn_ref, move_ref):
    def size_at(jz, jy, jx):
        return size_ref[pl.ds((jz * 9 + jy * 3 + jx) * 8, 8), :]

    turn_ref[192:, :] = jnp.zeros((64, 128), jnp.float32)

    def stress(jz):
        for jy in range(3):
            for jx in range(3):
                jac = jacobian_at(jac_ref, jz, jy, jx)
                size = size_at(jz, jy, jx)
                strain = strain_of(jac, size)
                scale = size * (-4.0 * weight_at(jz, jy, jx))
                for c in range(3):
                    for k in range(3):
                        part = (strain[k, 0] * jac[c][0] + strain[k, 1] * jac[c][1]) + strain[k, 2] * jac[c][2]
                        part_ref[at_point(c, k, jz, jy, jx), :] = part * scale

    each(stress)
    each(lambda c: backward(c, part_ref, turn_ref))
    for row in range(2):
        move_ref[pl.ds(row, 24, stride=2), :] = turn_ref[pl.ds(row + 2, 24, stride=8), :]


def line_sums(size_ref, jac_ref, part_ref, turn_ref, terms_out):
    def packed(node, upper, shift):
        rows = [
            turn_ref[pl.ds(node * 8 + upper * 4 + 1 + shift + ey, 4, stride=64), :] for ey in range(2)
        ]
        return jnp.concatenate(rows, axis=0)

    def sought(z, y, x):
        node = (z % 2) * 4 + (y % 2) * 2 + x % 2
        shift = y // 2
        value = packed(node, 0, shift)
        if z == 2:
            value = pltpu.roll(value, 64, 1)
        else:
            value = jnp.where(lane_index() < 64, value, packed(node, 1, shift))
        return x_up(value) if x == 2 else value

    forward(sought, part_ref, lambda k, jz, jy, jx: pl.ds(((jz * 9 + jy * 3 + jx) * 3 + k) * 8, 8))

    def middle(ref, at, stride):
        return jnp.where(lane_index() < 64, ref[pl.ds(at, 8, stride=stride), :], ref[pl.ds(at + 4, 8, stride=stride), :])

    sub = lax.broadcasted_iota(jnp.int32, (8, 128), 0)
    sums = [jnp.zeros((8, 128), jnp.float32) for _ in range(6)]
    for start, fresh in ((0, 0), (8, 8), (16, 16), (19, 24)):
        weight = jnp.zeros((8, 128), jnp.float32)
        for i in range(fresh - start, 8):
            point = start + i
            parts = [MIDDLE if (point // by) % 3 == 1 else OUTER for by in (9, 3, 1)]
            weight = jnp.where(sub == i, (parts[0] * parts[1]) * parts[2], weight)
        for ey in range(2):
            jac = [
                [middle(jac_ref, (start * 9 + c * 3 + k) * 8 + 1 + ey, 72) for k in range(3)]
                for c in range(3)
            ]
            jac = [[jac[c][k] + 1.0 if c == k else jac[c][k] for k in range(3)] for c in range(3)]
            motion = [
                [part_ref[pl.ds((start * 3 + k) * 8 + ey * 4 + c, 8, stride=24), :] for k in range(3)]
                for c in range(3)
            ]
            size = middle(size_ref, start * 8 + 1 + ey, 8)
            zero = strain_of(jac, size)
            one = symmetric(lambda k, l: (column_dot(jac, motion, k, l) + column_dot(motion, jac, k, l)) * size)
            two = symmetric(lambda k, l: column_dot(motion, motion, k, l) * size)
            pairs = ((zero, zero), (zero, one), (zero, two), (one, two), (two, two), (one, one))
            sums = [total + weight * inner(*pair) for total, pair in zip(sums, pairs)]
    zz, zo, zt, ot, tt, gn = (jnp.sum(total, keepdims=True) for total in sums)
    lane = lax.broadcasted_iota(jnp.int32, (1, 128), 1)
    terms = jnp.zeros((1, 128), jnp.float32)
    for i, term in enumerate((zz, 2.0 * zo, gn + 2.0 * zt, 2.0 * ot, tt, gn)):
        terms = jnp.where(lane == i, term, terms)
    terms_out[...] = jnp.broadcast_to(terms, (SRC, 128))


def jacobian_kernel(*refs):
    jacobians(field_pieces(refs[:3]), refs[4], refs[3])


def descent_kernel(jac_ref, own, z_low, y_low, corner, move_ref, turn_ref, size_ref, part_ref):
    sizes = {at: (ref, 0) for at, ref in size_pieces([own, z_low, y_low, corner]).items()}
    ring(sizes, 27, size_ref, 0, 0, 0)
    descend(size_ref, jac_ref, part_ref, turn_ref, move_ref)


def line_kernel(jac_ref, turn_ref, size_ref, terms_out, part_ref):
    line_sums(size_ref, jac_ref, part_ref, turn_ref, terms_out)


def second_kernel(before_ref, drift_ref, size_ref, terms_in, move_ref, terms_out, step_ref, jac_ref, part_ref, turn_ref):
    step = newton_step(add_up(terms_in))
    step_ref[...] = step
    for row in range(0, JAC_ROWS, 8):
        rows = slice(row, row + 8)
        jac_ref[rows, :] = before_ref[rows, :] + step * drift_ref[rows, :]
    descend(size_ref, jac_ref, part_ref, turn_ref, move_ref)
    line_sums(size_ref, jac_ref, part_ref, turn_ref, terms_out)


NODE = jax.ShapeDtypeStruct((48, 128), jnp.float32)
TERMS = jax.ShapeDtypeStruct((SRC, 128), jnp.float32)
NODES_ROWS, JAC_ROWS, TURN_ROWS, SIZE_ROWS = 4 * 192, 243 * 8, 32 * 8, 27 * 8


def rows_of(count):
    return jax.ShapeDtypeStruct((count, 128), jnp.float32)


def scratch_of(count):
    return pltpu.VMEM((count, 128), jnp.float32)


def all_jacobians(field):
    return call(jacobian_kernel, rows_of(JAC_ROWS), field, [scratch_of(NODES_ROWS)])


def first_descent(jac, sizes):
    outs = [NODE, rows_of(TURN_ROWS), rows_of(SIZE_ROWS)]
    return call(descent_kernel, outs, [jac, *sizes], [scratch_of(JAC_ROWS)])


def first_line(jac, turn, size):
    return call(line_kernel, TERMS, [jac, turn, size], [scratch_of(81 * 8)])


def second_pass(jac, drift, size, terms):
    scratch = [scratch_of(rows) for rows in (JAC_ROWS, JAC_ROWS, TURN_ROWS)]
    return call(second_kernel, [NODE, TERMS, rows_of(8)], [jac, drift, size, terms], scratch)


def interleave(back):
    row = lax.broadcasted_iota(jnp.int32, (128, 128), 0)
    col = lax.broadcasted_iota(jnp.int32, (128, 128), 1)
    if back:
        row, col = col, row
    return (col == (row & 1) * 64 + (row >> 1)).astype(jnp.float32)


def split_kernel(nodes_ref, out_ref, rows_ref):
    rows = nodes_ref[...].reshape(48, 128)
    rows_ref[...] = jnp.dot(rows, interleave(False), precision=lax.Precision.HIGHEST, preferred_element_type=jnp.float32)
    low = lax.broadcasted_iota(jnp.int32, (1, 128), 1) < 64
    for c in range(3):
        for az in range(2):
            for ay in range(2):
                for ey in range(2):
                    at = c * 16 + az * 4 + ey * 2 + ay
                    first = rows_ref[at : at + 1, :]
                    second = rows_ref[at + 8 : at + 9, :]
                    to = (c * 8 + az * 4 + ay * 2) * 2 + ey
                    out_ref[to : to + 1, :] = jnp.where(low, first, pltpu.roll(second, 64, 1))
                    out_ref[to + 2 : to + 3, :] = jnp.where(low, pltpu.roll(first, 64, 1), second)


def split_nodes(nodes):
    out = jax.ShapeDtypeStruct((48, 128), jnp.float32)
    return call(split_kernel, out, [nodes], [pltpu.VMEM((48, 128), jnp.float32)], far=(0,))


def join_kernel(count, *refs):
    rows_ref = refs[-1]
    low = lax.broadcasted_iota(jnp.int32, (1, 128), 1) < 64
    for i, new_ref in enumerate(refs[:count]):
        for c in range(3):
            for az in range(2):
                for ay in range(2):
                    for ey in range(2):
                        at = (c * 8 + az * 4 + ay * 2) * 2 + ey
                        even = new_ref[at : at + 1, :]
                        odd = new_ref[at + 2 : at + 3, :]
                        to = i * 48 + c * 16 + az * 4 + ey * 2 + ay
                        rows_ref[to : to + 1, :] = jnp.where(low, even, pltpu.roll(odd, 64, 1))
                        rows_ref[to + 8 : to + 9, :] = jnp.where(low, pltpu.roll(even, 64, 1), odd)
    rows = jnp.dot(
        rows_ref[...], interleave(True), precision=lax.Precision.HIGHEST, preferred_element_type=jnp.float32
    )
    for i, out_ref in enumerate(refs[count : 2 * count]):
        out_ref[...] = rows[i * 48 : i * 48 + 48].reshape(3, 4, 4, 128)


def join_nodes(*nodes):
    outs = [jax.ShapeDtypeStruct((3, 4, 4, 128), jnp.float32) for _ in nodes]
    kernel = functools.partial(join_kernel, len(nodes))
    return call(kernel, outs, list(nodes), [scratch_of(48 * len(nodes))])


def finish_kernel(own_ref, first_move_ref, last_move_ref, step_ref, first_ref, second_ref, out_ref, coeff_ref):
    second = add_up(second_ref)
    step = newton_step(second)[:4]
    first_step = step_ref[:4, :]
    for c in range(3):
        for z in range(4):
            field = own_ref[c, z] + first_step * first_move_ref[c, z]
            out_ref[c, z] = field + step * last_move_ref[c, z]
    coeff_ref[0:1, :] = add_up(first_ref)[:, :5] * (1.0 / 32768.0)
    coeff_ref[1:2, :] = second[:, :5] * (1.0 / 32768.0)


def finish(*args):
    outs = [jax.ShapeDtypeStruct((3, 4, 4, 128), jnp.float32), jax.ShapeDtypeStruct((2, 5), jnp.float32)]
    return call(finish_kernel, outs, list(args), [], last=True)


def pack_kernel(elem_ref, coord_ref, out_ref):
    parts = [elem_ref[...].astype(jnp.float32)] + [coord_ref[j] for j in range(3)]
    for j, part in enumerate(parts):
        out_ref[:, 0, j * 128 : j * 128 + 128] = part[:128].T
    tails = jnp.concatenate([part[128:] for part in parts] + [jnp.zeros((96, 128), jnp.float32)], axis=0)
    out_ref[:, 0, 512:] = tails.T


def pack(elem, coord):
    return call(pack_kernel, jax.ShapeDtypeStruct((SRC, 1, 640), jnp.float32), [elem, coord], [], far=(0, 1))


def exchange(values):
    return lax.all_to_all(values, ("mesh", "bg"), split_axis=0, concat_axis=0, tiled=True)


def moved(values, axis, by):
    count = lax.axis_size(axis)
    return lax.ppermute(values, axis, [(i, (i - by) % count) for i in range(count)])


def along_mesh(block):
    return jnp.concatenate([block, moved(block, "mesh", 1), moved(block, "mesh", -1)], axis=0)


def from_below(block):
    mesh, bg = lax.axis_size("mesh"), lax.axis_size("bg")
    steps = [
        (z * bg + y, ((z + 1) % mesh) * bg + (y + 1) % bg) for z in range(mesh) for y in range(bg)
    ]
    return [block, moved(block, "mesh", -1), moved(block, "bg", -1), lax.ppermute(block, ("mesh", "bg"), steps)]


def along_bg(rows):
    return [rows, moved(rows, "bg", 1), moved(rows, "bg", -1)]


def shards(displacement, bg_coef, query_elem, query_point, query_coord):
    asked = exchange(pack(query_elem[0].T, query_coord[0].transpose(1, 2, 0)))
    own = split_nodes(displacement)
    rows = along_mesh(own)
    asked, prepared = lax.optimization_barrier((asked, prepare(bg_coef)))
    found = lookup(asked, prepared)
    found = exchange(found)
    field = along_bg(rows)
    sizes = place(found, query_point[0].T)
    sizes = from_below(sizes)
    jac = all_jacobians(field)
    move, turn, size = first_descent(jac, sizes)
    rows = along_mesh(move)
    terms = first_line(jac, turn, size)
    first_terms = exchange(terms)
    shift = along_bg(rows)
    drift = all_jacobians(shift)
    last_move, last_terms, step = second_pass(jac, drift, size, first_terms)
    last_terms = exchange(last_terms)
    nodes = join_nodes(own, move, last_move)
    return finish(*nodes, step, first_terms, last_terms)


def solution(mesh):
    in_specs = (
        P(None, "mesh", "bg", None),
        P(None, ("mesh", "bg")),
        P(("mesh", "bg"), None, None),
        P(("mesh", "bg"), None, None),
        P(("mesh", "bg"), None, None, None),
    )
    out_specs = (P(None, "mesh", "bg", None), P())
    return jax.shard_map(shards, mesh=mesh, in_specs=in_specs, out_specs=out_specs, check_vma=False)
```

```python
import functools

import jax
import jax.numpy as jnp
import numpy as np
from jax import lax
from jax.experimental import pallas as pl
from jax.experimental.pallas import tpu as pltpu
from jax.sharding import PartitionSpec as P

SRC = 128
SLOTS = 136
TABLE = 16384
COLS = 256


ROUNDS = 2
GATHERED = 34
PAIRS = 17


def in_vmem(count):
    return [pl.BlockSpec(memory_space=pltpu.VMEM) for _ in range(count)]


def call(kernel, outs, args, scratch, far=(), last=False):
    args = [a if i in far else pltpu.with_memory_space_constraint(a, pltpu.VMEM) for i, a in enumerate(args)]
    many = isinstance(outs, list)
    if not last:
        outs = [pltpu.VMEM(o.shape, o.dtype) for o in outs] if many else pltpu.VMEM(outs.shape, outs.dtype)
    return pl.pallas_call(
        kernel,
        out_shape=outs,
        in_specs=in_vmem(len(args)),
        out_specs=in_vmem(len(outs)) if many else in_vmem(1)[0],
        scratch_shapes=scratch,
    )(*args)


def prepare_kernel(table_ref, split_ref, packed_ref, unit_ref):
    top = jnp.zeros((8, 128), jnp.float32)
    for block in range(TABLE // 128):
        top = jnp.maximum(top, jnp.abs(table_ref[:, block * 128 : block * 128 + 128]))
    top = jnp.maximum(jnp.max(top, keepdims=True), 1e-30)
    unit_ref[...] = jnp.broadcast_to(top * (1.0 / 32767.0), (8, 128))
    scale = 32767.0 / top

    def whole(values):
        return (values * scale + 32768.5).astype(jnp.int32) - 32768

    for block in range(TABLE // 256):
        low = table_ref[:, block * 128 : block * 128 + 128]
        high = table_ref[:, TABLE // 2 + block * 128 : TABLE // 2 + block * 128 + 128]
        packed_ref[:, block * 128 : block * 128 + 128] = (whole(high) << 16) | (whole(low) & 65535)
    for pair in range(TABLE // (2 * COLS)):
        start = pair * 2 * COLS
        rows = jnp.concatenate(
            [table_ref[:, start : start + COLS], table_ref[:, start + COLS : start + 2 * COLS]], axis=0
        )
        upper = rows.astype(jnp.bfloat16)
        split_ref[pair * 16 : pair * 16 + 16, :COLS] = upper
        split_ref[pair * 16 : pair * 16 + 16, COLS:] = (rows - upper.astype(jnp.float32)).astype(jnp.bfloat16)


def prepare(table):
    outs = [
        jax.ShapeDtypeStruct((8 * TABLE // COLS, 2 * COLS), jnp.bfloat16),
        jax.ShapeDtypeStruct((8, TABLE // 2), jnp.int32),
        jax.ShapeDtypeStruct((8, 128), jnp.float32),
    ]
    return call(prepare_kernel, outs, [table], [], far=(0,))


def choose(leaf, masks, first, count):
    if count == 1:
        return leaf(first)
    half = count // 2
    mask = masks[half.bit_length() - 1]
    return jnp.where(mask, choose(leaf, masks, first + half, half), choose(leaf, masks, first, half))


def tall(row):
    return jnp.broadcast_to(row, (16, 128)).astype(jnp.bfloat16)


def at_rows(index_ref, count, row, *values):
    index = tall(row)
    zero = jnp.zeros((16, 128), jnp.bfloat16)
    masks = [index_ref[at : at + 16, :] == index for at in range(0, count, 16)]
    return jnp.concatenate([jnp.where(mask, value, zero) for value in values for mask in masks], axis=0)


def weigh(coef, x, y, z):
    corner = lax.broadcasted_iota(jnp.int32, coef.shape, 0)
    weight_x = jnp.where((corner & 1) == 1, x, 1.0 - x)
    weight_y = jnp.where((corner & 2) == 2, y, 1.0 - y)
    weight_z = jnp.where((corner & 4) == 4, z, 1.0 - z)
    lsize = jnp.sum(weight_x * weight_y * weight_z * coef, axis=0, keepdims=True)
    return jnp.exp(-2.0 * lsize)


def lookup_kernel(asked_ref, split_ref, packed_ref, unit_ref, found_ref, turned_ref, result_ref, column_ref):
    for j in range(4):
        turned_ref[j * SLOTS : j * SLOTS + 128, :] = asked_ref[:, 0, j * 128 : j * 128 + 128].T
    tails = asked_ref[:, 0, 512:].T
    for j in range(4):
        turned_ref[j * SLOTS + 128 : (j + 1) * SLOTS, :] = tails[j * 8 : j * 8 + 8]
    column_ref[...] = lax.broadcasted_iota(jnp.int32, (COLS, 128), 0).astype(jnp.float32).astype(jnp.bfloat16)

    def step(i, carry):
        unit = unit_ref[...]
        for r in range(GATHERED):
            at = i * GATHERED + r
            ids, x, y, z = (turned_ref[pl.ds(j * SLOTS + at, 1), :] for j in range(4))
            own = jnp.broadcast_to(ids.astype(jnp.int32), (8, 128))
            lane = own & 127
            masks = [(own & (128 << bit)) != 0 for bit in range(6)]

            def leaf(block):
                return jnp.take_along_axis(packed_ref[:, block * 128 : block * 128 + 128], lane, axis=1)

            word = choose(leaf, masks, 0, 64)
            whole = jnp.where((own & (TABLE // 2)) != 0, word, word << 16) >> 16
            coef = whole.astype(jnp.float32) * unit
            result_ref[pl.ds(at, 1), :] = weigh(coef, x, y, z)

        for pair in range(PAIRS):
            at = ROUNDS * GATHERED + (i * PAIRS + pair) * 2
            pair_ids, px, py, pz = (
                jnp.concatenate([turned_ref[pl.ds(j * SLOTS + at + k, 1), :] for k in range(2)], axis=1)
                for j in range(4)
            )
            pair_ids = pair_ids.astype(jnp.int32)
            column = (pair_ids & (COLS - 1)).astype(jnp.float32)
            ones = jnp.ones((16, 128), jnp.bfloat16)
            chosen = jnp.concatenate(
                [at_rows(column_ref, COLS, column[:, k * 128 : k * 128 + 128], ones) for k in range(2)], axis=1
            )
            picked = jnp.dot(split_ref[:, :COLS], chosen, preferred_element_type=jnp.float32) + jnp.dot(
                split_ref[:, COLS:], chosen, preferred_element_type=jnp.float32
            )
            own = jnp.broadcast_to(pair_ids, (8, 256))
            masks = [(own & (COLS << bit)) != 0 for bit in range(6)]
            coef = choose(lambda row: picked[row * 8 : row * 8 + 8], masks, 0, 64)
            value = weigh(coef, px, py, pz)
            for k in range(2):
                result_ref[pl.ds(at + k, 1), :] = value[:, k * 128 : k * 128 + 128]
        return carry

    lax.fori_loop(0, ROUNDS, step, 0)
    found_ref[:, 0, :128] = result_ref[:128, :].T
    found_ref[:, 0, 128:] = result_ref[128:, :].T


def lookup(asked, prepared):
    scratch = [
        pltpu.VMEM((4 * SLOTS, 128), jnp.float32),
        pltpu.VMEM((SLOTS, 128), jnp.float32),
        pltpu.VMEM((COLS, 128), jnp.bfloat16),
    ]
    out = jax.ShapeDtypeStruct((SRC, 1, SLOTS), jnp.float32)
    return call(lookup_kernel, out, [asked, *prepared], scratch)


def place_kernel(found_ref, point_ref, size_ref, value_ref, row_ref, lane_ref, at_ref):
    value_ref[:128, :] = found_ref[:, 0, :128].T
    value_ref[128:, :] = found_ref[:, 0, 128:].T
    point = point_ref[...]
    line = (point * 10923) >> 21
    qx = point - line * 192
    qz = (line * 43) >> 8
    qy = line - qz * 6
    ex = (qx * 171) >> 9
    jx = qx - ex * 3
    ey = (qy * 11) >> 5
    jy = qy - ey * 3
    ez = (qz * 11) >> 5
    jz = qz - ez * 3
    row_ref[...] = (((jz * 3 + jy) * 3 + jx) * 2 + ey).astype(jnp.float32)
    lane_ref[...] = (ez * 64 + ex).astype(jnp.float32)
    at_ref[...] = lax.broadcasted_iota(jnp.int32, (128, 128), 0).astype(jnp.float32).astype(jnp.bfloat16)
    ones = jnp.ones((16, 128), jnp.bfloat16)

    def step(i, total):
        values = value_ref[i * 8 : i * 8 + 8, :]
        rows = row_ref[i * 8 : i * 8 + 8, :]
        lanes = lane_ref[i * 8 : i * 8 + 8, :]
        left, right = [], []
        for r in range(8):
            value = values[r : r + 1]
            upper = tall(value)
            lower = tall(value - upper[:1].astype(jnp.float32))
            left.append(at_rows(at_ref, 64, rows[r : r + 1], upper, lower))
            right.append(at_rows(at_ref, 128, lanes[r : r + 1], ones))
        left = jnp.concatenate(left, axis=1)
        right = jnp.concatenate(right, axis=1)
        return total + lax.dot_general(left, right, (((1,), (1,)), ((), ())), preferred_element_type=jnp.float32)

    total = jnp.zeros((128, 128), jnp.float32)
    for i in range(SLOTS // 8):
        total = step(i, total)
    size_ref[...] = total[:56] + total[64:120]


def place(found, point):
    scratch = [pltpu.VMEM((SLOTS, 128), jnp.float32) for _ in range(3)] + [pltpu.VMEM((128, 128), jnp.bfloat16)]
    return call(place_kernel, jax.ShapeDtypeStruct((56, 128), jnp.float32), [found, point], scratch, far=(1,))


HALF_GAP = float(np.sqrt(0.15))
OUTER, MIDDLE = 5.0 / 18.0, 8.0 / 18.0


def shift_pieces(refs):
    return {(z, y): (refs[z], (y % 3) * 48) for z in (-1, 0, 1) for y in (-1, 0, 1)}


def field_pieces(refs):
    return {(z, y): (refs[y], (z % 3) * 48) for z in (-1, 0, 1) for y in (-1, 0, 1)}


def size_pieces(refs):
    own, z_low, y_low, corner = refs
    return {(0, 0): own, (-1, 0): z_low, (0, -1): y_low, (-1, -1): corner}


def lane_index():
    return lax.broadcasted_iota(jnp.int32, (8, 128), 1)


def x_up(v):
    return jnp.where((lane_index() & 63) == 63, pltpu.roll(v, 63, 1), pltpu.roll(v, 127, 1))


def x_down(v):
    return jnp.where((lane_index() & 63) == 0, pltpu.roll(v, 65, 1), pltpu.roll(v, 1, 1))


def z_down(v):
    turned = pltpu.roll(v, 64, 1)
    return jnp.where(lane_index() < 64, pltpu.roll(turned, 4, 0), turned)


def y_down(v):
    return pltpu.roll(v, 1, 0)


def spread(low, mid, high, slopes=True, values=True):
    bend = (low + high) - 2.0 * mid
    rise = high - low
    vals = slps = None
    if values:
        centre = mid + (2.0 * HALF_GAP * HALF_GAP) * bend
        lean = HALF_GAP * rise
        vals = (centre - lean, mid, centre + lean)
    if slopes:
        change = (4.0 * HALF_GAP) * bend
        slps = (rise - change, rise, rise + change)
    return vals, slps


def collect(vals, slps):
    bend = rise = mid = None
    if vals is not None:
        outer = vals[0] + vals[2]
        bend = (2.0 * HALF_GAP * HALF_GAP) * outer
        rise = HALF_GAP * (vals[2] - vals[0])
        mid = outer + vals[1]
    if slps is not None:
        slope_bend = (4.0 * HALF_GAP) * (slps[2] - slps[0])
        slope_rise = (slps[0] + slps[2]) + slps[1]
        bend = slope_bend if bend is None else bend + slope_bend
        rise = slope_rise if rise is None else rise + slope_rise
    twice = -2.0 * bend
    return bend - rise, twice if mid is None else mid + twice, bend + rise


def at_point(c, k, jz, jy, jx):
    row = (((jz * 3 + jy) * 3 + jx) * 9 + k) * 8
    return pl.ds(row + c * 24, 8)


def forward(local, out_ref, at):
    along_z = [[spread(local(0, y, x), local(1, y, x), local(2, y, x)) for x in range(3)] for y in range(3)]
    for jz in range(3):
        value = [[along_z[y][x][0][jz] for x in range(3)] for y in range(3)]
        slope = [[along_z[y][x][1][jz] for x in range(3)] for y in range(3)]
        plain = [spread(value[0][x], value[1][x], value[2][x]) for x in range(3)]
        steep = [spread(slope[0][x], slope[1][x], slope[2][x], slopes=False)[0] for x in range(3)]
        for jy in range(3):
            dx = spread(*(plain[x][0][jy] for x in range(3)), values=False)[1]
            dy = spread(*(plain[x][1][jy] for x in range(3)), slopes=False)[0]
            dz = spread(*(steep[x][jy] for x in range(3)), slopes=False)[0]
            for jx in range(3):
                for k, part in enumerate((dx, dy, dz)):
                    out_ref[at(k, jz, jy, jx), :] = part[jx]


def backward(c, from_ref, out_ref):
    planes = []
    for jz in range(3):
        lines = []
        for jy in range(3):
            dx, dy, dz = (
                tuple(from_ref[at_point(c, k, jz, jy, jx), :] for jx in range(3)) for k in range(3)
            )
            lines.append((collect(None, dx), collect(dy, None), collect(dz, None)))
        value = [
            collect(tuple(lines[jy][0][x] for jy in range(3)), tuple(lines[jy][1][x] for jy in range(3)))
            for x in range(3)
        ]
        slope = [collect(tuple(lines[jy][2][x] for jy in range(3)), None) for x in range(3)]
        planes.append((value, slope))
    whole = [
        [
            collect(
                tuple(planes[jz][0][x][y] for jz in range(3)), tuple(planes[jz][1][x][y] for jz in range(3))
            )
            for x in range(3)
        ]
        for y in range(3)
    ]
    folded_x = [[(whole[y][0][z] + x_down(whole[y][2][z]), whole[y][1][z]) for z in range(3)] for y in range(3)]
    for x in range(2):
        folded = [(folded_x[0][z][x] + y_down(folded_x[2][z][x]), folded_x[1][z][x]) for z in range(3)]
        for y in range(2):
            for z, node in enumerate((folded[0][y] + z_down(folded[2][y]), folded[1][y])):
                row = (z * 4 + y * 2 + x) * 8
                out_ref[pl.ds(row + c * 64, 8), :] = node


def symmetric(build):
    upper = {(k, l): build(k, l) for k in range(3) for l in range(k, 3)}
    return {(k, l): upper[min(k, l), max(k, l)] for k in range(3) for l in range(3)}


def inner(a, b):
    square = (a[0, 0] * b[0, 0] + a[1, 1] * b[1, 1]) + a[2, 2] * b[2, 2]
    cross = (a[0, 1] * b[0, 1] + a[0, 2] * b[0, 2]) + a[1, 2] * b[1, 2]
    return square + 2.0 * cross


def column_dot(a, b, k, l):
    return (a[0][k] * b[0][l] + a[1][k] * b[1][l]) + a[2][k] * b[2][l]


def load_tensor(ref, jz, jy, jx):
    tensor = [[ref[at_point(c, k, jz, jy, jx), :] for k in range(3)] for c in range(3)]
    return tensor


def jacobian_at(ref, jz, jy, jx):
    tensor = load_tensor(ref, jz, jy, jx)
    return [[tensor[c][k] + 1.0 if c == k else tensor[c][k] for k in range(3)] for c in range(3)]


def strain_of(jac, size):
    return symmetric(lambda k, l: column_dot(jac, jac, k, l) * size - (1.0 if k == l else 0.0))


def weight_at(jz, jy, jx):
    along_z = MIDDLE if jz == 1 else OUTER
    return along_z * ((MIDDLE if jy == 1 else OUTER) * (MIDDLE if jx == 1 else OUTER))


def newton_step(totals):
    _, linear, quadratic, cubic, quartic, floor = (jnp.broadcast_to(totals[:, i : i + 1], (8, 128)) for i in range(6))
    step = jnp.zeros_like(linear)
    for _ in range(4):
        slope = linear + step * (2.0 * quadratic + step * (3.0 * cubic + step * 4.0 * quartic))
        curvature = 2.0 * quadratic + step * (6.0 * cubic + step * 12.0 * quartic)
        step = step - slope / jnp.maximum(curvature, floor + 1e-06)
    return step


def add_up(terms_ref):
    return jnp.sum(terms_ref[...], axis=0, keepdims=True)


def ring(pieces, count, out_ref, out_at, z_shift, y_shift):
    low = lax.broadcasted_iota(jnp.int32, (count, 128), 1) < 64
    places = ((-1, 1), (0, 0), (0, 1), (1, 0)) if y_shift else ((-1, 0), (-1, 1), (0, 0), (0, 1))
    for upper in range(2):
        for y, (piece_y, row) in enumerate(places):

            def piece(z):
                ref, at = pieces[z, piece_y]
                return ref[pl.ds(at + row, count, stride=2), :]

            value = piece(-upper)
            if z_shift:
                value = jnp.where(low, pltpu.roll(value, 64, 1), pltpu.roll(piece(1 - upper), 64, 1))
            out_ref[pl.ds(out_at + upper * 4 + y, count, stride=8), :] = value


def each(body):
    for i in range(3):
        body(i)


def jacobians(field, nodes_ref, jac_ref):
    for z_shift in range(2):
        for y_shift in range(2):
            ring(field, 24, nodes_ref, (z_shift * 2 + y_shift) * 192, z_shift, y_shift)

    def known(c):
        def local(z, y, x):
            row = ((z == 2) * 2 + (y == 2)) * 192 + ((z % 2) * 4 + (y % 2) * 2 + x % 2) * 8
            value = nodes_ref[pl.ds(row + c * 64, 8), :]
            return x_up(value) if x == 2 else value

        return local

    each(lambda c: forward(known(c), jac_ref, functools.partial(at_point, c)))


def descend(size_ref, jac_ref, part_ref, turn_ref, move_ref):
    def size_at(jz, jy, jx):
        return size_ref[pl.ds((jz * 9 + jy * 3 + jx) * 8, 8), :]

    turn_ref[192:, :] = jnp.zeros((64, 128), jnp.float32)

    def stress(jz):
        for jy in range(3):
            for jx in range(3):
                jac = jacobian_at(jac_ref, jz, jy, jx)
                size = size_at(jz, jy, jx)
                strain = strain_of(jac, size)
                scale = size * (-4.0 * weight_at(jz, jy, jx))
                for c in range(3):
                    for k in range(3):
                        part = (strain[k, 0] * jac[c][0] + strain[k, 1] * jac[c][1]) + strain[k, 2] * jac[c][2]
                        part_ref[at_point(c, k, jz, jy, jx), :] = part * scale

    each(stress)
    each(lambda c: backward(c, part_ref, turn_ref))
    for row in range(2):
        move_ref[pl.ds(row, 24, stride=2), :] = turn_ref[pl.ds(row + 2, 24, stride=8), :]


def line_sums(size_ref, jac_ref, part_ref, turn_ref, terms_out):
    def packed(node, upper, shift):
        rows = [
            turn_ref[pl.ds(node * 8 + upper * 4 + 1 + shift + ey, 4, stride=64), :] for ey in range(2)
        ]
        return jnp.concatenate(rows, axis=0)

    def sought(z, y, x):
        node = (z % 2) * 4 + (y % 2) * 2 + x % 2
        shift = y // 2
        value = packed(node, 0, shift)
        if z == 2:
            value = pltpu.roll(value, 64, 1)
        else:
            value = jnp.where(lane_index() < 64, value, packed(node, 1, shift))
        return x_up(value) if x == 2 else value

    forward(sought, part_ref, lambda k, jz, jy, jx: pl.ds(((jz * 9 + jy * 3 + jx) * 3 + k) * 8, 8))

    def middle(ref, at, stride):
        return jnp.where(lane_index() < 64, ref[pl.ds(at, 8, stride=stride), :], ref[pl.ds(at + 4, 8, stride=stride), :])

    sub = lax.broadcasted_iota(jnp.int32, (8, 128), 0)
    sums = [jnp.zeros((8, 128), jnp.float32) for _ in range(6)]
    for start, fresh in ((0, 0), (8, 8), (16, 16), (19, 24)):
        weight = jnp.zeros((8, 128), jnp.float32)
        for i in range(fresh - start, 8):
            point = start + i
            parts = [MIDDLE if (point // by) % 3 == 1 else OUTER for by in (9, 3, 1)]
            weight = jnp.where(sub == i, (parts[0] * parts[1]) * parts[2], weight)
        for ey in range(2):
            jac = [
                [middle(jac_ref, (start * 9 + c * 3 + k) * 8 + 1 + ey, 72) for k in range(3)]
                for c in range(3)
            ]
            jac = [[jac[c][k] + 1.0 if c == k else jac[c][k] for k in range(3)] for c in range(3)]
            motion = [
                [part_ref[pl.ds((start * 3 + k) * 8 + ey * 4 + c, 8, stride=24), :] for k in range(3)]
                for c in range(3)
            ]
            size = middle(size_ref, start * 8 + 1 + ey, 8)
            zero = strain_of(jac, size)
            one = symmetric(lambda k, l: (column_dot(jac, motion, k, l) + column_dot(motion, jac, k, l)) * size)
            two = symmetric(lambda k, l: column_dot(motion, motion, k, l) * size)
            pairs = ((zero, zero), (zero, one), (zero, two), (one, two), (two, two), (one, one))
            sums = [total + weight * inner(*pair) for total, pair in zip(sums, pairs)]
    zz, zo, zt, ot, tt, gn = (jnp.sum(total, keepdims=True) for total in sums)
    lane = lax.broadcasted_iota(jnp.int32, (1, 128), 1)
    terms = jnp.zeros((1, 128), jnp.float32)
    for i, term in enumerate((zz, 2.0 * zo, gn + 2.0 * zt, 2.0 * ot, tt, gn)):
        terms = jnp.where(lane == i, term, terms)
    terms_out[...] = jnp.broadcast_to(terms, (SRC, 128))


def jacobian_kernel(pieces, *refs):
    jacobians(pieces(refs[:3]), refs[4], refs[3])


def descent_kernel(jac_ref, own, z_low, y_low, corner, move_ref, turn_ref, size_ref, part_ref):
    sizes = {at: (ref, 0) for at, ref in size_pieces([own, z_low, y_low, corner]).items()}
    ring(sizes, 27, size_ref, 0, 0, 0)
    descend(size_ref, jac_ref, part_ref, turn_ref, move_ref)


def line_kernel(jac_ref, turn_ref, size_ref, terms_out, part_ref):
    line_sums(size_ref, jac_ref, part_ref, turn_ref, terms_out)


def second_kernel(before_ref, drift_ref, size_ref, terms_in, move_ref, terms_out, step_ref, jac_ref, part_ref, turn_ref):
    step = newton_step(add_up(terms_in))
    step_ref[...] = step
    for row in range(0, JAC_ROWS, 8):
        rows = slice(row, row + 8)
        jac_ref[rows, :] = before_ref[rows, :] + step * drift_ref[rows, :]
    descend(size_ref, jac_ref, part_ref, turn_ref, move_ref)
    line_sums(size_ref, jac_ref, part_ref, turn_ref, terms_out)


NODE = jax.ShapeDtypeStruct((48, 128), jnp.float32)
TERMS = jax.ShapeDtypeStruct((SRC, 128), jnp.float32)
NODES_ROWS, JAC_ROWS, TURN_ROWS, SIZE_ROWS = 4 * 192, 243 * 8, 32 * 8, 27 * 8


def rows_of(count):
    return jax.ShapeDtypeStruct((count, 128), jnp.float32)


def scratch_of(count):
    return pltpu.VMEM((count, 128), jnp.float32)


def all_jacobians(field, pieces):
    kernel = functools.partial(jacobian_kernel, pieces)
    return call(kernel, rows_of(JAC_ROWS), field, [scratch_of(NODES_ROWS)])


def first_descent(jac, sizes):
    outs = [NODE, rows_of(TURN_ROWS), rows_of(SIZE_ROWS)]
    return call(descent_kernel, outs, [jac, *sizes], [scratch_of(JAC_ROWS)])


def first_line(jac, turn, size):
    return call(line_kernel, TERMS, [jac, turn, size], [scratch_of(81 * 8)])


def second_pass(jac, drift, size, terms):
    scratch = [scratch_of(rows) for rows in (JAC_ROWS, JAC_ROWS, TURN_ROWS)]
    return call(second_kernel, [NODE, TERMS, rows_of(8)], [jac, drift, size, terms], scratch)


def interleave(back):
    row = lax.broadcasted_iota(jnp.int32, (128, 128), 0)
    col = lax.broadcasted_iota(jnp.int32, (128, 128), 1)
    if back:
        row, col = col, row
    return (col == (row & 1) * 64 + (row >> 1)).astype(jnp.float32)


def split_kernel(nodes_ref, out_ref, rows_ref):
    rows = nodes_ref[...].reshape(48, 128)
    rows_ref[...] = jnp.dot(rows, interleave(False), precision=lax.Precision.HIGHEST, preferred_element_type=jnp.float32)
    low = lax.broadcasted_iota(jnp.int32, (1, 128), 1) < 64
    for c in range(3):
        for az in range(2):
            for ay in range(2):
                for ey in range(2):
                    at = c * 16 + az * 4 + ey * 2 + ay
                    first = rows_ref[at : at + 1, :]
                    second = rows_ref[at + 8 : at + 9, :]
                    to = (c * 8 + az * 4 + ay * 2) * 2 + ey
                    out_ref[to : to + 1, :] = jnp.where(low, first, pltpu.roll(second, 64, 1))
                    out_ref[to + 2 : to + 3, :] = jnp.where(low, pltpu.roll(first, 64, 1), second)


def split_nodes(nodes):
    out = jax.ShapeDtypeStruct((48, 128), jnp.float32)
    return call(split_kernel, out, [nodes], [pltpu.VMEM((48, 128), jnp.float32)], far=(0,))


def join_kernel(count, *refs):
    rows_ref = refs[-1]
    low = lax.broadcasted_iota(jnp.int32, (1, 128), 1) < 64
    for i, new_ref in enumerate(refs[:count]):
        for c in range(3):
            for az in range(2):
                for ay in range(2):
                    for ey in range(2):
                        at = (c * 8 + az * 4 + ay * 2) * 2 + ey
                        even = new_ref[at : at + 1, :]
                        odd = new_ref[at + 2 : at + 3, :]
                        to = i * 48 + c * 16 + az * 4 + ey * 2 + ay
                        rows_ref[to : to + 1, :] = jnp.where(low, even, pltpu.roll(odd, 64, 1))
                        rows_ref[to + 8 : to + 9, :] = jnp.where(low, pltpu.roll(even, 64, 1), odd)
    rows = jnp.dot(
        rows_ref[...], interleave(True), precision=lax.Precision.HIGHEST, preferred_element_type=jnp.float32
    )
    for i, out_ref in enumerate(refs[count : 2 * count]):
        out_ref[...] = rows[i * 48 : i * 48 + 48].reshape(3, 4, 4, 128)


def join_nodes(*nodes):
    outs = [jax.ShapeDtypeStruct((3, 4, 4, 128), jnp.float32) for _ in nodes]
    kernel = functools.partial(join_kernel, len(nodes))
    return call(kernel, outs, list(nodes), [scratch_of(48 * len(nodes))])


def finish_kernel(own_ref, first_move_ref, last_move_ref, step_ref, first_ref, second_ref, out_ref, coeff_ref):
    second = add_up(second_ref)
    step = newton_step(second)[:4]
    first_step = step_ref[:4, :]
    for c in range(3):
        for z in range(4):
            field = own_ref[c, z] + first_step * first_move_ref[c, z]
            out_ref[c, z] = field + step * last_move_ref[c, z]
    coeff_ref[0:1, :] = add_up(first_ref)[:, :5] * (1.0 / 32768.0)
    coeff_ref[1:2, :] = second[:, :5] * (1.0 / 32768.0)


def finish(*args):
    outs = [jax.ShapeDtypeStruct((3, 4, 4, 128), jnp.float32), jax.ShapeDtypeStruct((2, 5), jnp.float32)]
    return call(finish_kernel, outs, list(args), [], last=True)


def pack_kernel(elem_ref, coord_ref, out_ref):
    parts = [elem_ref[...].astype(jnp.float32)] + [coord_ref[j] for j in range(3)]
    for j, part in enumerate(parts):
        out_ref[:, 0, j * 128 : j * 128 + 128] = part[:128].T
    tails = jnp.concatenate([part[128:] for part in parts] + [jnp.zeros((96, 128), jnp.float32)], axis=0)
    out_ref[:, 0, 512:] = tails.T


def pack(elem, coord):
    return call(pack_kernel, jax.ShapeDtypeStruct((SRC, 1, 640), jnp.float32), [elem, coord], [], far=(0, 1))


def exchange(values):
    return lax.all_to_all(values, ("mesh", "bg"), split_axis=0, concat_axis=0, tiled=True)


def moved(values, axis, by):
    count = lax.axis_size(axis)
    return lax.ppermute(values, axis, [(i, (i - by) % count) for i in range(count)])


def along_mesh(block):
    return jnp.concatenate([block, moved(block, "mesh", 1), moved(block, "mesh", -1)], axis=0)


def from_below(block):
    mesh, bg = lax.axis_size("mesh"), lax.axis_size("bg")
    steps = [
        (z * bg + y, ((z + 1) % mesh) * bg + (y + 1) % bg) for z in range(mesh) for y in range(bg)
    ]
    return [block, moved(block, "mesh", -1), moved(block, "bg", -1), lax.ppermute(block, ("mesh", "bg"), steps)]


def along_bg(rows):
    return [rows, moved(rows, "bg", 1), moved(rows, "bg", -1)]


def shards(displacement, bg_coef, query_elem, query_point, query_coord):
    asked = exchange(pack(query_elem[0].T, query_coord[0].transpose(1, 2, 0)))
    own = split_nodes(displacement)
    rows = along_mesh(own)
    asked, prepared = lax.optimization_barrier((asked, prepare(bg_coef)))
    found = lookup(asked, prepared)
    found = exchange(found)
    field = along_bg(rows)
    sizes = place(found, query_point[0].T)
    sizes = from_below(sizes)
    jac = all_jacobians(field, field_pieces)
    move, turn, size = first_descent(jac, sizes)
    rows = jnp.concatenate(along_bg(move), axis=0)
    terms = first_line(jac, turn, size)
    first_terms = exchange(terms)
    shift = [rows, moved(rows, "mesh", 1), moved(rows, "mesh", -1)]
    drift = all_jacobians(shift, shift_pieces)
    last_move, last_terms, step = second_pass(jac, drift, size, first_terms)
    last_terms = exchange(last_terms)
    nodes = join_nodes(own, move, last_move)
    return finish(*nodes, step, first_terms, last_terms)


def solution(mesh):
    in_specs = (
        P(None, "mesh", "bg", None),
        P(None, ("mesh", "bg")),
        P(("mesh", "bg"), None, None),
        P(("mesh", "bg"), None, None),
        P(("mesh", "bg"), None, None, None),
    )
    out_specs = (P(None, "mesh", "bg", None), P())
    return jax.shard_map(shards, mesh=mesh, in_specs=in_specs, out_specs=out_specs, check_vma=False)
```

```python
import functools

import jax
import jax.numpy as jnp
import numpy as np
from jax import lax
from jax.experimental import pallas as pl
from jax.experimental.pallas import tpu as pltpu
from jax.sharding import PartitionSpec as P

SRC = 128
SLOTS = 136
TABLE = 16384
COLS = 256


ROUNDS = 2
GATHERED = 34
PAIRS = 17


def in_vmem(count):
    return [pl.BlockSpec(memory_space=pltpu.VMEM) for _ in range(count)]


def call(kernel, outs, args, scratch, far=(), last=False):
    args = [a if i in far else pltpu.with_memory_space_constraint(a, pltpu.VMEM) for i, a in enumerate(args)]
    many = isinstance(outs, list)
    if not last:
        outs = [pltpu.VMEM(o.shape, o.dtype) for o in outs] if many else pltpu.VMEM(outs.shape, outs.dtype)
    return pl.pallas_call(
        kernel,
        out_shape=outs,
        in_specs=in_vmem(len(args)),
        out_specs=in_vmem(len(outs)) if many else in_vmem(1)[0],
        scratch_shapes=scratch,
    )(*args)


def prepare_kernel(table_ref, split_ref, packed_ref, unit_ref):
    top = jnp.zeros((8, 128), jnp.float32)
    for block in range(TABLE // 128):
        top = jnp.maximum(top, jnp.abs(table_ref[:, block * 128 : block * 128 + 128]))
    top = jnp.maximum(jnp.max(top, keepdims=True), 1e-30)
    unit_ref[...] = jnp.broadcast_to(top * (1.0 / 32767.0), (8, 128))
    scale = 32767.0 / top

    def whole(values):
        return (values * scale + 32768.5).astype(jnp.int32) - 32768

    for block in range(TABLE // 256):
        low = table_ref[:, block * 128 : block * 128 + 128]
        high = table_ref[:, TABLE // 2 + block * 128 : TABLE // 2 + block * 128 + 128]
        packed_ref[:, block * 128 : block * 128 + 128] = (whole(high) << 16) | (whole(low) & 65535)
    for pair in range(TABLE // (2 * COLS)):
        start = pair * 2 * COLS
        rows = jnp.concatenate(
            [table_ref[:, start : start + COLS], table_ref[:, start + COLS : start + 2 * COLS]], axis=0
        )
        upper = rows.astype(jnp.bfloat16)
        split_ref[pair * 16 : pair * 16 + 16, :COLS] = upper
        split_ref[pair * 16 : pair * 16 + 16, COLS:] = (rows - upper.astype(jnp.float32)).astype(jnp.bfloat16)


def prepare(table):
    outs = [
        jax.ShapeDtypeStruct((8 * TABLE // COLS, 2 * COLS), jnp.bfloat16),
        jax.ShapeDtypeStruct((8, TABLE // 2), jnp.int32),
        jax.ShapeDtypeStruct((8, 128), jnp.float32),
    ]
    return call(prepare_kernel, outs, [table], [], far=(0,))


def choose(leaf, masks, first, count):
    if count == 1:
        return leaf(first)
    half = count // 2
    mask = masks[half.bit_length() - 1]
    return jnp.where(mask, choose(leaf, masks, first + half, half), choose(leaf, masks, first, half))


def tall(row):
    return jnp.broadcast_to(row, (16, 128)).astype(jnp.bfloat16)


def at_rows(index_ref, count, row, *values):
    index = tall(row)
    zero = jnp.zeros((16, 128), jnp.bfloat16)
    masks = [index_ref[at : at + 16, :] == index for at in range(0, count, 16)]
    return jnp.concatenate([jnp.where(mask, value, zero) for value in values for mask in masks], axis=0)


def weigh(coef, x, y, z):
    corner = lax.broadcasted_iota(jnp.int32, coef.shape, 0)
    weight_x = jnp.where((corner & 1) == 1, x, 1.0 - x)
    weight_y = jnp.where((corner & 2) == 2, y, 1.0 - y)
    weight_z = jnp.where((corner & 4) == 4, z, 1.0 - z)
    lsize = jnp.sum(weight_x * weight_y * weight_z * coef, axis=0, keepdims=True)
    return jnp.exp(-2.0 * lsize)


def lookup_kernel(asked_ref, split_ref, packed_ref, unit_ref, found_ref, turned_ref, result_ref, column_ref):
    for j in range(4):
        turned_ref[j * SLOTS : j * SLOTS + 128, :] = asked_ref[:, 0, j * 128 : j * 128 + 128].T
    tails = asked_ref[:, 0, 512:].T
    for j in range(4):
        turned_ref[j * SLOTS + 128 : (j + 1) * SLOTS, :] = tails[j * 8 : j * 8 + 8]
    column_ref[...] = lax.broadcasted_iota(jnp.int32, (COLS, 128), 0).astype(jnp.float32).astype(jnp.bfloat16)

    def step(i, carry):
        unit = unit_ref[...]
        for r in range(GATHERED):
            at = i * GATHERED + r
            ids, x, y, z = (turned_ref[pl.ds(j * SLOTS + at, 1), :] for j in range(4))
            own = jnp.broadcast_to(ids.astype(jnp.int32), (8, 128))
            lane = own & 127
            masks = [(own & (128 << bit)) != 0 for bit in range(6)]

            def leaf(block):
                return jnp.take_along_axis(packed_ref[:, block * 128 : block * 128 + 128], lane, axis=1)

            word = choose(leaf, masks, 0, 64)
            whole = jnp.where((own & (TABLE // 2)) != 0, word, word << 16) >> 16
            coef = whole.astype(jnp.float32) * unit
            result_ref[pl.ds(at, 1), :] = weigh(coef, x, y, z)

        for pair in range(PAIRS):
            at = ROUNDS * GATHERED + (i * PAIRS + pair) * 2
            pair_ids, px, py, pz = (
                jnp.concatenate([turned_ref[pl.ds(j * SLOTS + at + k, 1), :] for k in range(2)], axis=1)
                for j in range(4)
            )
            pair_ids = pair_ids.astype(jnp.int32)
            column = (pair_ids & (COLS - 1)).astype(jnp.float32)
            ones = jnp.ones((16, 128), jnp.bfloat16)
            chosen = jnp.concatenate(
                [at_rows(column_ref, COLS, column[:, k * 128 : k * 128 + 128], ones) for k in range(2)], axis=1
            )
            picked = jnp.dot(split_ref[:, :COLS], chosen, preferred_element_type=jnp.float32) + jnp.dot(
                split_ref[:, COLS:], chosen, preferred_element_type=jnp.float32
            )
            own = jnp.broadcast_to(pair_ids, (8, 256))
            masks = [(own & (COLS << bit)) != 0 for bit in range(6)]
            coef = choose(lambda row: picked[row * 8 : row * 8 + 8], masks, 0, 64)
            value = weigh(coef, px, py, pz)
            for k in range(2):
                result_ref[pl.ds(at + k, 1), :] = value[:, k * 128 : k * 128 + 128]
        return carry

    lax.fori_loop(0, ROUNDS, step, 0)
    found_ref[:, 0, :128] = result_ref[:128, :].T
    found_ref[:, 0, 128:] = result_ref[128:, :].T


def lookup(asked, prepared):
    scratch = [
        pltpu.VMEM((4 * SLOTS, 128), jnp.float32),
        pltpu.VMEM((SLOTS, 128), jnp.float32),
        pltpu.VMEM((COLS, 128), jnp.bfloat16),
    ]
    out = jax.ShapeDtypeStruct((SRC, 1, SLOTS), jnp.float32)
    return call(lookup_kernel, out, [asked, *prepared], scratch)


def place_kernel(found_ref, point_ref, size_ref, value_ref, row_ref, lane_ref, at_ref):
    value_ref[:128, :] = found_ref[:, 0, :128].T
    value_ref[128:, :] = found_ref[:, 0, 128:].T
    point = point_ref[...]
    line = (point * 10923) >> 21
    qx = point - line * 192
    qz = (line * 43) >> 8
    qy = line - qz * 6
    ex = (qx * 171) >> 9
    jx = qx - ex * 3
    ey = (qy * 11) >> 5
    jy = qy - ey * 3
    ez = (qz * 11) >> 5
    jz = qz - ez * 3
    row_ref[...] = (((jz * 3 + jy) * 3 + jx) * 2 + ey).astype(jnp.float32)
    lane_ref[...] = (ez * 64 + ex).astype(jnp.float32)
    at_ref[...] = lax.broadcasted_iota(jnp.int32, (128, 128), 0).astype(jnp.float32).astype(jnp.bfloat16)
    ones = jnp.ones((16, 128), jnp.bfloat16)

    def step(i, total):
        values = value_ref[i * 8 : i * 8 + 8, :]
        rows = row_ref[i * 8 : i * 8 + 8, :]
        lanes = lane_ref[i * 8 : i * 8 + 8, :]
        left, right = [], []
        for r in range(8):
            value = values[r : r + 1]
            upper = tall(value)
            lower = tall(value - upper[:1].astype(jnp.float32))
            left.append(at_rows(at_ref, 64, rows[r : r + 1], upper, lower))
            right.append(at_rows(at_ref, 128, lanes[r : r + 1], ones))
        left = jnp.concatenate(left, axis=1)
        right = jnp.concatenate(right, axis=1)
        return total + lax.dot_general(left, right, (((1,), (1,)), ((), ())), preferred_element_type=jnp.float32)

    total = jnp.zeros((128, 128), jnp.float32)
    for i in range(SLOTS // 8):
        total = step(i, total)
    size_ref[...] = total[:56] + total[64:120]


def place(found, point):
    scratch = [pltpu.VMEM((SLOTS, 128), jnp.float32) for _ in range(3)] + [pltpu.VMEM((128, 128), jnp.bfloat16)]
    return call(place_kernel, jax.ShapeDtypeStruct((56, 128), jnp.float32), [found, point], scratch, far=(1,))


HALF_GAP = float(np.sqrt(0.15))
OUTER, MIDDLE = 5.0 / 18.0, 8.0 / 18.0


def field_pieces(refs):
    return {(z, y): (refs[y], (z % 3) * 48) for z in (-1, 0, 1) for y in (-1, 0, 1)}


def size_pieces(refs):
    own, z_low, y_low, corner = refs
    return {(0, 0): own, (-1, 0): z_low, (0, -1): y_low, (-1, -1): corner}


def lane_index():
    return lax.broadcasted_iota(jnp.int32, (8, 128), 1)


def x_up(v):
    return jnp.where((lane_index() & 63) == 63, pltpu.roll(v, 63, 1), pltpu.roll(v, 127, 1))


def x_down(v):
    return jnp.where((lane_index() & 63) == 0, pltpu.roll(v, 65, 1), pltpu.roll(v, 1, 1))


def z_down(v):
    turned = pltpu.roll(v, 64, 1)
    return jnp.where(lane_index() < 64, pltpu.roll(turned, 4, 0), turned)


def y_down(v):
    return pltpu.roll(v, 1, 0)


def spread(low, mid, high, slopes=True, values=True):
    bend = (low + high) - 2.0 * mid
    rise = high - low
    vals = slps = None
    if values:
        centre = mid + (2.0 * HALF_GAP * HALF_GAP) * bend
        lean = HALF_GAP * rise
        vals = (centre - lean, mid, centre + lean)
    if slopes:
        change = (4.0 * HALF_GAP) * bend
        slps = (rise - change, rise, rise + change)
    return vals, slps


def collect(vals, slps):
    bend = rise = mid = None
    if vals is not None:
        outer = vals[0] + vals[2]
        bend = (2.0 * HALF_GAP * HALF_GAP) * outer
        rise = HALF_GAP * (vals[2] - vals[0])
        mid = outer + vals[1]
    if slps is not None:
        slope_bend = (4.0 * HALF_GAP) * (slps[2] - slps[0])
        slope_rise = (slps[0] + slps[2]) + slps[1]
        bend = slope_bend if bend is None else bend + slope_bend
        rise = slope_rise if rise is None else rise + slope_rise
    twice = -2.0 * bend
    return bend - rise, twice if mid is None else mid + twice, bend + rise


def at_point(c, k, jz, jy, jx):
    row = (((jz * 3 + jy) * 3 + jx) * 9 + k) * 8
    return pl.ds(row + c * 24, 8)


def forward(local, out_ref, at):
    along_z = [[spread(local(0, y, x), local(1, y, x), local(2, y, x)) for x in range(3)] for y in range(3)]
    for jz in range(3):
        value = [[along_z[y][x][0][jz] for x in range(3)] for y in range(3)]
        slope = [[along_z[y][x][1][jz] for x in range(3)] for y in range(3)]
        plain = [spread(value[0][x], value[1][x], value[2][x]) for x in range(3)]
        steep = [spread(slope[0][x], slope[1][x], slope[2][x], slopes=False)[0] for x in range(3)]
        for jy in range(3):
            dx = spread(*(plain[x][0][jy] for x in range(3)), values=False)[1]
            dy = spread(*(plain[x][1][jy] for x in range(3)), slopes=False)[0]
            dz = spread(*(steep[x][jy] for x in range(3)), slopes=False)[0]
            for jx in range(3):
                for k, part in enumerate((dx, dy, dz)):
                    out_ref[at(k, jz, jy, jx), :] = part[jx]


def backward(c, from_ref, out_ref):
    planes = []
    for jz in range(3):
        lines = []
        for jy in range(3):
            dx, dy, dz = (
                tuple(from_ref[at_point(c, k, jz, jy, jx), :] for jx in range(3)) for k in range(3)
            )
            lines.append((collect(None, dx), collect(dy, None), collect(dz, None)))
        value = [
            collect(tuple(lines[jy][0][x] for jy in range(3)), tuple(lines[jy][1][x] for jy in range(3)))
            for x in range(3)
        ]
        slope = [collect(tuple(lines[jy][2][x] for jy in range(3)), None) for x in range(3)]
        planes.append((value, slope))
    whole = [
        [
            collect(
                tuple(planes[jz][0][x][y] for jz in range(3)), tuple(planes[jz][1][x][y] for jz in range(3))
            )
            for x in range(3)
        ]
        for y in range(3)
    ]
    folded_x = [[(whole[y][0][z] + x_down(whole[y][2][z]), whole[y][1][z]) for z in range(3)] for y in range(3)]
    for x in range(2):
        folded = [(folded_x[0][z][x] + y_down(folded_x[2][z][x]), folded_x[1][z][x]) for z in range(3)]
        for y in range(2):
            for z, node in enumerate((folded[0][y] + z_down(folded[2][y]), folded[1][y])):
                row = (z * 4 + y * 2 + x) * 8
                out_ref[pl.ds(row + c * 64, 8), :] = node


def symmetric(build):
    upper = {(k, l): build(k, l) for k in range(3) for l in range(k, 3)}
    return {(k, l): upper[min(k, l), max(k, l)] for k in range(3) for l in range(3)}


def inner(a, b):
    square = (a[0, 0] * b[0, 0] + a[1, 1] * b[1, 1]) + a[2, 2] * b[2, 2]
    cross = (a[0, 1] * b[0, 1] + a[0, 2] * b[0, 2]) + a[1, 2] * b[1, 2]
    return square + 2.0 * cross


def column_dot(a, b, k, l):
    return (a[0][k] * b[0][l] + a[1][k] * b[1][l]) + a[2][k] * b[2][l]


def load_tensor(ref, jz, jy, jx):
    tensor = [[ref[at_point(c, k, jz, jy, jx), :] for k in range(3)] for c in range(3)]
    return tensor


def jacobian_at(ref, jz, jy, jx):
    tensor = load_tensor(ref, jz, jy, jx)
    return [[tensor[c][k] + 1.0 if c == k else tensor[c][k] for k in range(3)] for c in range(3)]


def strain_of(jac, size):
    return symmetric(lambda k, l: column_dot(jac, jac, k, l) * size - (1.0 if k == l else 0.0))


def weight_at(jz, jy, jx):
    along_z = MIDDLE if jz == 1 else OUTER
    return along_z * ((MIDDLE if jy == 1 else OUTER) * (MIDDLE if jx == 1 else OUTER))


def newton_step(totals):
    _, linear, quadratic, cubic, quartic, floor = (jnp.broadcast_to(totals[:, i : i + 1], (8, 128)) for i in range(6))
    step = jnp.zeros_like(linear)
    for _ in range(4):
        slope = linear + step * (2.0 * quadratic + step * (3.0 * cubic + step * 4.0 * quartic))
        curvature = 2.0 * quadratic + step * (6.0 * cubic + step * 12.0 * quartic)
        step = step - slope / jnp.maximum(curvature, floor + 1e-06)
    return step


def add_up(terms_ref):
    return jnp.sum(terms_ref[...], axis=0, keepdims=True)


def ring(pieces, count, out_ref, out_at, z_shift, y_shift):
    low = lax.broadcasted_iota(jnp.int32, (count, 128), 1) < 64
    places = ((-1, 1), (0, 0), (0, 1), (1, 0)) if y_shift else ((-1, 0), (-1, 1), (0, 0), (0, 1))
    for upper in range(2):
        for y, (piece_y, row) in enumerate(places):

            def piece(z):
                ref, at = pieces[z, piece_y]
                return ref[pl.ds(at + row, count, stride=2), :]

            value = piece(-upper)
            if z_shift:
                value = jnp.where(low, pltpu.roll(value, 64, 1), pltpu.roll(piece(1 - upper), 64, 1))
            out_ref[pl.ds(out_at + upper * 4 + y, count, stride=8), :] = value


def each(body):
    for i in range(3):
        body(i)


def jacobians(field, nodes_ref, jac_ref):
    for z_shift in range(2):
        for y_shift in range(2):
            ring(field, 24, nodes_ref, (z_shift * 2 + y_shift) * 192, z_shift, y_shift)

    def known(c):
        def local(z, y, x):
            row = ((z == 2) * 2 + (y == 2)) * 192 + ((z % 2) * 4 + (y % 2) * 2 + x % 2) * 8
            value = nodes_ref[pl.ds(row + c * 64, 8), :]
            return x_up(value) if x == 2 else value

        return local

    each(lambda c: forward(known(c), jac_ref, functools.partial(at_point, c)))


def descend(size_ref, jac_ref, part_ref, turn_ref, move_ref):
    def size_at(jz, jy, jx):
        return size_ref[pl.ds((jz * 9 + jy * 3 + jx) * 8, 8), :]

    turn_ref[192:, :] = jnp.zeros((64, 128), jnp.float32)

    def stress(jz):
        for jy in range(3):
            for jx in range(3):
                jac = jacobian_at(jac_ref, jz, jy, jx)
                size = size_at(jz, jy, jx)
                strain = strain_of(jac, size)
                scale = size * (-4.0 * weight_at(jz, jy, jx))
                for c in range(3):
                    for k in range(3):
                        part = (strain[k, 0] * jac[c][0] + strain[k, 1] * jac[c][1]) + strain[k, 2] * jac[c][2]
                        part_ref[at_point(c, k, jz, jy, jx), :] = part * scale

    each(stress)
    each(lambda c: backward(c, part_ref, turn_ref))
    for row in range(2):
        move_ref[pl.ds(row, 24, stride=2), :] = turn_ref[pl.ds(row + 2, 24, stride=8), :]


def line_sums(size_ref, jac_ref, part_ref, turn_ref, terms_out):
    def packed(node, upper, shift):
        rows = [
            turn_ref[pl.ds(node * 8 + upper * 4 + 1 + shift + ey, 4, stride=64), :] for ey in range(2)
        ]
        return jnp.concatenate(rows, axis=0)

    def sought(z, y, x):
        node = (z % 2) * 4 + (y % 2) * 2 + x % 2
        shift = y // 2
        value = packed(node, 0, shift)
        if z == 2:
            value = pltpu.roll(value, 64, 1)
        else:
            value = jnp.where(lane_index() < 64, value, packed(node, 1, shift))
        return x_up(value) if x == 2 else value

    forward(sought, part_ref, lambda k, jz, jy, jx: pl.ds(((jz * 9 + jy * 3 + jx) * 3 + k) * 8, 8))

    def middle(ref, at, stride):
        return jnp.where(lane_index() < 64, ref[pl.ds(at, 8, stride=stride), :], ref[pl.ds(at + 4, 8, stride=stride), :])

    sub = lax.broadcasted_iota(jnp.int32, (8, 128), 0)
    sums = [jnp.zeros((8, 128), jnp.float32) for _ in range(6)]
    for start, fresh in ((0, 0), (8, 8), (16, 16), (19, 24)):
        weight = jnp.zeros((8, 128), jnp.float32)
        for i in range(fresh - start, 8):
            point = start + i
            parts = [MIDDLE if (point // by) % 3 == 1 else OUTER for by in (9, 3, 1)]
            weight = jnp.where(sub == i, (parts[0] * parts[1]) * parts[2], weight)
        for ey in range(2):
            jac = [
                [middle(jac_ref, (start * 9 + c * 3 + k) * 8 + 1 + ey, 72) for k in range(3)]
                for c in range(3)
            ]
            jac = [[jac[c][k] + 1.0 if c == k else jac[c][k] for k in range(3)] for c in range(3)]
            motion = [
                [part_ref[pl.ds((start * 3 + k) * 8 + ey * 4 + c, 8, stride=24), :] for k in range(3)]
                for c in range(3)
            ]
            size = middle(size_ref, start * 8 + 1 + ey, 8)
            zero = strain_of(jac, size)
            one = symmetric(lambda k, l: (column_dot(jac, motion, k, l) + column_dot(motion, jac, k, l)) * size)
            two = symmetric(lambda k, l: column_dot(motion, motion, k, l) * size)
            pairs = ((zero, zero), (zero, one), (zero, two), (one, two), (two, two), (one, one))
            sums = [total + weight * inner(*pair) for total, pair in zip(sums, pairs)]
    zz, zo, zt, ot, tt, gn = (jnp.sum(total, keepdims=True) for total in sums)
    lane = lax.broadcasted_iota(jnp.int32, (1, 128), 1)
    terms = jnp.zeros((1, 128), jnp.float32)
    for i, term in enumerate((zz, 2.0 * zo, gn + 2.0 * zt, 2.0 * ot, tt, gn)):
        terms = jnp.where(lane == i, term, terms)
    terms_out[...] = jnp.broadcast_to(terms, (SRC, 128))


def jacobian_kernel(*refs):
    jacobians(field_pieces(refs[:3]), refs[4], refs[3])


def descent_kernel(jac_ref, own, z_low, y_low, corner, move_ref, turn_ref, size_ref, part_ref):
    sizes = {at: (ref, 0) for at, ref in size_pieces([own, z_low, y_low, corner]).items()}
    ring(sizes, 27, size_ref, 0, 0, 0)
    descend(size_ref, jac_ref, part_ref, turn_ref, move_ref)


def line_kernel(jac_ref, turn_ref, size_ref, terms_out, part_ref):
    line_sums(size_ref, jac_ref, part_ref, turn_ref, terms_out)


def second_kernel(before_ref, drift_ref, size_ref, terms_in, move_ref, terms_out, step_ref, jac_ref, part_ref, turn_ref):
    step = newton_step(add_up(terms_in))
    step_ref[...] = step
    for row in range(0, JAC_ROWS, 8):
        rows = slice(row, row + 8)
        jac_ref[rows, :] = before_ref[rows, :] + step * drift_ref[rows, :]
    descend(size_ref, jac_ref, part_ref, turn_ref, move_ref)
    line_sums(size_ref, jac_ref, part_ref, turn_ref, terms_out)


NODE = jax.ShapeDtypeStruct((48, 128), jnp.float32)
TERMS = jax.ShapeDtypeStruct((SRC, 128), jnp.float32)
NODES_ROWS, JAC_ROWS, TURN_ROWS, SIZE_ROWS = 4 * 192, 243 * 8, 32 * 8, 27 * 8


def rows_of(count):
    return jax.ShapeDtypeStruct((count, 128), jnp.float32)


def scratch_of(count):
    return pltpu.VMEM((count, 128), jnp.float32)


def all_jacobians(field):
    return call(jacobian_kernel, rows_of(JAC_ROWS), field, [scratch_of(NODES_ROWS)])


def first_descent(jac, sizes):
    outs = [NODE, rows_of(TURN_ROWS), rows_of(SIZE_ROWS)]
    return call(descent_kernel, outs, [jac, *sizes], [scratch_of(JAC_ROWS)])


def first_line(jac, turn, size):
    return call(line_kernel, TERMS, [jac, turn, size], [scratch_of(81 * 8)])


def second_pass(jac, drift, size, terms):
    scratch = [scratch_of(rows) for rows in (JAC_ROWS, JAC_ROWS, TURN_ROWS)]
    return call(second_kernel, [NODE, TERMS, rows_of(8)], [jac, drift, size, terms], scratch)


def interleave(back):
    row = lax.broadcasted_iota(jnp.int32, (128, 128), 0)
    col = lax.broadcasted_iota(jnp.int32, (128, 128), 1)
    if back:
        row, col = col, row
    return (col == (row & 1) * 64 + (row >> 1)).astype(jnp.float32)


def split_kernel(nodes_ref, out_ref, rows_ref):
    rows = nodes_ref[...].reshape(48, 128)
    rows_ref[...] = jnp.dot(rows, interleave(False), precision=lax.Precision.HIGHEST, preferred_element_type=jnp.float32)
    low = lax.broadcasted_iota(jnp.int32, (1, 128), 1) < 64
    for c in range(3):
        for az in range(2):
            for ay in range(2):
                for ey in range(2):
                    at = c * 16 + az * 4 + ey * 2 + ay
                    first = rows_ref[at : at + 1, :]
                    second = rows_ref[at + 8 : at + 9, :]
                    to = (c * 8 + az * 4 + ay * 2) * 2 + ey
                    out_ref[to : to + 1, :] = jnp.where(low, first, pltpu.roll(second, 64, 1))
                    out_ref[to + 2 : to + 3, :] = jnp.where(low, pltpu.roll(first, 64, 1), second)


def split_nodes(nodes):
    out = jax.ShapeDtypeStruct((48, 128), jnp.float32)
    return call(split_kernel, out, [nodes], [pltpu.VMEM((48, 128), jnp.float32)], far=(0,))


def join_kernel(count, *refs):
    rows_ref = refs[-1]
    low = lax.broadcasted_iota(jnp.int32, (1, 128), 1) < 64
    for i, new_ref in enumerate(refs[:count]):
        for c in range(3):
            for az in range(2):
                for ay in range(2):
                    for ey in range(2):
                        at = (c * 8 + az * 4 + ay * 2) * 2 + ey
                        even = new_ref[at : at + 1, :]
                        odd = new_ref[at + 2 : at + 3, :]
                        to = i * 48 + c * 16 + az * 4 + ey * 2 + ay
                        rows_ref[to : to + 1, :] = jnp.where(low, even, pltpu.roll(odd, 64, 1))
                        rows_ref[to + 8 : to + 9, :] = jnp.where(low, pltpu.roll(even, 64, 1), odd)
    rows = jnp.dot(
        rows_ref[...], interleave(True), precision=lax.Precision.HIGHEST, preferred_element_type=jnp.float32
    )
    for i, out_ref in enumerate(refs[count : 2 * count]):
        out_ref[...] = rows[i * 48 : i * 48 + 48].reshape(3, 4, 4, 128)


def join_nodes(*nodes):
    outs = [jax.ShapeDtypeStruct((3, 4, 4, 128), jnp.float32) for _ in nodes]
    kernel = functools.partial(join_kernel, len(nodes))
    return call(kernel, outs, list(nodes), [scratch_of(48 * len(nodes))])


def finish_kernel(own_ref, first_move_ref, last_move_ref, step_ref, first_ref, second_ref, out_ref, coeff_ref):
    second = add_up(second_ref)
    step = newton_step(second)[:4]
    first_step = step_ref[:4, :]
    for c in range(3):
        for z in range(4):
            field = own_ref[c, z] + first_step * first_move_ref[c, z]
            out_ref[c, z] = field + step * last_move_ref[c, z]
    coeff_ref[0:1, :] = add_up(first_ref)[:, :5] * (1.0 / 32768.0)
    coeff_ref[1:2, :] = second[:, :5] * (1.0 / 32768.0)


def finish(*args):
    outs = [jax.ShapeDtypeStruct((3, 4, 4, 128), jnp.float32), jax.ShapeDtypeStruct((2, 5), jnp.float32)]
    return call(finish_kernel, outs, list(args), [], last=True)


def pack_kernel(elem_ref, coord_ref, out_ref):
    parts = [elem_ref[...].astype(jnp.float32)] + [coord_ref[j] for j in range(3)]
    for j, part in enumerate(parts):
        out_ref[:, 0, j * 128 : j * 128 + 128] = part[:128].T
    tails = jnp.concatenate([part[128:] for part in parts] + [jnp.zeros((96, 128), jnp.float32)], axis=0)
    out_ref[:, 0, 512:] = tails.T


def pack(elem, coord):
    return call(pack_kernel, jax.ShapeDtypeStruct((SRC, 1, 640), jnp.float32), [elem, coord], [], far=(0, 1))


def exchange(values):
    return lax.all_to_all(values, ("mesh", "bg"), split_axis=0, concat_axis=0, tiled=True)


def moved(values, axis, by):
    count = lax.axis_size(axis)
    return lax.ppermute(values, axis, [(i, (i - by) % count) for i in range(count)])


def along_mesh(block):
    return jnp.concatenate([block, moved(block, "mesh", 1), moved(block, "mesh", -1)], axis=0)


def from_below(block):
    mesh, bg = lax.axis_size("mesh"), lax.axis_size("bg")
    steps = [
        (z * bg + y, ((z + 1) % mesh) * bg + (y + 1) % bg) for z in range(mesh) for y in range(bg)
    ]
    corner = lax.ppermute(block, ("mesh", "bg"), steps)
    z_low = moved(block, "mesh", -1)
    y_low = moved(block, "bg", -1)
    return [block, z_low, y_low, corner]


def along_bg(rows):
    return [rows, moved(rows, "bg", 1), moved(rows, "bg", -1)]


def shards(displacement, bg_coef, query_elem, query_point, query_coord):
    asked = exchange(pack(query_elem[0].T, query_coord[0].transpose(1, 2, 0)))
    own = split_nodes(displacement)
    rows = along_mesh(own)
    asked, prepared = lax.optimization_barrier((asked, prepare(bg_coef)))
    found = lookup(asked, prepared)
    found = exchange(found)
    field = along_bg(rows)
    sizes = place(found, query_point[0].T)
    sizes = from_below(sizes)
    jac = all_jacobians(field)
    move, turn, size = first_descent(jac, sizes)
    rows = along_mesh(move)
    terms = first_line(jac, turn, size)
    first_terms = exchange(terms)
    shift = along_bg(rows)
    drift = all_jacobians(shift)
    last_move, last_terms, step = second_pass(jac, drift, size, first_terms)
    last_terms = exchange(last_terms)
    nodes = join_nodes(own, move, last_move)
    return finish(*nodes, step, first_terms, last_terms)


def solution(mesh):
    in_specs = (
        P(None, "mesh", "bg", None),
        P(None, ("mesh", "bg")),
        P(("mesh", "bg"), None, None),
        P(("mesh", "bg"), None, None),
        P(("mesh", "bg"), None, None, None),
    )
    out_specs = (P(None, "mesh", "bg", None), P())
    return jax.shard_map(shards, mesh=mesh, in_specs=in_specs, out_specs=out_specs, check_vma=False)
```

```python
import functools

import jax
import jax.numpy as jnp
import numpy as np
from jax import lax
from jax.experimental import pallas as pl
from jax.experimental.pallas import tpu as pltpu
from jax.sharding import PartitionSpec as P

SRC = 128
SLOTS = 136
TABLE = 16384
COLS = 256


ROUNDS = 2
GATHERED = 34
PAIRS = 17


def in_vmem(count):
    return [pl.BlockSpec(memory_space=pltpu.VMEM) for _ in range(count)]


def call(kernel, outs, args, scratch, far=(), last=False):
    args = [a if i in far else pltpu.with_memory_space_constraint(a, pltpu.VMEM) for i, a in enumerate(args)]
    many = isinstance(outs, list)
    if not last:
        outs = [pltpu.VMEM(o.shape, o.dtype) for o in outs] if many else pltpu.VMEM(outs.shape, outs.dtype)
    return pl.pallas_call(
        kernel,
        out_shape=outs,
        in_specs=in_vmem(len(args)),
        out_specs=in_vmem(len(outs)) if many else in_vmem(1)[0],
        scratch_shapes=scratch,
    )(*args)


def prepare_kernel(table_ref, split_ref, packed_ref, unit_ref):
    top = jnp.zeros((8, 128), jnp.float32)
    for block in range(TABLE // 128):
        top = jnp.maximum(top, jnp.abs(table_ref[:, block * 128 : block * 128 + 128]))
    top = jnp.maximum(jnp.max(top, keepdims=True), 1e-30)
    unit_ref[...] = jnp.broadcast_to(top * (1.0 / 32767.0), (8, 128))
    scale = 32767.0 / top

    def whole(values):
        return (values * scale + 32768.5).astype(jnp.int32) - 32768

    for block in range(TABLE // 256):
        low = table_ref[:, block * 128 : block * 128 + 128]
        high = table_ref[:, TABLE // 2 + block * 128 : TABLE // 2 + block * 128 + 128]
        packed_ref[:, block * 128 : block * 128 + 128] = (whole(high) << 16) | (whole(low) & 65535)
    for pair in range(TABLE // (2 * COLS)):
        start = pair * 2 * COLS
        rows = jnp.concatenate(
            [table_ref[:, start : start + COLS], table_ref[:, start + COLS : start + 2 * COLS]], axis=0
        )
        upper = rows.astype(jnp.bfloat16)
        split_ref[pair * 16 : pair * 16 + 16, :COLS] = upper
        split_ref[pair * 16 : pair * 16 + 16, COLS:] = (rows - upper.astype(jnp.float32)).astype(jnp.bfloat16)


def prepare(table):
    outs = [
        jax.ShapeDtypeStruct((8 * TABLE // COLS, 2 * COLS), jnp.bfloat16),
        jax.ShapeDtypeStruct((8, TABLE // 2), jnp.int32),
        jax.ShapeDtypeStruct((8, 128), jnp.float32),
    ]
    return call(prepare_kernel, outs, [table], [], far=(0,))


def choose(leaf, masks, first, count):
    if count == 1:
        return leaf(first)
    half = count // 2
    mask = masks[half.bit_length() - 1]
    return jnp.where(mask, choose(leaf, masks, first + half, half), choose(leaf, masks, first, half))


def tall(row):
    return jnp.broadcast_to(row, (16, 128)).astype(jnp.bfloat16)


def at_rows(index_ref, count, row, *values):
    index = tall(row)
    zero = jnp.zeros((16, 128), jnp.bfloat16)
    masks = [index_ref[at : at + 16, :] == index for at in range(0, count, 16)]
    return jnp.concatenate([jnp.where(mask, value, zero) for value in values for mask in masks], axis=0)


def weigh(coef, x, y, z):
    corner = lax.broadcasted_iota(jnp.int32, coef.shape, 0)
    weight_x = jnp.where((corner & 1) == 1, x, 1.0 - x)
    weight_y = jnp.where((corner & 2) == 2, y, 1.0 - y)
    weight_z = jnp.where((corner & 4) == 4, z, 1.0 - z)
    lsize = jnp.sum(weight_x * weight_y * weight_z * coef, axis=0, keepdims=True)
    return jnp.exp(-2.0 * lsize)


def lookup_kernel(asked_ref, split_ref, packed_ref, unit_ref, found_ref, turned_ref, result_ref, column_ref):
    for j in range(4):
        turned_ref[j * SLOTS : j * SLOTS + 128, :] = asked_ref[:, 0, j * 128 : j * 128 + 128].T
    tails = asked_ref[:, 0, 512:].T
    for j in range(4):
        turned_ref[j * SLOTS + 128 : (j + 1) * SLOTS, :] = tails[j * 8 : j * 8 + 8]
    column_ref[...] = lax.broadcasted_iota(jnp.int32, (COLS, 128), 0).astype(jnp.float32).astype(jnp.bfloat16)

    def step(i, carry):
        unit = unit_ref[...]
        for r in range(GATHERED):
            at = i * GATHERED + r
            ids, x, y, z = (turned_ref[pl.ds(j * SLOTS + at, 1), :] for j in range(4))
            own = jnp.broadcast_to(ids.astype(jnp.int32), (8, 128))
            lane = own & 127
            masks = [(own & (128 << bit)) != 0 for bit in range(6)]

            def leaf(block):
                return jnp.take_along_axis(packed_ref[:, block * 128 : block * 128 + 128], lane, axis=1)

            word = choose(leaf, masks, 0, 64)
            whole = jnp.where((own & (TABLE // 2)) != 0, word, word << 16) >> 16
            coef = whole.astype(jnp.float32) * unit
            result_ref[pl.ds(at, 1), :] = weigh(coef, x, y, z)

        for pair in range(PAIRS):
            at = ROUNDS * GATHERED + (i * PAIRS + pair) * 2
            pair_ids, px, py, pz = (
                jnp.concatenate([turned_ref[pl.ds(j * SLOTS + at + k, 1), :] for k in range(2)], axis=1)
                for j in range(4)
            )
            pair_ids = pair_ids.astype(jnp.int32)
            column = (pair_ids & (COLS - 1)).astype(jnp.float32)
            ones = jnp.ones((16, 128), jnp.bfloat16)
            chosen = jnp.concatenate(
                [at_rows(column_ref, COLS, column[:, k * 128 : k * 128 + 128], ones) for k in range(2)], axis=1
            )
            picked = jnp.dot(split_ref[:, :COLS], chosen, preferred_element_type=jnp.float32) + jnp.dot(
                split_ref[:, COLS:], chosen, preferred_element_type=jnp.float32
            )
            own = jnp.broadcast_to(pair_ids, (8, 256))
            masks = [(own & (COLS << bit)) != 0 for bit in range(6)]
            coef = choose(lambda row: picked[row * 8 : row * 8 + 8], masks, 0, 64)
            value = weigh(coef, px, py, pz)
            for k in range(2):
                result_ref[pl.ds(at + k, 1), :] = value[:, k * 128 : k * 128 + 128]
        return carry

    lax.fori_loop(0, ROUNDS, step, 0)
    found_ref[:, 0, :128] = result_ref[:128, :].T
    found_ref[:, 0, 128:] = result_ref[128:, :].T


def lookup(asked, prepared):
    scratch = [
        pltpu.VMEM((4 * SLOTS, 128), jnp.float32),
        pltpu.VMEM((SLOTS, 128), jnp.float32),
        pltpu.VMEM((COLS, 128), jnp.bfloat16),
    ]
    out = jax.ShapeDtypeStruct((SRC, 1, SLOTS), jnp.float32)
    return call(lookup_kernel, out, [asked, *prepared], scratch)


def place_kernel(found_ref, point_ref, size_ref, value_ref, row_ref, lane_ref, at_ref):
    value_ref[:128, :] = found_ref[:, 0, :128].T
    value_ref[128:, :] = found_ref[:, 0, 128:].T
    point = point_ref[...]
    line = (point * 10923) >> 21
    qx = point - line * 192
    qz = (line * 43) >> 8
    qy = line - qz * 6
    ex = (qx * 171) >> 9
    jx = qx - ex * 3
    ey = (qy * 11) >> 5
    jy = qy - ey * 3
    ez = (qz * 11) >> 5
    jz = qz - ez * 3
    row_ref[...] = (((jz * 3 + jy) * 3 + jx) * 2 + ey).astype(jnp.float32)
    lane_ref[...] = (ez * 64 + ex).astype(jnp.float32)
    at_ref[...] = lax.broadcasted_iota(jnp.int32, (128, 128), 0).astype(jnp.float32).astype(jnp.bfloat16)
    ones = jnp.ones((16, 128), jnp.bfloat16)

    def step(i, total):
        values = value_ref[i * 8 : i * 8 + 8, :]
        rows = row_ref[i * 8 : i * 8 + 8, :]
        lanes = lane_ref[i * 8 : i * 8 + 8, :]
        left, right = [], []
        for r in range(8):
            value = values[r : r + 1]
            upper = tall(value)
            lower = tall(value - upper[:1].astype(jnp.float32))
            left.append(at_rows(at_ref, 64, rows[r : r + 1], upper, lower))
            right.append(at_rows(at_ref, 128, lanes[r : r + 1], ones))
        left = jnp.concatenate(left, axis=1)
        right = jnp.concatenate(right, axis=1)
        return total + lax.dot_general(left, right, (((1,), (1,)), ((), ())), preferred_element_type=jnp.float32)

    total = jnp.zeros((128, 128), jnp.float32)
    for i in range(SLOTS // 8):
        total = step(i, total)
    size_ref[...] = total[:56] + total[64:120]


def place(found, point):
    scratch = [pltpu.VMEM((SLOTS, 128), jnp.float32) for _ in range(3)] + [pltpu.VMEM((128, 128), jnp.bfloat16)]
    return call(place_kernel, jax.ShapeDtypeStruct((56, 128), jnp.float32), [found, point], scratch, far=(1,))


HALF_GAP = float(np.sqrt(0.15))
OUTER, MIDDLE = 5.0 / 18.0, 8.0 / 18.0


def shift_pieces(refs):
    return {(z, y): (refs[z], (y % 3) * 48) for z in (-1, 0, 1) for y in (-1, 0, 1)}


def field_pieces(refs):
    return {(z, y): (refs[y], (z % 3) * 48) for z in (-1, 0, 1) for y in (-1, 0, 1)}


def size_pieces(refs):
    own, z_low, y_low, corner = refs
    return {(0, 0): own, (-1, 0): z_low, (0, -1): y_low, (-1, -1): corner}


def lane_index():
    return lax.broadcasted_iota(jnp.int32, (8, 128), 1)


def x_up(v):
    return jnp.where((lane_index() & 63) == 63, pltpu.roll(v, 63, 1), pltpu.roll(v, 127, 1))


def x_down(v):
    return jnp.where((lane_index() & 63) == 0, pltpu.roll(v, 65, 1), pltpu.roll(v, 1, 1))


def z_down(v):
    turned = pltpu.roll(v, 64, 1)
    return jnp.where(lane_index() < 64, pltpu.roll(turned, 4, 0), turned)


def y_down(v):
    return pltpu.roll(v, 1, 0)


def spread(low, mid, high, slopes=True, values=True):
    bend = (low + high) - 2.0 * mid
    rise = high - low
    vals = slps = None
    if values:
        centre = mid + (2.0 * HALF_GAP * HALF_GAP) * bend
        lean = HALF_GAP * rise
        vals = (centre - lean, mid, centre + lean)
    if slopes:
        change = (4.0 * HALF_GAP) * bend
        slps = (rise - change, rise, rise + change)
    return vals, slps


def collect(vals, slps):
    bend = rise = mid = None
    if vals is not None:
        outer = vals[0] + vals[2]
        bend = (2.0 * HALF_GAP * HALF_GAP) * outer
        rise = HALF_GAP * (vals[2] - vals[0])
        mid = outer + vals[1]
    if slps is not None:
        slope_bend = (4.0 * HALF_GAP) * (slps[2] - slps[0])
        slope_rise = (slps[0] + slps[2]) + slps[1]
        bend = slope_bend if bend is None else bend + slope_bend
        rise = slope_rise if rise is None else rise + slope_rise
    twice = -2.0 * bend
    return bend - rise, twice if mid is None else mid + twice, bend + rise


def at_point(c, k, jz, jy, jx):
    row = (((jz * 3 + jy) * 3 + jx) * 9 + k) * 8
    return pl.ds(row + c * 24, 8)


def forward(local, out_ref, at):
    along_z = [[spread(local(0, y, x), local(1, y, x), local(2, y, x)) for x in range(3)] for y in range(3)]
    for jz in range(3):
        value = [[along_z[y][x][0][jz] for x in range(3)] for y in range(3)]
        slope = [[along_z[y][x][1][jz] for x in range(3)] for y in range(3)]
        plain = [spread(value[0][x], value[1][x], value[2][x]) for x in range(3)]
        steep = [spread(slope[0][x], slope[1][x], slope[2][x], slopes=False)[0] for x in range(3)]
        for jy in range(3):
            dx = spread(*(plain[x][0][jy] for x in range(3)), values=False)[1]
            dy = spread(*(plain[x][1][jy] for x in range(3)), slopes=False)[0]
            dz = spread(*(steep[x][jy] for x in range(3)), slopes=False)[0]
            for jx in range(3):
                for k, part in enumerate((dx, dy, dz)):
                    out_ref[at(k, jz, jy, jx), :] = part[jx]


def backward(c, from_ref, out_ref):
    planes = []
    for jz in range(3):
        lines = []
        for jy in range(3):
            dx, dy, dz = (
                tuple(from_ref[at_point(c, k, jz, jy, jx), :] for jx in range(3)) for k in range(3)
            )
            lines.append((collect(None, dx), collect(dy, None), collect(dz, None)))
        value = [
            collect(tuple(lines[jy][0][x] for jy in range(3)), tuple(lines[jy][1][x] for jy in range(3)))
            for x in range(3)
        ]
        slope = [collect(tuple(lines[jy][2][x] for jy in range(3)), None) for x in range(3)]
        planes.append((value, slope))
    whole = [
        [
            collect(
                tuple(planes[jz][0][x][y] for jz in range(3)), tuple(planes[jz][1][x][y] for jz in range(3))
            )
            for x in range(3)
        ]
        for y in range(3)
    ]
    folded_x = [[(whole[y][0][z] + x_down(whole[y][2][z]), whole[y][1][z]) for z in range(3)] for y in range(3)]
    for x in range(2):
        folded = [(folded_x[0][z][x] + y_down(folded_x[2][z][x]), folded_x[1][z][x]) for z in range(3)]
        for y in range(2):
            for z, node in enumerate((folded[0][y] + z_down(folded[2][y]), folded[1][y])):
                row = (z * 4 + y * 2 + x) * 8
                out_ref[pl.ds(row + c * 64, 8), :] = node


def symmetric(build):
    upper = {(k, l): build(k, l) for k in range(3) for l in range(k, 3)}
    return {(k, l): upper[min(k, l), max(k, l)] for k in range(3) for l in range(3)}


def inner(a, b):
    square = (a[0, 0] * b[0, 0] + a[1, 1] * b[1, 1]) + a[2, 2] * b[2, 2]
    cross = (a[0, 1] * b[0, 1] + a[0, 2] * b[0, 2]) + a[1, 2] * b[1, 2]
    return square + 2.0 * cross


def column_dot(a, b, k, l):
    return (a[0][k] * b[0][l] + a[1][k] * b[1][l]) + a[2][k] * b[2][l]


def load_tensor(ref, jz, jy, jx):
    tensor = [[ref[at_point(c, k, jz, jy, jx), :] for k in range(3)] for c in range(3)]
    return tensor


def jacobian_at(ref, jz, jy, jx):
    tensor = load_tensor(ref, jz, jy, jx)
    return [[tensor[c][k] + 1.0 if c == k else tensor[c][k] for k in range(3)] for c in range(3)]


def strain_of(jac, size):
    return symmetric(lambda k, l: column_dot(jac, jac, k, l) * size - (1.0 if k == l else 0.0))


def weight_at(jz, jy, jx):
    along_z = MIDDLE if jz == 1 else OUTER
    return along_z * ((MIDDLE if jy == 1 else OUTER) * (MIDDLE if jx == 1 else OUTER))


def newton_step(totals):
    _, linear, quadratic, cubic, quartic, floor = (jnp.broadcast_to(totals[:, i : i + 1], (8, 128)) for i in range(6))
    step = jnp.zeros_like(linear)
    for _ in range(4):
        slope = linear + step * (2.0 * quadratic + step * (3.0 * cubic + step * 4.0 * quartic))
        curvature = 2.0 * quadratic + step * (6.0 * cubic + step * 12.0 * quartic)
        step = step - slope / jnp.maximum(curvature, floor + 1e-06)
    return step


def add_up(terms_ref):
    return jnp.sum(terms_ref[...], axis=0, keepdims=True)


def ring(pieces, count, out_ref, out_at, z_shift, y_shift):
    low = lax.broadcasted_iota(jnp.int32, (count, 128), 1) < 64
    places = ((-1, 1), (0, 0), (0, 1), (1, 0)) if y_shift else ((-1, 0), (-1, 1), (0, 0), (0, 1))
    for upper in range(2):
        for y, (piece_y, row) in enumerate(places):

            def piece(z):
                ref, at = pieces[z, piece_y]
                return ref[pl.ds(at + row, count, stride=2), :]

            value = piece(-upper)
            if z_shift:
                value = jnp.where(low, pltpu.roll(value, 64, 1), pltpu.roll(piece(1 - upper), 64, 1))
            out_ref[pl.ds(out_at + upper * 4 + y, count, stride=8), :] = value


def each(body):
    for i in range(3):
        body(i)


def jacobians(field, nodes_ref, jac_ref):
    for z_shift in range(2):
        for y_shift in range(2):
            ring(field, 24, nodes_ref, (z_shift * 2 + y_shift) * 192, z_shift, y_shift)

    def known(c):
        def local(z, y, x):
            row = ((z == 2) * 2 + (y == 2)) * 192 + ((z % 2) * 4 + (y % 2) * 2 + x % 2) * 8
            value = nodes_ref[pl.ds(row + c * 64, 8), :]
            return x_up(value) if x == 2 else value

        return local

    each(lambda c: forward(known(c), jac_ref, functools.partial(at_point, c)))


def descend(size_ref, jac_ref, part_ref, turn_ref, move_ref):
    def size_at(jz, jy, jx):
        return size_ref[pl.ds((jz * 9 + jy * 3 + jx) * 8, 8), :]

    turn_ref[192:, :] = jnp.zeros((64, 128), jnp.float32)

    def stress(jz):
        for jy in range(3):
            for jx in range(3):
                jac = jacobian_at(jac_ref, jz, jy, jx)
                size = size_at(jz, jy, jx)
                strain = strain_of(jac, size)
                scale = size * (-4.0 * weight_at(jz, jy, jx))
                for c in range(3):
                    for k in range(3):
                        part = (strain[k, 0] * jac[c][0] + strain[k, 1] * jac[c][1]) + strain[k, 2] * jac[c][2]
                        part_ref[at_point(c, k, jz, jy, jx), :] = part * scale

    each(stress)
    each(lambda c: backward(c, part_ref, turn_ref))
    for row in range(2):
        move_ref[pl.ds(row, 24, stride=2), :] = turn_ref[pl.ds(row + 2, 24, stride=8), :]


def line_sums(size_ref, jac_ref, part_ref, turn_ref, terms_out):
    def packed(node, upper, shift):
        rows = [
            turn_ref[pl.ds(node * 8 + upper * 4 + 1 + shift + ey, 4, stride=64), :] for ey in range(2)
        ]
        return jnp.concatenate(rows, axis=0)

    def sought(z, y, x):
        node = (z % 2) * 4 + (y % 2) * 2 + x % 2
        shift = y // 2
        value = packed(node, 0, shift)
        if z == 2:
            value = pltpu.roll(value, 64, 1)
        else:
            value = jnp.where(lane_index() < 64, value, packed(node, 1, shift))
        return x_up(value) if x == 2 else value

    forward(sought, part_ref, lambda k, jz, jy, jx: pl.ds(((jz * 9 + jy * 3 + jx) * 3 + k) * 8, 8))

    def middle(ref, at, stride):
        return jnp.where(lane_index() < 64, ref[pl.ds(at, 8, stride=stride), :], ref[pl.ds(at + 4, 8, stride=stride), :])

    sub = lax.broadcasted_iota(jnp.int32, (8, 128), 0)
    sums = [jnp.zeros((8, 128), jnp.float32) for _ in range(6)]
    for start, fresh in ((0, 0), (8, 8), (16, 16), (19, 24)):
        weight = jnp.zeros((8, 128), jnp.float32)
        for i in range(fresh - start, 8):
            point = start + i
            parts = [MIDDLE if (point // by) % 3 == 1 else OUTER for by in (9, 3, 1)]
            weight = jnp.where(sub == i, (parts[0] * parts[1]) * parts[2], weight)
        for ey in range(2):
            jac = [
                [middle(jac_ref, (start * 9 + c * 3 + k) * 8 + 1 + ey, 72) for k in range(3)]
                for c in range(3)
            ]
            jac = [[jac[c][k] + 1.0 if c == k else jac[c][k] for k in range(3)] for c in range(3)]
            motion = [
                [part_ref[pl.ds((start * 3 + k) * 8 + ey * 4 + c, 8, stride=24), :] for k in range(3)]
                for c in range(3)
            ]
            size = middle(size_ref, start * 8 + 1 + ey, 8)
            zero = strain_of(jac, size)
            one = symmetric(lambda k, l: (column_dot(jac, motion, k, l) + column_dot(motion, jac, k, l)) * size)
            two = symmetric(lambda k, l: column_dot(motion, motion, k, l) * size)
            pairs = ((zero, zero), (zero, one), (zero, two), (one, two), (two, two), (one, one))
            sums = [total + weight * inner(*pair) for total, pair in zip(sums, pairs)]
    zz, zo, zt, ot, tt, gn = (jnp.sum(total, keepdims=True) for total in sums)
    lane = lax.broadcasted_iota(jnp.int32, (1, 128), 1)
    terms = jnp.zeros((1, 128), jnp.float32)
    for i, term in enumerate((zz, 2.0 * zo, gn + 2.0 * zt, 2.0 * ot, tt, gn)):
        terms = jnp.where(lane == i, term, terms)
    terms_out[...] = jnp.broadcast_to(terms, (SRC, 128))


def jacobian_kernel(pieces, *refs):
    jacobians(pieces(refs[:3]), refs[4], refs[3])


def descent_kernel(jac_ref, own, z_low, y_low, corner, move_ref, turn_ref, size_ref, part_ref):
    sizes = {at: (ref, 0) for at, ref in size_pieces([own, z_low, y_low, corner]).items()}
    ring(sizes, 27, size_ref, 0, 0, 0)
    descend(size_ref, jac_ref, part_ref, turn_ref, move_ref)


def line_kernel(jac_ref, turn_ref, size_ref, terms_out, part_ref):
    line_sums(size_ref, jac_ref, part_ref, turn_ref, terms_out)


def second_kernel(before_ref, drift_ref, size_ref, terms_in, move_ref, terms_out, step_ref, jac_ref, part_ref, turn_ref):
    step = newton_step(add_up(terms_in))
    step_ref[...] = step
    for row in range(0, JAC_ROWS, 8):
        rows = slice(row, row + 8)
        jac_ref[rows, :] = before_ref[rows, :] + step * drift_ref[rows, :]
    descend(size_ref, jac_ref, part_ref, turn_ref, move_ref)
    line_sums(size_ref, jac_ref, part_ref, turn_ref, terms_out)


NODE = jax.ShapeDtypeStruct((48, 128), jnp.float32)
TERMS = jax.ShapeDtypeStruct((SRC, 128), jnp.float32)
NODES_ROWS, JAC_ROWS, TURN_ROWS, SIZE_ROWS = 4 * 192, 243 * 8, 32 * 8, 27 * 8


def rows_of(count):
    return jax.ShapeDtypeStruct((count, 128), jnp.float32)


def scratch_of(count):
    return pltpu.VMEM((count, 128), jnp.float32)


def all_jacobians(field, pieces):
    kernel = functools.partial(jacobian_kernel, pieces)
    return call(kernel, rows_of(JAC_ROWS), field, [scratch_of(NODES_ROWS)])


def first_descent(jac, sizes):
    outs = [NODE, rows_of(TURN_ROWS), rows_of(SIZE_ROWS)]
    return call(descent_kernel, outs, [jac, *sizes], [scratch_of(JAC_ROWS)])


def first_line(jac, turn, size):
    return call(line_kernel, TERMS, [jac, turn, size], [scratch_of(81 * 8)])


def second_pass(jac, drift, size, terms):
    scratch = [scratch_of(rows) for rows in (JAC_ROWS, JAC_ROWS, TURN_ROWS)]
    return call(second_kernel, [NODE, TERMS, rows_of(8)], [jac, drift, size, terms], scratch)


def interleave(back):
    row = lax.broadcasted_iota(jnp.int32, (128, 128), 0)
    col = lax.broadcasted_iota(jnp.int32, (128, 128), 1)
    if back:
        row, col = col, row
    return (col == (row & 1) * 64 + (row >> 1)).astype(jnp.float32)


def split_kernel(nodes_ref, out_ref, rows_ref):
    rows = nodes_ref[...].reshape(48, 128)
    rows_ref[...] = jnp.dot(rows, interleave(False), precision=lax.Precision.HIGHEST, preferred_element_type=jnp.float32)
    low = lax.broadcasted_iota(jnp.int32, (1, 128), 1) < 64
    for c in range(3):
        for az in range(2):
            for ay in range(2):
                for ey in range(2):
                    at = c * 16 + az * 4 + ey * 2 + ay
                    first = rows_ref[at : at + 1, :]
                    second = rows_ref[at + 8 : at + 9, :]
                    to = (c * 8 + az * 4 + ay * 2) * 2 + ey
                    out_ref[to : to + 1, :] = jnp.where(low, first, pltpu.roll(second, 64, 1))
                    out_ref[to + 2 : to + 3, :] = jnp.where(low, pltpu.roll(first, 64, 1), second)


def split_nodes(nodes):
    out = jax.ShapeDtypeStruct((48, 128), jnp.float32)
    return call(split_kernel, out, [nodes], [pltpu.VMEM((48, 128), jnp.float32)], far=(0,))


def join_kernel(count, *refs):
    rows_ref = refs[-1]
    low = lax.broadcasted_iota(jnp.int32, (1, 128), 1) < 64
    for i, new_ref in enumerate(refs[:count]):
        for c in range(3):
            for az in range(2):
                for ay in range(2):
                    for ey in range(2):
                        at = (c * 8 + az * 4 + ay * 2) * 2 + ey
                        even = new_ref[at : at + 1, :]
                        odd = new_ref[at + 2 : at + 3, :]
                        to = i * 48 + c * 16 + az * 4 + ey * 2 + ay
                        rows_ref[to : to + 1, :] = jnp.where(low, even, pltpu.roll(odd, 64, 1))
                        rows_ref[to + 8 : to + 9, :] = jnp.where(low, pltpu.roll(even, 64, 1), odd)
    rows = jnp.dot(
        rows_ref[...], interleave(True), precision=lax.Precision.HIGHEST, preferred_element_type=jnp.float32
    )
    for i, out_ref in enumerate(refs[count : 2 * count]):
        out_ref[...] = rows[i * 48 : i * 48 + 48].reshape(3, 4, 4, 128)


def join_nodes(*nodes):
    outs = [jax.ShapeDtypeStruct((3, 4, 4, 128), jnp.float32) for _ in nodes]
    kernel = functools.partial(join_kernel, len(nodes))
    return call(kernel, outs, list(nodes), [scratch_of(48 * len(nodes))])


def finish_kernel(own_ref, first_move_ref, last_move_ref, step_ref, first_ref, second_ref, out_ref, coeff_ref):
    second = add_up(second_ref)
    step = newton_step(second)[:4]
    first_step = step_ref[:4, :]
    for c in range(3):
        for z in range(4):
            field = own_ref[c, z] + first_step * first_move_ref[c, z]
            out_ref[c, z] = field + step * last_move_ref[c, z]
    coeff_ref[0:1, :] = add_up(first_ref)[:, :5] * (1.0 / 32768.0)
    coeff_ref[1:2, :] = second[:, :5] * (1.0 / 32768.0)


def finish(*args):
    outs = [jax.ShapeDtypeStruct((3, 4, 4, 128), jnp.float32), jax.ShapeDtypeStruct((2, 5), jnp.float32)]
    return call(finish_kernel, outs, list(args), [], last=True)


def pack_kernel(elem_ref, coord_ref, out_ref):
    parts = [elem_ref[...].astype(jnp.float32)] + [coord_ref[j] for j in range(3)]
    for j, part in enumerate(parts):
        out_ref[:, 0, j * 128 : j * 128 + 128] = part[:128].T
    tails = jnp.concatenate([part[128:] for part in parts] + [jnp.zeros((96, 128), jnp.float32)], axis=0)
    out_ref[:, 0, 512:] = tails.T


def pack(elem, coord):
    return call(pack_kernel, jax.ShapeDtypeStruct((SRC, 1, 640), jnp.float32), [elem, coord], [], far=(0, 1))


def exchange(values):
    return lax.all_to_all(values, ("mesh", "bg"), split_axis=0, concat_axis=0, tiled=True)


def moved(values, axis, by):
    count = lax.axis_size(axis)
    return lax.ppermute(values, axis, [(i, (i - by) % count) for i in range(count)])


def along_mesh(block):
    return jnp.concatenate([block, moved(block, "mesh", 1), moved(block, "mesh", -1)], axis=0)


def from_below(block):
    mesh, bg = lax.axis_size("mesh"), lax.axis_size("bg")
    steps = [
        (z * bg + y, ((z + 1) % mesh) * bg + (y + 1) % bg) for z in range(mesh) for y in range(bg)
    ]
    corner = lax.ppermute(block, ("mesh", "bg"), steps)
    z_low = moved(block, "mesh", -1)
    y_low = moved(block, "bg", -1)
    return [block, z_low, y_low, corner]


def along_bg(rows):
    return [rows, moved(rows, "bg", 1), moved(rows, "bg", -1)]


def shards(displacement, bg_coef, query_elem, query_point, query_coord):
    asked = exchange(pack(query_elem[0].T, query_coord[0].transpose(1, 2, 0)))
    own = split_nodes(displacement)
    rows = along_mesh(own)
    asked, prepared = lax.optimization_barrier((asked, prepare(bg_coef)))
    found = lookup(asked, prepared)
    found = exchange(found)
    field = along_bg(rows)
    sizes = place(found, query_point[0].T)
    sizes = from_below(sizes)
    jac = all_jacobians(field, field_pieces)
    move, turn, size = first_descent(jac, sizes)
    rows = jnp.concatenate(along_bg(move), axis=0)
    terms = first_line(jac, turn, size)
    first_terms = exchange(terms)
    shift = [rows, moved(rows, "mesh", 1), moved(rows, "mesh", -1)]
    drift = all_jacobians(shift, shift_pieces)
    last_move, last_terms, step = second_pass(jac, drift, size, first_terms)
    last_terms = exchange(last_terms)
    nodes = join_nodes(own, move, last_move)
    return finish(*nodes, step, first_terms, last_terms)


def solution(mesh):
    in_specs = (
        P(None, "mesh", "bg", None),
        P(None, ("mesh", "bg")),
        P(("mesh", "bg"), None, None),
        P(("mesh", "bg"), None, None),
        P(("mesh", "bg"), None, None, None),
    )
    out_specs = (P(None, "mesh", "bg", None), P())
    return jax.shard_map(shards, mesh=mesh, in_specs=in_specs, out_specs=out_specs, check_vma=False)
```
